512 devices in a mesh: wide: 32 (over x, y), grp: 16 (over z, core).
Axes of the slice: x: 4, y: 8, z: 8, core: 2. Of those that a mesh axis runs over, the one named last changes fastest.
Arguments:
- source: float32 [256, 256, 128], P('wide', 'grp'), may hold values from -6 to 6
- conductivity: float32 [256, 256, 128], P('wide', 'grp'), may hold values from 0.02 to 0.5
- ice_cells: int32 [256, 256], P('wide', 'grp'), may hold values from 1 to 128, as said below
Outputs:
- pressure: float32 [256, 256, 128], P('wide', 'grp')
The draws below stay inside these ranges and needn't reach their ends.
Inputs may be any that keep to these rules, and one draw needn't show every extreme that they name: Column (x, y) holds ice in its lowest ice_cells[x, y] cells; some column is 128 cells high.
All inputs are finite; a program needn't handle non-finite values.
Results may differ from the reference program's by a relative error of at most 0.0001.
Values sent between devices are 32-bit elements; how exact they have to be, the bound alone decides.
No kernel may reach another device: no remote copies, remote signals or barrier semaphores. Data moves between devices by JAX's collectives and lax.ppermute only.
A program may use at most 64 MiB of HBM per device.

```python
import math
import jax
import jax.numpy as jnp

CZ = 128
ITERS = 6
NX = 256
NY = 256


def draw_source(key, part):
    values = jax.random.truncated_normal(key, -6.0, 6.0, (NX, NY, CZ), jnp.float32)
    return values


def draw_ice_cells(key, part):
    key_plateau = jax.random.fold_in(key, 11)
    key_rough = jax.random.fold_in(key, 12)
    key_summit = jax.random.fold_in(key, 13)
    plateau = jax.random.randint(key_plateau, (NX // 4, NY // 4), CZ // 8, CZ + 1)
    plateau = jnp.repeat(jnp.repeat(plateau, 4, 0), 4, 1)
    roughness = jax.random.randint(key_rough, (NX, NY), 0, CZ // 8 + 1)
    heights = jnp.clip(plateau - roughness, 1, CZ)
    summit = jax.random.randint(key_summit, (), 0, NX * NY)
    flattened = heights.reshape(-1)
    flattened = jnp.where(jnp.arange(NX * NY) == summit, CZ, flattened)
    return flattened.reshape(NX, NY).astype(jnp.int32)


def steps_of(stream_key, dims, split, low, top_value):
    level = 1.0
    for dim, blocks in split:
        steps = jax.random.uniform(jax.random.fold_in(jax.random.fold_in(stream_key, 6), dim), (blocks,), jnp.float32, low / len(split), top_value / len(split))
        level = level * jnp.repeat(jnp.exp(steps), dims[dim] // blocks).reshape((-1,) + (1,) * (len(dims) - 1 - dim))
    return level


def setup_inputs(seed: int = 0) -> dict:
    keys = jax.random.split(jax.random.key(seed), 4)
    source = draw_source(jax.random.fold_in(keys[3], 71), 0)
    conductivity = jnp.clip(jnp.exp(math.log(0.5) - 3.218876 * jax.random.uniform(keys[1], (NX, NY, CZ), jnp.float32) ** steps_of(keys[1], (NX, NY, CZ), ((0, 32), (1, 16)), -0.2, 0.2)), 0.02, 0.5)
    ice_cells = draw_ice_cells(jax.random.fold_in(keys[3], 71), 0)
    return dict(source=source, conductivity=conductivity, ice_cells=ice_cells)


cheb_center = (2.0 + 0.3) / 2.0
cheb_radius = (2.0 - 0.3) / 2.0
first_ratio = cheb_radius / cheb_center
second_ratio = 1.0 / (2.0 * cheb_center / cheb_radius - first_ratio)
carry_weight = second_ratio * first_ratio
fresh_weight = 2.0 * second_ratio / cheb_radius


def beside_all(values, above):
    padded = jnp.pad(values, ((1, 1), (1, 1), (0, 0)))
    below = jnp.zeros_like(above)
    return (padded[2:, 1:-1], padded[:-2, 1:-1], padded[1:-1, 2:], padded[1:-1, :-2],
            jnp.concatenate([values[:, :, 1:], above], 2),
            jnp.concatenate([below, values[:, :, :-1]], 2))


def level_setup(coef_field, heights, coarsening):
    factor = float(2 ** coarsening)
    others = beside_all(coef_field, coef_field[:, :, -1:])
    weights = tuple(factor * 2.0 * coef_field * neighbour / (coef_field + neighbour) for neighbour in others)
    diagonal = weights[0]
    for weight in weights[1:]:
        diagonal = diagonal + weight
    layers = jnp.arange(coef_field.shape[2], dtype=jnp.float32) * factor
    active = (layers[None, None, :] < heights[:, :, None]).astype(jnp.float32)
    return weights, diagonal, active


def operate(values, setup):
    weights, diagonal, active = setup
    others = beside_all(values, jnp.zeros_like(values[:, :, :1]))
    coupled = weights[0] * others[0]
    for weight, neighbour in zip(weights[1:], others[1:]):
        coupled = coupled + weight * neighbour
    return active * (diagonal * values - coupled)


def smooth(guess, source_term, setup, fresh):
    diagonal = setup[1]
    if fresh:
        residual = source_term
    else:
        residual = source_term - operate(guess, setup)
    update = residual / (cheb_center * diagonal)
    guess = update if fresh else guess + update
    residual = source_term - operate(guess, setup)
    update = carry_weight * update + fresh_weight * residual / diagonal
    return guess + update


def children_sum(values):
    extent_x, extent_y, extent_z = values.shape
    return values.reshape(extent_x // 2, 2, extent_y // 2, 2, extent_z // 2, 2).sum(axis=(1, 3, 5))


def column_top(heights):
    extent_x, extent_y = heights.shape
    return heights.reshape(extent_x // 2, 2, extent_y // 2, 2).max(axis=(1, 3))


def spread_children(values):
    return jnp.repeat(jnp.repeat(jnp.repeat(values, 2, 0), 2, 1), 2, 2)


def conjugate(source_term, setup):
    solution = jnp.zeros_like(source_term)
    residual = source_term
    direction = source_term
    current = jnp.sum(residual * residual)
    for iteration in range(ITERS):
        applied = operate(direction, setup)
        step_size = current / jnp.sum(direction * applied)
        solution = solution + step_size * direction
        residual = residual - step_size * applied
        following = jnp.sum(residual * residual)
        direction = residual + (following / current) * direction
        current = following
    return solution


def reference(source, conductivity, ice_cells):
    heights = ice_cells.astype(jnp.float32)
    setup_fine = level_setup(conductivity, heights, 0)
    load_fine = setup_fine[2] * source
    smooth_fine = smooth(jnp.zeros_like(load_fine), load_fine, setup_fine, True)
    load_middle = children_sum(load_fine - operate(smooth_fine, setup_fine))
    coef_middle = children_sum(conductivity) * 0.125
    heights_middle = column_top(heights)
    setup_middle = level_setup(coef_middle, heights_middle, 1)
    smooth_middle = smooth(jnp.zeros_like(load_middle), load_middle, setup_middle, True)
    load_coarse = children_sum(load_middle - operate(smooth_middle, setup_middle))
    coef_coarse = children_sum(coef_middle) * 0.125
    setup_coarse = level_setup(coef_coarse, column_top(heights_middle), 2)
    coarse = conjugate(load_coarse, setup_coarse)
    smooth_middle = smooth_middle + setup_middle[2] * spread_children(coarse)
    smooth_middle = smooth(smooth_middle, load_middle, setup_middle, False)
    smooth_fine = smooth_fine + setup_fine[2] * spread_children(smooth_middle)
    return smooth(smooth_fine, load_fine, setup_fine, False)
```

```python
import functools

import jax
import jax.numpy as jnp
from jax import lax
from jax.experimental import pallas as pl
from jax.experimental.pallas import tpu as pltpu
from jax.sharding import Mesh
from jax.sharding import PartitionSpec as P

ITERS = 6

cheb_center = (2.0 + 0.3) / 2.0
cheb_radius = (2.0 - 0.3) / 2.0
first_ratio = cheb_radius / cheb_center
second_ratio = 1.0 / (2.0 * cheb_center / cheb_radius - first_ratio)
carry_weight = second_ratio * first_ratio
fresh_weight = 2.0 * second_ratio / cheb_radius
inverse_center = 1.0 / cheb_center

F32 = jnp.float32
BX, BY, BZ = 8, 16, 128
PACK = 2 * BX + 1
EX, EY = 3 * BX, 3 * BY
MX, MY = EX // 2, EY // 2
TX, TY = 12, 32
X0, Y0 = 6, 8
ROWS = 5


def lane_index(shape):
    return lax.broadcasted_iota(jnp.int32, shape, len(shape) - 1)


def pair_weight(factor, coef, neighbour):
    total = coef + neighbour
    return (2.0 * factor) * coef * neighbour / jnp.where(total > 0.0, total, 1.0)


def shift(value, amount, axis):
    return pltpu.roll(value, amount % value.shape[axis], axis)


def operate(before, value, after, weight_x, weight_x_before, weight_y, weight_z, diagonal, active, step_z):
    coupled = weight_x * after + weight_x_before * before
    coupled = coupled + weight_y * shift(value, -1, 0)
    coupled = coupled + shift(weight_y * value, 1, 0)
    coupled = coupled + weight_z * shift(value, -step_z, 1)
    coupled = coupled + shift(weight_z * value, step_z, 1)
    return active * (diagonal * value - coupled)


def pair_lanes(value, step, combine):
    lanes = lane_index(value.shape)
    other = jnp.where((lanes & step) == 0, shift(value, -step, 1), shift(value, step, 1))
    return combine(value, other)


def face_weights(factor, coef_ref, wx_ref, wy_ref, wz_ref, extent, step_z):
    wx_ref[0] = jnp.zeros(wx_ref.shape[1:], F32)
    wx_ref[extent] = jnp.zeros(wx_ref.shape[1:], F32)

    def body(x, carry):
        coef = coef_ref[x]
        lanes = lane_index(coef.shape)
        wx_ref[x] = pair_weight(factor, coef_ref[x - 1], coef)
        wy_ref[x] = pair_weight(factor, coef, shift(coef, -1, 0))
        weight = pair_weight(factor, coef, shift(coef, -step_z, 1))
        wz_ref[x] = jnp.where(lanes >= BZ - step_z, 0.0, weight)
        return carry

    coef = coef_ref[0]
    lanes = lane_index(coef.shape)
    wy_ref[0] = pair_weight(factor, coef, shift(coef, -1, 0))
    wz_ref[0] = jnp.where(lanes >= BZ - step_z, 0.0, pair_weight(factor, coef, shift(coef, -step_z, 1)))
    lax.fori_loop(1, extent, body, 0)


def diagonal_of(factor, x, coef_ref, wx_ref, wy_ref, wz_ref, step_z):
    coef = coef_ref[x]
    lanes = lane_index(coef.shape)
    weight_y, weight_z = wy_ref[x], wz_ref[x]
    top = jnp.where(lanes >= BZ - step_z, factor * coef, weight_z)
    total = wx_ref[x + 1] + wx_ref[x] + weight_y + shift(weight_y, 1, 0)
    return total + top + shift(weight_z, step_z, 1)


def inverse_of(diagonal):
    return 1.0 / jnp.where(diagonal > 0.0, diagonal, 1.0)


def local_kernel(
    own_ref, up_ref, down_ref,
    fan_ref, edge_ref,
    load1_ref, active1_ref, wx1_ref, wy1_ref, wz1_ref, diag1_ref, inv1_ref, smooth1_ref,
    load0_ref, active0_ref, wx0_ref, wy0_ref, wz0_ref, diag0_ref, inv0_ref, smooth0_ref,
    source, coef, active, wx, wy, wz, diag, inv, update, smooth, coef1, update1, pairs, tops, coarse,
):
    for j in range(3):
        def gather(i, carry, j=j):
            for target, row in ((source, 0), (coef, BX)):
                for k, ref in enumerate((up_ref, own_ref, down_ref)):
                    target[j * BX + i, k * BY:(k + 1) * BY, :] = ref[j * PACK + row + i]
            return carry

        lax.fori_loop(0, BX, gather, 0)
        for i in range(BX):
            for k, ref in enumerate((up_ref, own_ref, down_ref)):
                column = ref[j * PACK + 2 * BX, :, i:i + 1]
                active[j * BX + i, k * BY:(k + 1) * BY, :] = jnp.broadcast_to(column, (BY, BZ))

    def middle_tops(x, carry):
        pairs[...] = jnp.maximum(active[2 * x], active[2 * x + 1])
        value = jnp.maximum(pairs[pl.ds(0, MY, stride=2), :], pairs[pl.ds(1, MY, stride=2), :])
        tops[x] = value
        layer = (lane_index((MY, BZ)) & ~1).astype(F32)
        active1_ref[x] = (layer < value).astype(F32)
        return carry

    lax.fori_loop(0, MX, middle_tops, 0)

    def fine_mask(x, carry):
        layer = lane_index((EY, BZ)).astype(F32)
        mask = (layer < active[x]).astype(F32)
        active[x] = mask
        source[x] = mask * source[x]
        return carry

    lax.fori_loop(0, EX, fine_mask, 0)

    face_weights(1.0, coef, wx, wy, wz, EX, 1)

    def fine_start(x, carry):
        diagonal = diagonal_of(1.0, x, coef, wx, wy, wz, 1)
        inverse = inverse_of(diagonal)
        diag[x] = diagonal
        inv[x] = inverse
        update[x] = source[x] * (inverse * inverse_center)
        return carry

    lax.fori_loop(0, EX, fine_start, 0)

    def fine_operate(ref, x):
        return operate(ref[x - 1], ref[x], ref[x + 1], wx[x + 1], wx[x], wy[x], wz[x], diag[x], active[x], 1)

    def fine_finish(x, carry):
        residual = source[x] - fine_operate(update, x)
        first = update[x]
        smooth[x] = first + (carry_weight * first + fresh_weight * residual * inv[x])
        return carry

    smooth[0] = jnp.zeros((EY, BZ), F32)
    smooth[EX - 1] = jnp.zeros((EY, BZ), F32)
    lax.fori_loop(1, EX - 1, fine_finish, 0)

    def keep(i, carry):
        for kept, ref in (
            (load0_ref, source), (active0_ref, active), (wy0_ref, wy), (wz0_ref, wz),
            (diag0_ref, diag), (inv0_ref, inv), (smooth0_ref, smooth),
        ):
            kept[i] = ref[X0 + i, Y0:Y0 + TY, :]
        wx0_ref[i] = wx[X0 + i, Y0:Y0 + TY, :]
        return carry

    lax.fori_loop(0, TX, keep, 0)

    def restrict(value):
        pairs[...] = pair_lanes(value, 1, jnp.add)
        return pairs[pl.ds(0, MY, stride=2), :] + pairs[pl.ds(1, MY, stride=2), :]

    def middle_coef(x, carry):
        coef1[x] = restrict(coef[2 * x] + coef[2 * x + 1]) * 0.125
        return carry

    lax.fori_loop(0, MX, middle_coef, 0)

    def middle_load(x, carry):
        left = source[2 * x] - fine_operate(smooth, 2 * x)
        right = source[2 * x + 1] - fine_operate(smooth, 2 * x + 1)
        load1_ref[x] = restrict(left + right)
        return carry

    for x in (0, 1, MX - 2, MX - 1):
        load1_ref[x] = jnp.zeros((MY, BZ), F32)
    lax.fori_loop(2, MX - 2, middle_load, 0)

    face_weights(2.0, coef1, wx1_ref, wy1_ref, wz1_ref, MX, 2)

    def middle_start(x, carry):
        diagonal = diagonal_of(2.0, x, coef1, wx1_ref, wy1_ref, wz1_ref, 2)
        inverse = inverse_of(diagonal)
        diag1_ref[x] = diagonal
        inv1_ref[x] = inverse
        update1[x] = load1_ref[x] * (inverse * inverse_center)
        return carry

    lax.fori_loop(0, MX, middle_start, 0)

    def middle_operate(ref, x):
        return operate(
            ref[x - 1], ref[x], ref[x + 1], wx1_ref[x + 1], wx1_ref[x], wy1_ref[x], wz1_ref[x],
            diag1_ref[x], active1_ref[x], 2,
        )

    def middle_finish(x, carry):
        residual = load1_ref[x] - middle_operate(update1, x)
        first = update1[x]
        smooth1_ref[x] = first + (carry_weight * first + fresh_weight * residual * inv1_ref[x])
        return carry

    for x in (0, 1, 2, MX - 3, MX - 2, MX - 1):
        smooth1_ref[x] = jnp.zeros((MY, BZ), F32)
    lax.fori_loop(3, MX - 3, middle_finish, 0)
    for i in range(2):
        edge_ref[i] = smooth1_ref[MX // 2 - 1 + i]

    first_x, first_y = MX // 3, MY // 3
    rows = []
    for part in range(2):
        for cx in range(2):
            if part == 0:
                total = sum(
                    load1_ref[x] - middle_operate(smooth1_ref, x)
                    for x in (first_x + 2 * cx, first_x + 2 * cx + 1)
                )
            else:
                total = (coef1[first_x + 2 * cx] + coef1[first_x + 2 * cx + 1]) * 0.125
            coarse[...] = pair_lanes(total, 2, jnp.add)
            value = (
                coarse[pl.ds(first_y, 4, stride=2), :] + coarse[pl.ds(first_y + 1, 4, stride=2), :]
            )
            rows.append(jnp.concatenate([value[i:i + 1] for i in range(4)], 1))
    spread = jnp.concatenate(rows + [jnp.zeros((4, 4 * BZ), F32)], 0)
    entry = lax.broadcasted_iota(jnp.int32, (4 * BZ, BZ), 0)
    lanes = lane_index((4 * BZ, BZ))
    chosen = (entry // BZ == lanes // 32) & (entry % BZ == (lanes % 32) * 4)
    packed = jnp.dot(
        spread, chosen.astype(F32), precision=lax.Precision.HIGHEST, preferred_element_type=F32
    )
    lanes = lane_index((1, BZ))
    top_row = jnp.zeros((1, BZ), F32)
    for cx in range(2):
        coarse[...] = jnp.maximum(tops[first_x + 2 * cx], tops[first_x + 2 * cx + 1])
        value = jnp.maximum(
            coarse[pl.ds(first_y, 4, stride=2), :], coarse[pl.ds(first_y + 1, 4, stride=2), :]
        )
        for cy in range(4):
            top_row = jnp.where(lanes // 16 == 2 * cy + cx, value[cy:cy + 1], top_row)
    block = [packed[i:i + 1] for i in range(4)] + [top_row]
    pattern = jnp.concatenate(block * 8, 0)

    def fan(i, carry):
        fan_ref[pl.ds(pl.multiple_of(i * 8 * ROWS, 8), 8 * ROWS), :] = pattern
        return carry

    lax.fori_loop(0, fan_ref.shape[0] // (8 * ROWS), fan, 0)


def finish_kernel(
    wide, deep, all_ref, before_ref, after_ref,
    load1_ref, active1_ref, wx1_ref, wy1_ref, wz1_ref, diag1_ref, inv1_ref, smooth1_ref,
    load0_ref, active0_ref, wx0_ref, wy0_ref, wz0_ref, diag0_ref, inv0_ref, smooth0_ref,
    out_ref,
    coef, active, wx, wy, wz, diag, residual, direction, image, solution, wanted, spread,
    guess1, update1, second1, children, guess0, update0, second0,
):
    count = 2 * wide
    vector = (deep, BZ)
    lanes = lane_index(vector)
    zero = jnp.zeros(vector, F32)
    pad = 2

    def y_after(value):
        first, second = (shift(v, -32, 1) for v in value)
        return jnp.where(lanes < 96, first, second), jnp.where(lanes < 96, second, shift(first, -1, 0))

    def y_before(value):
        first, second = (shift(v, 32, 1) for v in value)
        return jnp.where(lanes >= 32, first, shift(second, 1, 0)), jnp.where(lanes >= 32, second, first)

    def load(ref, x):
        return ref[x, 0], ref[x, 1]

    def store(ref, x, value):
        ref[x, 0] = value[0]
        ref[x, 1] = value[1]

    def each(fun, *values):
        return fun(*(v[0] for v in values)), fun(*(v[1] for v in values))

    for x in (*range(pad), *range(count + pad, count + 2 * pad)):
        store(residual, x, (zero, zero))
        store(direction, x, (zero, zero))

    stride = deep * ROWS

    def unpack(w, carry):
        for c in range(2):
            def row(k):
                return all_ref[pl.ds(c * wide * stride + w * stride + k, deep, stride=ROWS), :]

            top = row(4)
            low = (lanes & 16) == 0
            layer = ((lanes & 31) * 4).astype(F32)
            for i in range(2):
                residual[2 * w + i + pad, c] = row(i)
                direction[2 * w + i + pad, c] = zero
                coef[2 * w + i, c] = row(2 + i)
                if i == 0:
                    tall = jnp.where(low, top, shift(top, 16, 1))
                else:
                    tall = jnp.where(low, shift(top, -16, 1), top)
                active[2 * w + i, c] = (layer < tall).astype(F32)
        return carry

    lax.fori_loop(0, wide, unpack, 0)

    highest = (lanes & 31) == 31
    last_y = (lanes >= 96) & (lax.broadcasted_iota(jnp.int32, vector, 0) == deep - 1)

    def weights(x, carry):
        here = load(coef, x)
        there = load(coef, jnp.maximum(x - 1, 0))
        value = each(lambda a, b: jnp.where(x > 0, pair_weight(4.0, a, b), 0.0), here, there)
        store(wx, x, value)
        value = each(lambda a, b: pair_weight(4.0, a, b), here, y_after(here))
        store(wy, x, (value[0], jnp.where(last_y, 0.0, value[1])))
        value = each(lambda a: jnp.where(highest, 0.0, pair_weight(4.0, a, shift(a, -1, 1))), here)
        store(wz, x, value)
        return carry

    lax.fori_loop(0, count, weights, 0)
    store(wx, count, (zero, zero))

    def diagonals(x, carry):
        weight_y, weight_z = load(wy, x), load(wz, x)
        top = each(lambda a, w: jnp.where(highest, 4.0 * a, w), load(coef, x), weight_z)
        value = each(
            lambda a, b, c, d, e, f: a + b + c + d + e + shift(f, 1, 1),
            load(wx, x + 1), load(wx, x), weight_y, y_before(weight_y), top, weight_z,
        )
        store(diag, x, value)
        return carry

    lax.fori_loop(0, count, diagonals, 0)

    def square(x, total):
        value = load(residual, x + pad)
        return total + value[0] * value[0] + value[1] * value[1]

    def whole(total):
        return jnp.sum(jnp.sum(total, axis=0, keepdims=True), axis=1, keepdims=True)

    current = whole(lax.fori_loop(0, count, square, zero))
    ratio = jnp.zeros((1, 1), F32)
    first = 2 * lax.axis_index("wide")
    for i in range(6):
        store(solution, i, (zero, zero))

    for iteration in range(ITERS):
        scale = jnp.broadcast_to(ratio, vector)

        def fresh_direction(x):
            value = each(lambda r, d: r + scale * d, load(residual, x), load(direction, x))
            store(direction, x, value)
            return value

        def apply(x, carry):
            total, before, here = carry
            after = fresh_direction(x + 1 + pad)
            weight_y, weight_z = load(wy, x), load(wz, x)
            product = each(jnp.multiply, weight_y, here)
            coupled = each(
                lambda wa, a, wb, b, wc, c, d, we, e: (
                    wa * a + wb * b + wc * c + d + we * shift(e, -1, 1) + shift(we * e, 1, 1)
                ),
                load(wx, x + 1), after, load(wx, x), before, weight_y, y_after(here),
                y_before(product), weight_z, here,
            )
            value = each(
                lambda m, d, v, c: m * (d * v - c), load(active, x), load(diag, x), here, coupled
            )
            store(image, x, value)
            total = total + here[0] * value[0] + here[1] * value[1]
            return total, here, after

        start = fresh_direction(pad)
        total, _, _ = lax.fori_loop(0, count, apply, (zero, (zero, zero), start))
        step = current / whole(total)
        scale_step = jnp.broadcast_to(step, vector)
        for i in range(6):
            value = each(
                lambda s, d: s + scale_step * d, load(solution, i), load(direction, first + i)
            )
            store(solution, i, value)
        if iteration == ITERS - 1:
            break

        def reduce(x, total):
            value = each(lambda r, a: r - scale_step * a, load(residual, x + pad), load(image, x))
            store(residual, x + pad, value)
            return total + value[0] * value[0] + value[1] * value[1]

        following = whole(lax.fori_loop(0, count, reduce, zero))
        ratio = following / current
        current = following

    position = 2 * lax.axis_index("z") + lax.axis_index("core")
    wanted[...] = jnp.zeros(wanted.shape, F32)
    for j in range(3):
        group = jnp.clip(position + j - 1, 0, 2 * deep - 1)
        core, row = group & 1, group >> 1
        for i in range(6):
            wanted[3 * i + j:3 * i + j + 1, :] = solution[i, core, pl.ds(row, 1), :]
    entry = lax.broadcasted_iota(jnp.int32, (BZ, 4 * BZ), 0)
    columns = lane_index((BZ, 4 * BZ))
    chosen = entry == (columns // BZ) * 32 + (columns % BZ) // 4
    spread[...] = jnp.dot(
        wanted[...], chosen.astype(F32), precision=lax.Precision.HIGHEST, preferred_element_type=F32
    )
    for i in range(6):
        rows = []
        for y in range(12):
            r, c = 3 * i + y // 4, y % 4
            row = spread[r:r + 1, c * BZ:(c + 1) * BZ]
            rows.append(jnp.broadcast_to(row, (2, BZ)))
        parent = jnp.concatenate(rows, 0)
        for x in (2 * i, 2 * i + 1):
            if x in (0, MX - 1):
                continue
            if x <= 2:
                value = before_ref[x - 1]
            elif x >= MX - 3:
                value = after_ref[x - (MX - 3)]
            else:
                value = smooth1_ref[x]
            guess1[x] = value + active1_ref[x] * parent

    def middle_operate(ref, x):
        return operate(
            ref[x - 1], ref[x], ref[x + 1], wx1_ref[x + 1], wx1_ref[x], wy1_ref[x], wz1_ref[x],
            diag1_ref[x], active1_ref[x], 2,
        )

    def middle_first(x, carry):
        residual_here = load1_ref[x] - middle_operate(guess1, x)
        value = residual_here * (inv1_ref[x] * inverse_center)
        update1[x] = value
        second1[x] = guess1[x] + value
        return carry

    lax.fori_loop(2, MX - 2, middle_first, 0)

    def middle_second(x, carry):
        residual_here = load1_ref[x] - middle_operate(second1, x)
        value = second1[x] + (
            carry_weight * update1[x] + fresh_weight * residual_here * inv1_ref[x]
        )
        guess1[x] = value
        return carry

    lax.fori_loop(3, MX - 3, middle_second, 0)

    def fine_guess(x, carry):
        value = guess1[x]
        children[pl.ds(0, MY, stride=2), :] = value
        children[pl.ds(1, MY, stride=2), :] = value
        child = children[Y0:Y0 + TY, :]
        for i in range(2):
            k = 2 * x + i - X0
            guess0[k] = smooth0_ref[k] + active0_ref[k] * child
        return carry

    lax.fori_loop(X0 // 2, (X0 + TX) // 2, fine_guess, 0)

    def fine_operate(ref, x):
        return operate(
            ref[x - 1], ref[x], ref[x + 1], wx0_ref[x + 1], wx0_ref[x], wy0_ref[x], wz0_ref[x],
            diag0_ref[x], active0_ref[x], 1,
        )

    def fine_first(x, carry):
        residual_here = load0_ref[x] - fine_operate(guess0, x)
        value = residual_here * (inv0_ref[x] * inverse_center)
        update0[x] = value
        second0[x] = guess0[x] + value
        return carry

    lax.fori_loop(1, TX - 1, fine_first, 0)
    margin = BX - X0

    def fine_second(x, carry):
        residual_here = load0_ref[x] - fine_operate(second0, x)
        value = second0[x] + (
            carry_weight * update0[x] + fresh_weight * residual_here * inv0_ref[x]
        )
        out_ref[x - margin] = value[BY - Y0:2 * BY - Y0]
        return carry

    lax.fori_loop(margin, margin + BX, fine_second, 0)


def in_vmem(count):
    return [pl.BlockSpec(memory_space=pltpu.VMEM)] * count


def grids(count, *shape):
    return [jax.ShapeDtypeStruct(shape, F32)] * count


def scratch(count, *shape):
    return [pltpu.VMEM(shape, F32)] * count


def local_part(strip, up, down, fan):
    middle = grids(8, MX, MY, BZ)
    middle[2] = jax.ShapeDtypeStruct((MX + 1, MY, BZ), F32)
    outs = (
        grids(1, fan * ROWS, BZ) + grids(1, 2, MY, BZ) + middle + grids(8, TX, TY, BZ)
    )
    big = scratch(10, EX, EY, BZ)
    big[3] = pltpu.VMEM((EX + 1, EY, BZ), F32)
    return pl.pallas_call(
        local_kernel,
        out_shape=outs,
        in_specs=in_vmem(3),
        out_specs=in_vmem(len(outs)),
        scratch_shapes=big + scratch(2, MX, MY, BZ) + scratch(1, EY, BZ)
        + scratch(1, MX, MY, BZ) + scratch(1, MY, BZ),
        compiler_params=pltpu.CompilerParams(vmem_limit_bytes=24 * 2**20),
        name="local_part",
    )(strip, up, down)


def finish_part(wide, deep, everything, before, after, kept):
    count = 2 * wide
    tile = (2, deep, BZ)
    return pl.pallas_call(
        functools.partial(finish_kernel, wide, deep),
        out_shape=jax.ShapeDtypeStruct((BX, BY, BZ), F32),
        in_specs=in_vmem(3 + len(kept)),
        out_specs=pl.BlockSpec(memory_space=pltpu.VMEM),
        scratch_shapes=scratch(2, count, *tile) + scratch(1, count + 1, *tile)
        + scratch(3, count, *tile) + scratch(2, count + 4, *tile) + scratch(1, count, *tile)
        + scratch(1, 6, *tile) + scratch(1, 24, BZ) + scratch(1, 24, 4 * BZ)
        + scratch(3, MX, MY, BZ) + scratch(1, EY, BZ) + scratch(3, TX, TY, BZ),
        compiler_params=pltpu.CompilerParams(vmem_limit_bytes=24 * 2**20),
        name="finish_part",
    )(everything, before, after, *kept)


def neighbours(value, axis, size):
    up = [(i, i + 1) for i in range(size - 1)]
    return (
        lax.ppermute(value, axis, up),
        lax.ppermute(value, axis, [(j, i) for i, j in up]),
    )


def shards(wide, deep, source, conductivity, ice_cells):
    tops = jnp.pad(ice_cells.astype(F32).T, ((0, 0), (0, BZ - BX)))
    packed = jnp.concatenate([source, conductivity, tops[None]], 0)
    left, right = neighbours(packed, "wide", wide)
    strip = jnp.concatenate([left, packed, right], 0)
    up, down = neighbours(strip, ("z", "core"), 2 * deep)
    fan, edge, *kept = local_part(strip, up, down, wide * deep)
    before, after = neighbours(edge, "wide", wide)
    fan = fan.reshape(wide * deep, 1, ROWS * BZ)
    rows = lax.all_to_all(fan, ("wide", "z"), 0, 0, tiled=True)
    rows = lax.all_gather(rows.reshape(wide * deep * ROWS, BZ), "core", tiled=True)
    return finish_part(wide, deep, rows, before, after, kept)


def solution(mesh):
    wide, deep = mesh.shape["wide"], mesh.shape["grp"] // 2
    split = Mesh(mesh.devices.reshape(wide, deep, 2), ("wide", "z", "core"))
    group = ("z", "core")
    return jax.shard_map(
        functools.partial(shards, wide, deep),
        mesh=split,
        in_specs=(P("wide", group, None), P("wide", group, None), P("wide", group)),
        out_specs=P("wide", group, None),
        check_vma=False,
    )
```

```python
import functools

import jax
import jax.numpy as jnp
from jax import lax
from jax.experimental import pallas as pl
from jax.experimental.pallas import tpu as pltpu
from jax.sharding import Mesh
from jax.sharding import PartitionSpec as P

ITERS = 6

cheb_center = (2.0 + 0.3) / 2.0
cheb_radius = (2.0 - 0.3) / 2.0
first_ratio = cheb_radius / cheb_center
second_ratio = 1.0 / (2.0 * cheb_center / cheb_radius - first_ratio)
carry_weight = second_ratio * first_ratio
fresh_weight = 2.0 * second_ratio / cheb_radius
inverse_center = 1.0 / cheb_center

F32 = jnp.float32
BX, BY, BZ = 8, 16, 128
PACK = 2 * BX + 1
EX, EY = 3 * BX, 3 * BY
MX, MY = EX // 2, EY // 2
TX, TY = 12, 32
X0, Y0 = 6, 8
BLOCK = 4
ROWS = 5


def lane_index(shape):
    return lax.broadcasted_iota(jnp.int32, shape, len(shape) - 1)


def pair_weight(factor, coef, neighbour):
    total = coef + neighbour
    return (2.0 * factor) * coef * neighbour / jnp.where(total > 0.0, total, 1.0)


def shift(value, amount, axis):
    return pltpu.roll(value, amount % value.shape[axis], axis)


def operate(before, value, after, weight_x, weight_x_before, weight_y, weight_z, diagonal, active, step_z):
    coupled = weight_x * after + weight_x_before * before
    coupled = coupled + weight_y * shift(value, -1, 0)
    coupled = coupled + shift(weight_y * value, 1, 0)
    coupled = coupled + weight_z * shift(value, -step_z, 1)
    coupled = coupled + shift(weight_z * value, step_z, 1)
    return active * (diagonal * value - coupled)


def pair_lanes(value, step, combine):
    lanes = lane_index(value.shape)
    other = jnp.where((lanes & step) == 0, shift(value, -step, 1), shift(value, step, 1))
    return combine(value, other)


def loop(low, high, step, body):
    assert (high - low) % step == 0

    def turn(i, carry):
        for k in range(step):
            body(low + i * step + k, k)
        return carry

    lax.fori_loop(0, (high - low) // step, turn, 0)


def face_weights(factor, coef_ref, wx_ref, wy_ref, wz_ref, extent, step_z):
    def body(x, slot):
        coef = coef_ref[x]
        lanes = lane_index(coef.shape)
        wx_ref[x] = pair_weight(factor, coef_ref[jnp.maximum(x - 1, 0)], coef)
        wy_ref[x] = pair_weight(factor, coef, shift(coef, -1, 0))
        weight = pair_weight(factor, coef, shift(coef, -step_z, 1))
        wz_ref[x] = jnp.where(lanes >= BZ - step_z, 0.0, weight)

    loop(0, extent, 2, body)
    wx_ref[0] = jnp.zeros(wx_ref.shape[1:], F32)
    wx_ref[extent] = jnp.zeros(wx_ref.shape[1:], F32)


def diagonal_of(factor, x, coef_ref, wx_ref, wy_ref, wz_ref, step_z):
    coef = coef_ref[x]
    lanes = lane_index(coef.shape)
    weight_y, weight_z = wy_ref[x], wz_ref[x]
    top = jnp.where(lanes >= BZ - step_z, factor * coef, weight_z)
    total = wx_ref[x + 1] + wx_ref[x] + weight_y + shift(weight_y, 1, 0)
    return total + top + shift(weight_z, step_z, 1)


def inverse_of(diagonal):
    return 1.0 / jnp.where(diagonal > 0.0, diagonal, 1.0)


def local_kernel(
    own_ref, up_ref, down_ref,
    fan_ref, edge_ref,
    load1_ref, active1_ref, wx1_ref, wy1_ref, wz1_ref, diag1_ref, inv1_ref, smooth1_ref,
    load0_ref, active0_ref, wx0_ref, wy0_ref, wz0_ref, diag0_ref, inv0_ref, smooth0_ref,
    source, coef, active, wx, wy, wz, diag, inv, update, smooth, coef1, update1, pairs, tops, coarse,
):
    for j in range(3):
        def gather(i, slot, j=j):
            for target, row in ((source, 0), (coef, BX)):
                for k, ref in enumerate((up_ref, own_ref, down_ref)):
                    target[j * BX + i, k * BY:(k + 1) * BY, :] = ref[j * PACK + row + i]

        loop(0, BX, 2, gather)
        for i in range(BX):
            for k, ref in enumerate((up_ref, own_ref, down_ref)):
                column = ref[j * PACK + 2 * BX, :, i:i + 1]
                active[j * BX + i, k * BY:(k + 1) * BY, :] = jnp.broadcast_to(column, (BY, BZ))

    def middle_tops(x, slot):
        pairs[slot] = jnp.maximum(active[2 * x], active[2 * x + 1])
        value = jnp.maximum(
            pairs[slot, pl.ds(0, MY, stride=2), :], pairs[slot, pl.ds(1, MY, stride=2), :]
        )
        tops[x] = value
        layer = (lane_index((MY, BZ)) & ~1).astype(F32)
        active1_ref[x] = (layer < value).astype(F32)

    loop(0, MX, 2, middle_tops)

    def fine_mask(x, slot):
        layer = lane_index((EY, BZ)).astype(F32)
        mask = (layer < active[x]).astype(F32)
        active[x] = mask
        source[x] = mask * source[x]

    loop(0, EX, 2, fine_mask)

    face_weights(1.0, coef, wx, wy, wz, EX, 1)

    def fine_start(x, slot):
        diagonal = diagonal_of(1.0, x, coef, wx, wy, wz, 1)
        inverse = inverse_of(diagonal)
        diag[x] = diagonal
        inv[x] = inverse
        update[x] = source[x] * (inverse * inverse_center)

    loop(0, EX, 2, fine_start)

    def fine_operate(ref, x):
        return operate(ref[x - 1], ref[x], ref[x + 1], wx[x + 1], wx[x], wy[x], wz[x], diag[x], active[x], 1)

    def fine_finish(x, slot):
        residual = source[x] - fine_operate(update, x)
        first = update[x]
        smooth[x] = first + (carry_weight * first + fresh_weight * residual * inv[x])

    smooth[0] = jnp.zeros((EY, BZ), F32)
    smooth[EX - 1] = jnp.zeros((EY, BZ), F32)
    loop(1, EX - 1, 2, fine_finish)

    def keep(i, slot):
        for kept, ref in (
            (load0_ref, source), (active0_ref, active), (wy0_ref, wy), (wz0_ref, wz),
            (diag0_ref, diag), (inv0_ref, inv), (smooth0_ref, smooth),
        ):
            kept[i] = ref[X0 + i, Y0:Y0 + TY, :]
        wx0_ref[i] = wx[X0 + i, Y0:Y0 + TY, :]

    loop(0, TX, 2, keep)

    def restrict(value, slot):
        pairs[slot] = pair_lanes(value, 1, jnp.add)
        return pairs[slot, pl.ds(0, MY, stride=2), :] + pairs[slot, pl.ds(1, MY, stride=2), :]

    def middle_coef(x, slot):
        coef1[x] = restrict(coef[2 * x] + coef[2 * x + 1], slot) * 0.125

    loop(0, MX, 2, middle_coef)

    def middle_load(x, slot):
        left = source[2 * x] - fine_operate(smooth, 2 * x)
        right = source[2 * x + 1] - fine_operate(smooth, 2 * x + 1)
        load1_ref[x] = restrict(left + right, slot)

    for x in (0, 1, MX - 2, MX - 1):
        load1_ref[x] = jnp.zeros((MY, BZ), F32)
    loop(2, MX - 2, 2, middle_load)

    face_weights(2.0, coef1, wx1_ref, wy1_ref, wz1_ref, MX, 2)

    def middle_start(x, slot):
        diagonal = diagonal_of(2.0, x, coef1, wx1_ref, wy1_ref, wz1_ref, 2)
        inverse = inverse_of(diagonal)
        diag1_ref[x] = diagonal
        inv1_ref[x] = inverse
        update1[x] = load1_ref[x] * (inverse * inverse_center)

    loop(0, MX, 4, middle_start)

    def middle_operate(ref, x):
        return operate(
            ref[x - 1], ref[x], ref[x + 1], wx1_ref[x + 1], wx1_ref[x], wy1_ref[x], wz1_ref[x],
            diag1_ref[x], active1_ref[x], 2,
        )

    def middle_finish(x, slot):
        residual = load1_ref[x] - middle_operate(update1, x)
        first = update1[x]
        smooth1_ref[x] = first + (carry_weight * first + fresh_weight * residual * inv1_ref[x])

    for x in (0, 1, 2, MX - 3, MX - 2, MX - 1):
        smooth1_ref[x] = jnp.zeros((MY, BZ), F32)
    loop(3, MX - 3, 3, middle_finish)
    for i in range(2):
        edge_ref[i] = smooth1_ref[MX // 2 - 1 + i]

    first_x, first_y = MX // 3, MY // 3
    rows = []
    for part in range(2):
        for cx in range(2):
            if part == 0:
                total = sum(
                    load1_ref[x] - middle_operate(smooth1_ref, x)
                    for x in (first_x + 2 * cx, first_x + 2 * cx + 1)
                )
            else:
                total = (coef1[first_x + 2 * cx] + coef1[first_x + 2 * cx + 1]) * 0.125
            coarse[...] = pair_lanes(total, 2, jnp.add)
            value = (
                coarse[pl.ds(first_y, 4, stride=2), :] + coarse[pl.ds(first_y + 1, 4, stride=2), :]
            )
            rows.append(jnp.concatenate([value[i:i + 1] for i in range(4)], 1))
    spread = jnp.concatenate(rows + [jnp.zeros((4, 4 * BZ), F32)], 0)
    entry = lax.broadcasted_iota(jnp.int32, (4 * BZ, BZ), 0)
    lanes = lane_index((4 * BZ, BZ))
    chosen = (entry // BZ == lanes // 32) & (entry % BZ == (lanes % 32) * 4)
    packed = jnp.dot(
        spread, chosen.astype(F32), precision=lax.Precision.HIGHEST, preferred_element_type=F32
    )
    lanes = lane_index((1, BZ))
    top_row = jnp.zeros((1, BZ), F32)
    for cx in range(2):
        coarse[...] = jnp.maximum(tops[first_x + 2 * cx], tops[first_x + 2 * cx + 1])
        value = jnp.maximum(
            coarse[pl.ds(first_y, 4, stride=2), :], coarse[pl.ds(first_y + 1, 4, stride=2), :]
        )
        for cy in range(4):
            top_row = jnp.where(lanes // 16 == 2 * cy + cx, value[cy:cy + 1], top_row)
    block = [packed[i:i + 1] for i in range(4)] + [top_row]
    pattern = jnp.concatenate(block * 8, 0)

    def fan(i, carry):
        fan_ref[pl.ds(pl.multiple_of(i * 8 * ROWS, 8), 8 * ROWS), :] = pattern
        return carry

    lax.fori_loop(0, fan_ref.shape[0] // (8 * ROWS), fan, 0)


def finish_kernel(
    wide, deep, mine_ref, other_ref, before_ref, after_ref,
    load1_ref, active1_ref, wx1_ref, wy1_ref, wz1_ref, diag1_ref, inv1_ref, smooth1_ref,
    load0_ref, active0_ref, wx0_ref, wy0_ref, wz0_ref, diag0_ref, inv0_ref, smooth0_ref,
    out_ref,
    coef, active, wx, wy, wz, diag, residual, image, slope, direction, solution, wanted, spread,
    guess1, update1, second1, children, guess0, update0, second0,
):
    count = 2 * wide
    vector = (deep, BZ)
    lanes = lane_index((BLOCK, deep, BZ))
    zero = jnp.zeros(vector, F32)
    pad = 2

    def pair(first, second):
        return jnp.stack([first, second], 1)

    def y_after(value):
        turned = shift(value, -32, 3)
        first, second = turned[:, 0], turned[:, 1]
        inside = lanes < 96
        return pair(jnp.where(inside, first, second), jnp.where(inside, second, shift(first, -1, 1)))

    def y_before(value):
        turned = shift(value, 32, 3)
        first, second = turned[:, 0], turned[:, 1]
        inside = lanes >= 32
        return pair(jnp.where(inside, first, shift(second, 1, 1)), jnp.where(inside, second, first))

    for ref, spare in ((residual, (*range(pad), *range(count + pad, count + 2 * pad))), (image, (count,)), (slope, (count,))):
        for x in spare:
            ref[x] = jnp.zeros((2, *vector), F32)

    stride = deep * ROWS
    flat = lane_index(vector)
    low = (flat & 16) == 0
    layer = ((flat & 31) * 4).astype(F32)

    def unpack(refs):
        def body(w, slot):
            for c in range(2):
                top, *rows = (
                    refs[c][pl.ds(w * stride + k, deep, stride=ROWS), :] for k in (4, 0, 1, 2, 3)
                )
                tall = (
                    jnp.where(low, top, shift(top, 16, 1)), jnp.where(low, shift(top, -16, 1), top)
                )
                for i in range(2):
                    residual[2 * w + i + pad, c] = rows[i]
                    coef[2 * w + i, c] = rows[2 + i]
                    active[2 * w + i, c] = (layer < tall[i]).astype(F32)

        loop(0, wide, 2, body)

    own_core = lax.axis_index("core")

    @pl.when(own_core == 0)
    def _():
        unpack((mine_ref, other_ref))

    @pl.when(own_core == 1)
    def _():
        unpack((other_ref, mine_ref))

    lanes4 = lane_index((BLOCK, 2, deep, BZ))
    highest = (lanes4 & 31) == 31
    shape4 = (BLOCK, 2, deep, BZ)
    last_y = (
        (lanes4 >= 96)
        & (lax.broadcasted_iota(jnp.int32, shape4, 1) == 1)
        & (lax.broadcasted_iota(jnp.int32, shape4, 2) == deep - 1)
    )

    def coarse_weight(a, b):
        return 8.0 * a * b / (a + b)

    def weights(i, previous):
        x = i * BLOCK
        here = coef[pl.ds(x, BLOCK)]
        there = jnp.concatenate([previous, here[:-1]], 0)
        wx[pl.ds(x, BLOCK)] = coarse_weight(there, here)
        wy[pl.ds(x, BLOCK)] = jnp.where(last_y, 0.0, coarse_weight(here, y_after(here)))
        wz[pl.ds(x, BLOCK)] = jnp.where(highest, 0.0, coarse_weight(here, shift(here, -1, 3)))
        return here[-1:]

    lax.fori_loop(0, count // BLOCK, weights, coef[0:1])
    wx[0] = jnp.zeros((2, *vector), F32)
    wx[count] = jnp.zeros((2, *vector), F32)

    def diagonals(i, carry):
        x = i * BLOCK
        weight_y, weight_z = wy[pl.ds(x, BLOCK)], wz[pl.ds(x, BLOCK)]
        top = jnp.where(highest, 4.0 * coef[pl.ds(x, BLOCK)], weight_z)
        value = wx[pl.ds(x + 1, BLOCK)] + wx[pl.ds(x, BLOCK)] + weight_y + y_before(weight_y)
        diag[pl.ds(x, BLOCK)] = value + top + shift(weight_z, 1, 3)
        return carry

    lax.fori_loop(0, count // BLOCK, diagonals, 0)

    def whole(total):
        return jnp.sum(jnp.sum(total, axis=0, keepdims=True), axis=1, keepdims=True)

    def fold(total, value):
        return total + jnp.sum(value, axis=(0, 1))

    first = 2 * lax.axis_index("wide")
    ratio = scale = norm = jnp.zeros((1, 1), F32)
    for iteration in range(ITERS):
        start = iteration == 0
        if not start:
            wide_ratio = jnp.broadcast_to(ratio, vector)[None, None]
            wide_scale = jnp.broadcast_to(scale, vector)[None, None]

        def renew(x, size):
            value = residual[pl.ds(x + pad, size)]
            if start:
                return value
            slope_here = image[pl.ds(x, size)]
            if iteration > 1:
                slope_here = slope_here + wide_ratio * slope[pl.ds(x, size)]
            if iteration < ITERS - 1:
                slope[pl.ds(x, size)] = slope_here
            value = value - wide_scale * slope_here
            residual[pl.ds(x + pad, size)] = value
            return value

        def apply(i, carry):
            x = i * BLOCK
            norm_sum, image_sum, last = carry
            grown = jnp.concatenate([last, renew(x + 1, BLOCK)], 0)
            before, here, after = grown[:BLOCK], grown[1:BLOCK + 1], grown[2:]
            weight_y, weight_z = wy[pl.ds(x, BLOCK)], wz[pl.ds(x, BLOCK)]
            coupled = wx[pl.ds(x + 1, BLOCK)] * after + wx[pl.ds(x, BLOCK)] * before
            coupled = coupled + weight_y * y_after(here) + y_before(weight_y * here)
            coupled = coupled + weight_z * shift(here, -1, 3) + shift(weight_z * here, 1, 3)
            value = active[pl.ds(x, BLOCK)] * (diag[pl.ds(x, BLOCK)] * here - coupled)
            image[pl.ds(x, BLOCK)] = value
            return fold(norm_sum, here * here), fold(image_sum, here * value), grown[BLOCK:]

        opening = jnp.concatenate([jnp.zeros((1, 2, *vector), F32), renew(0, 1)], 0)
        norm_sum, image_sum, _ = lax.fori_loop(0, count // BLOCK, apply, (zero, zero, opening))
        fresh, curvature = whole(norm_sum), whole(image_sum)
        here = residual[pl.ds(first, 6)]
        if start:
            scale = fresh / curvature
            direction[...] = here
            solution[...] = jnp.broadcast_to(scale, vector)[None, None] * here
        else:
            ratio = fresh / norm
            scale = fresh / (curvature - ratio * fresh / scale)
            here = here + jnp.broadcast_to(ratio, vector)[None, None] * direction[...]
            direction[...] = here
            solution[...] = solution[...] + jnp.broadcast_to(scale, vector)[None, None] * here
        norm = fresh

    position = 2 * lax.axis_index("z") + own_core
    wanted[...] = jnp.zeros(wanted.shape, F32)
    for j in range(3):
        group = jnp.clip(position + j - 1, 0, 2 * deep - 1)
        core, row = group & 1, group >> 1
        for i in range(6):
            wanted[3 * i + j:3 * i + j + 1, :] = solution[i, core, pl.ds(row, 1), :]
    entry = lax.broadcasted_iota(jnp.int32, (BZ, 4 * BZ), 0)
    columns = lane_index((BZ, 4 * BZ))
    chosen = entry == (columns // BZ) * 32 + (columns % BZ) // 4
    spread[...] = jnp.dot(
        wanted[...], chosen.astype(F32), precision=lax.Precision.HIGHEST, preferred_element_type=F32
    )
    for i in range(6):
        rows = []
        for y in range(12):
            r, c = 3 * i + y // 4, y % 4
            row = spread[r:r + 1, c * BZ:(c + 1) * BZ]
            rows.append(jnp.broadcast_to(row, (2, BZ)))
        parent = jnp.concatenate(rows, 0)
        for x in (2 * i, 2 * i + 1):
            if x in (0, MX - 1):
                continue
            if x <= 2:
                value = before_ref[x - 1]
            elif x >= MX - 3:
                value = after_ref[x - (MX - 3)]
            else:
                value = smooth1_ref[x]
            guess1[x] = value + active1_ref[x] * parent

    def middle_operate(ref, x):
        return operate(
            ref[x - 1], ref[x], ref[x + 1], wx1_ref[x + 1], wx1_ref[x], wy1_ref[x], wz1_ref[x],
            diag1_ref[x], active1_ref[x], 2,
        )

    def middle_first(x, slot):
        residual_here = load1_ref[x] - middle_operate(guess1, x)
        value = residual_here * (inv1_ref[x] * inverse_center)
        update1[x] = value
        second1[x] = guess1[x] + value

    loop(2, MX - 2, 4, middle_first)

    def middle_second(x, slot):
        residual_here = load1_ref[x] - middle_operate(second1, x)
        value = second1[x] + (
            carry_weight * update1[x] + fresh_weight * residual_here * inv1_ref[x]
        )
        guess1[x] = value

    loop(3, MX - 3, 3, middle_second)

    def fine_guess(x, slot):
        value = guess1[x]
        children[slot, pl.ds(0, MY, stride=2), :] = value
        children[slot, pl.ds(1, MY, stride=2), :] = value
        child = children[slot, Y0:Y0 + TY, :]
        for i in range(2):
            k = 2 * x + i - X0
            guess0[k] = smooth0_ref[k] + active0_ref[k] * child

    loop(X0 // 2, (X0 + TX) // 2, 2, fine_guess)

    def fine_operate(ref, x):
        return operate(
            ref[x - 1], ref[x], ref[x + 1], wx0_ref[x + 1], wx0_ref[x], wy0_ref[x], wz0_ref[x],
            diag0_ref[x], active0_ref[x], 1,
        )

    def fine_first(x, slot):
        residual_here = load0_ref[x] - fine_operate(guess0, x)
        value = residual_here * (inv0_ref[x] * inverse_center)
        update0[x] = value
        second0[x] = guess0[x] + value

    loop(1, TX - 1, 2, fine_first)
    margin = BX - X0

    def fine_second(x, slot):
        residual_here = load0_ref[x] - fine_operate(second0, x)
        value = second0[x] + (
            carry_weight * update0[x] + fresh_weight * residual_here * inv0_ref[x]
        )
        out_ref[x - margin] = value[BY - Y0:2 * BY - Y0]

    loop(margin, margin + BX, 2, fine_second)


def in_vmem(count):
    return [pl.BlockSpec(memory_space=pltpu.VMEM)] * count


def grids(count, *shape):
    return [jax.ShapeDtypeStruct(shape, F32)] * count


def scratch(count, *shape):
    return [pltpu.VMEM(shape, F32)] * count


def local_part(strip, up, down, fan):
    middle = grids(8, MX, MY, BZ)
    middle[2] = jax.ShapeDtypeStruct((MX + 1, MY, BZ), F32)
    outs = (
        grids(1, fan * ROWS, BZ) + grids(1, 2, MY, BZ) + middle + grids(8, TX, TY, BZ)
    )
    big = scratch(10, EX, EY, BZ)
    big[3] = pltpu.VMEM((EX + 1, EY, BZ), F32)
    return pl.pallas_call(
        local_kernel,
        out_shape=outs,
        in_specs=in_vmem(3),
        out_specs=in_vmem(len(outs)),
        scratch_shapes=big + scratch(2, MX, MY, BZ) + scratch(1, 2, EY, BZ)
        + scratch(1, MX, MY, BZ) + scratch(1, MY, BZ),
        compiler_params=pltpu.CompilerParams(vmem_limit_bytes=24 * 2**20),
        name="local_part",
    )(strip, up, down)


def finish_part(wide, deep, mine, other, before, after, kept):
    count = 2 * wide
    tile = (2, deep, BZ)
    return pl.pallas_call(
        functools.partial(finish_kernel, wide, deep),
        out_shape=jax.ShapeDtypeStruct((BX, BY, BZ), F32),
        in_specs=in_vmem(4 + len(kept)),
        out_specs=pl.BlockSpec(memory_space=pltpu.VMEM),
        scratch_shapes=scratch(2, count, *tile) + scratch(1, count + 1, *tile)
        + scratch(3, count, *tile) + scratch(1, count + 4, *tile) + scratch(2, count + 1, *tile)
        + scratch(2, 6, *tile) + scratch(1, 24, BZ) + scratch(1, 24, 4 * BZ)
        + scratch(3, MX, MY, BZ) + scratch(1, 2, EY, BZ) + scratch(3, TX, TY, BZ),
        compiler_params=pltpu.CompilerParams(vmem_limit_bytes=24 * 2**20),
        name="finish_part",
    )(mine, other, before, after, *kept)


def neighbours(value, axis, size):
    up = [(i, i + 1) for i in range(size - 1)]
    return (
        lax.ppermute(value, axis, up),
        lax.ppermute(value, axis, [(j, i) for i, j in up]),
    )


def pack_kernel(source_ref, coef_ref, tops_ref, out_ref, tops, sems):
    copies = (
        pltpu.make_async_copy(tops_ref, tops, sems.at[0]),
        pltpu.make_async_copy(source_ref, out_ref.at[pl.ds(0, BX)], sems.at[1]),
        pltpu.make_async_copy(coef_ref, out_ref.at[pl.ds(BX, BX)], sems.at[2]),
    )
    for copy in copies:
        copy.start()
    copies[0].wait()
    values = tops[...].astype(F32)
    same = lax.broadcasted_iota(jnp.int32, (BY, BY), 0) == lane_index((BY, BY))
    lanes = lane_index((BY, BZ))
    turned = jnp.zeros((BY, BZ), F32)
    for x in range(BX):
        column = jnp.sum(jnp.where(same, values[x:x + 1], 0.0), axis=1, keepdims=True)
        turned = jnp.where(lanes == x, column, turned)
    out_ref[2 * BX] = turned
    for copy in copies[1:]:
        copy.wait()


def pack_part(source, conductivity, ice_cells):
    return pl.pallas_call(
        pack_kernel,
        out_shape=jax.ShapeDtypeStruct((PACK, BY, BZ), F32),
        in_specs=[pl.BlockSpec(memory_space=pl.ANY)] * 3,
        out_specs=pl.BlockSpec(memory_space=pltpu.VMEM),
        scratch_shapes=[pltpu.VMEM((BX, BY), jnp.int32), pltpu.SemaphoreType.DMA((3,))],
        name="pack_part",
    )(source, conductivity, ice_cells)


def shards(wide, deep, source, conductivity, ice_cells):
    packed = pack_part(source, conductivity, ice_cells)
    left, right = neighbours(packed, "wide", wide)
    strip = jnp.concatenate([left, packed, right], 0)
    up, down = neighbours(strip, ("z", "core"), 2 * deep)
    fan, edge, *kept = local_part(strip, up, down, wide * deep)
    before, after = neighbours(edge, "wide", wide)
    fan = fan.reshape(wide * deep, 1, ROWS * BZ)
    mine = lax.all_to_all(fan, ("wide", "z"), 0, 0, tiled=True).reshape(wide * deep * ROWS, BZ)
    other = lax.ppermute(mine, "core", [(0, 1), (1, 0)])
    return finish_part(wide, deep, mine, other, before, after, kept)


def solution(mesh):
    wide, deep = mesh.shape["wide"], mesh.shape["grp"] // 2
    split = Mesh(mesh.devices.reshape(wide, deep, 2), ("wide", "z", "core"))
    group = ("z", "core")
    return jax.shard_map(
        functools.partial(shards, wide, deep),
        mesh=split,
        in_specs=(P("wide", group, None), P("wide", group, None), P("wide", group)),
        out_specs=P("wide", group, None),
        check_vma=False,
    )
```

```python
import functools

import jax
import jax.numpy as jnp
from jax import lax
from jax.experimental import pallas as pl
from jax.experimental.pallas import tpu as pltpu
from jax.sharding import Mesh
from jax.sharding import PartitionSpec as P

ITERS = 6

cheb_center = (2.0 + 0.3) / 2.0
cheb_radius = (2.0 - 0.3) / 2.0
first_ratio = cheb_radius / cheb_center
second_ratio = 1.0 / (2.0 * cheb_center / cheb_radius - first_ratio)
carry_weight = second_ratio * first_ratio
fresh_weight = 2.0 * second_ratio / cheb_radius
inverse_center = 1.0 / cheb_center

F32 = jnp.float32
BX, BY, BZ = 8, 16, 128
PACK = 2 * BX + 1
NS, NC = 6, 7
SIDE = NS + NC + 1
STRIP = 2 * SIDE + PACK
HALF = 4
EX, EY = 3 * BX, 3 * BY
MX, MY = EX // 2, EY // 2
TX, TY = 12, 32
X0, Y0 = 6, 8
BLOCK = 16
ROWS = 5


def lane_index(shape):
    return lax.broadcasted_iota(jnp.int32, shape, len(shape) - 1)


def pair_weight(factor, coef, neighbour):
    total = coef + neighbour
    return (2.0 * factor) * coef * neighbour / jnp.where(total > 0.0, total, 1.0)


def shift(value, amount, axis):
    return pltpu.roll(value, amount % value.shape[axis], axis)


def operate(before, value, after, weight_x, weight_x_before, weight_y, weight_z, diagonal, active, step_z):
    coupled = weight_x * after + weight_x_before * before
    coupled = coupled + weight_y * shift(value, -1, 0)
    coupled = coupled + shift(weight_y * value, 1, 0)
    coupled = coupled + weight_z * shift(value, -step_z, 1)
    coupled = coupled + shift(weight_z * value, step_z, 1)
    return active * (diagonal * value - coupled)


def pair_lanes(value, step, combine):
    lanes = lane_index(value.shape)
    other = jnp.where((lanes & step) == 0, shift(value, -step, 1), shift(value, step, 1))
    return combine(value, other)


def loop(low, high, step, body):
    assert (high - low) % step == 0

    def turn(i, carry):
        for k in range(step):
            body(low + i * step + k, k)
        return carry

    lax.fori_loop(0, (high - low) // step, turn, 0)


def face_weights(factor, coef_ref, wx_ref, wy_ref, wz_ref, low, high, step, step_z):
    def body(x, slot):
        coef = coef_ref[x]
        lanes = lane_index(coef.shape)
        wx_ref[x + 1] = pair_weight(factor, coef, coef_ref[x + 1])
        wy_ref[x] = pair_weight(factor, coef, shift(coef, -1, 0))
        weight = pair_weight(factor, coef, shift(coef, -step_z, 1))
        wz_ref[x] = jnp.where(lanes >= BZ - step_z, 0.0, weight)

    wx_ref[low] = pair_weight(factor, coef_ref[low - 1], coef_ref[low])
    loop(low, high, step, body)


def diagonal_of(factor, x, coef_ref, wx_ref, wy_ref, wz_ref, step_z):
    coef = coef_ref[x]
    lanes = lane_index(coef.shape)
    weight_y, weight_z = wy_ref[x], wz_ref[x]
    top = jnp.where(lanes >= BZ - step_z, factor * coef, weight_z)
    total = wx_ref[x + 1] + wx_ref[x] + weight_y + shift(weight_y, 1, 0)
    return total + top + shift(weight_z, step_z, 1)


def inverse_of(diagonal):
    return 1.0 / jnp.where(diagonal > 0.0, diagonal, 1.0)


def strip_kernel(own_ref, before_ref, after_ref, up_ref, down_ref):
    for i in range(STRIP):
        if i < SIDE:
            row = before_ref[i]
        elif i < SIDE + PACK:
            row = own_ref[i - SIDE]
        else:
            row = after_ref[i - SIDE - PACK]
        k, part = STRIP + i // 2, slice(HALF * (i % 2), HALF * (i % 2 + 1))
        up_ref[i] = row[BY - 8:]
        up_ref[k, part] = row[BY - 8 - HALF:BY - 8]
        down_ref[i] = row[:8]
        down_ref[k, part] = row[8:8 + HALF]


def local_kernel(
    own_ref, before_ref, after_ref, up_ref, down_ref,
    fan_ref, edge_ref,
    load1_ref, active1_ref, wx1_ref, wy1_ref, wz1_ref, diag1_ref, inv1_ref, smooth1_ref,
    load0_ref, active0_ref, wx0_ref, wy0_ref, wz0_ref, diag0_ref, inv0_ref, smooth0_ref,
    source, coef, active, wx, wy, wz, diag, inv, update, smooth, coef1, update1, pairs, tops, coarse,
):
    edge_rows = jnp.zeros((8 - HALF, BZ), F32)

    def extended(i):
        if i < SIDE:
            own = before_ref[i]
        elif i < SIDE + PACK:
            own = own_ref[i - SIDE]
        else:
            own = after_ref[i - SIDE - PACK]
        k, part = STRIP + i // 2, slice(HALF * (i % 2), HALF * (i % 2 + 1))
        return jnp.concatenate(
            [edge_rows, up_ref[k, part], up_ref[i], own, down_ref[i], down_ref[k, part], edge_rows], 0
        )

    middle = SIDE
    last = SIDE + PACK
    for i in range(NS):
        source[BX - NS + i] = extended(i)
        source[2 * BX + i] = extended(last + i)
    for i in range(NC):
        coef[BX - NC + i] = extended(NS + i)
        coef[2 * BX + i] = extended(last + NS + i)
    for i in range(BX):
        source[BX + i] = extended(middle + i)
        coef[BX + i] = extended(middle + BX + i)
    for j, i in enumerate((SIDE - 1, last - 1, STRIP - 1)):
        columns = extended(i)
        for x in range(BX):
            active[j * BX + x] = jnp.broadcast_to(columns[:, x:x + 1], (EY, BZ))

    low0, high0 = BX - NS, 2 * BX + NS
    low1, high1 = low0 // 2 + 1, high0 // 2 - 1

    def middle_tops(x, slot):
        pairs[slot] = jnp.maximum(active[2 * x], active[2 * x + 1])
        value = jnp.maximum(
            pairs[slot, pl.ds(0, MY, stride=2), :], pairs[slot, pl.ds(1, MY, stride=2), :]
        )
        tops[x] = value
        layer = (lane_index((MY, BZ)) & ~1).astype(F32)
        active1_ref[x] = (layer < value).astype(F32)

    loop(0, MX, 2, middle_tops)

    def fine_mask(x, slot):
        layer = lane_index((EY, BZ)).astype(F32)
        mask = (layer < active[x]).astype(F32)
        active[x] = mask
        source[x] = mask * source[x]

    loop(low0, high0, 2, fine_mask)

    face_weights(1.0, coef, wx, wy, wz, low0, high0, 2, 1)

    def fine_start(x, slot):
        diagonal = diagonal_of(1.0, x, coef, wx, wy, wz, 1)
        inverse = inverse_of(diagonal)
        diag[x] = diagonal
        inv[x] = inverse
        update[x] = source[x] * (inverse * inverse_center)

    loop(low0, high0, 2, fine_start)

    def fine_operate(ref, x):
        return operate(ref[x - 1], ref[x], ref[x + 1], wx[x + 1], wx[x], wy[x], wz[x], diag[x], active[x], 1)

    def fine_finish(x, slot):
        residual = source[x] - fine_operate(update, x)
        first = update[x]
        smooth[x] = first + (carry_weight * first + fresh_weight * residual * inv[x])

    loop(low0 + 1, high0 - 1, 2, fine_finish)

    def keep(i, slot):
        for kept, ref in (
            (load0_ref, source), (active0_ref, active), (wy0_ref, wy), (wz0_ref, wz),
            (diag0_ref, diag), (inv0_ref, inv), (smooth0_ref, smooth),
        ):
            kept[i] = ref[X0 + i, Y0:Y0 + TY, :]
        wx0_ref[i] = wx[X0 + i, Y0:Y0 + TY, :]

    loop(0, TX, 2, keep)

    def restrict(value, slot):
        pairs[slot] = pair_lanes(value, 1, jnp.add)
        return pairs[slot, pl.ds(0, MY, stride=2), :] + pairs[slot, pl.ds(1, MY, stride=2), :]

    def middle_coef(x, slot):
        coef1[x] = restrict(coef[2 * x] + coef[2 * x + 1], slot) * 0.125

    loop(low1 - 1, high1 + 1, 2, middle_coef)

    def middle_load(x, slot):
        left = source[2 * x] - fine_operate(smooth, 2 * x)
        right = source[2 * x + 1] - fine_operate(smooth, 2 * x + 1)
        load1_ref[x] = restrict(left + right, slot)

    loop(low1, high1, 2, middle_load)

    face_weights(2.0, coef1, wx1_ref, wy1_ref, wz1_ref, low1, high1, 4, 2)

    def middle_start(x, slot):
        diagonal = diagonal_of(2.0, x, coef1, wx1_ref, wy1_ref, wz1_ref, 2)
        inverse = inverse_of(diagonal)
        diag1_ref[x] = diagonal
        inv1_ref[x] = inverse
        update1[x] = load1_ref[x] * (inverse * inverse_center)

    loop(low1, high1, 4, middle_start)

    def middle_operate(ref, x):
        return operate(
            ref[x - 1], ref[x], ref[x + 1], wx1_ref[x + 1], wx1_ref[x], wy1_ref[x], wz1_ref[x],
            diag1_ref[x], active1_ref[x], 2,
        )

    def middle_finish(x, slot):
        residual = load1_ref[x] - middle_operate(update1, x)
        first = update1[x]
        smooth1_ref[x] = first + (carry_weight * first + fresh_weight * residual * inv1_ref[x])

    loop(low1 + 1, high1 - 1, 3, middle_finish)
    for i in range(2):
        edge_ref[i] = smooth1_ref[MX // 2 - 1 + i]

    first_x, first_y = MX // 3, MY // 3
    rows = []
    for part in range(2):
        for cx in range(2):
            if part == 0:
                total = sum(
                    load1_ref[x] - middle_operate(smooth1_ref, x)
                    for x in (first_x + 2 * cx, first_x + 2 * cx + 1)
                )
            else:
                total = (coef1[first_x + 2 * cx] + coef1[first_x + 2 * cx + 1]) * 0.125
            coarse[...] = pair_lanes(total, 2, jnp.add)
            value = (
                coarse[pl.ds(first_y, 4, stride=2), :] + coarse[pl.ds(first_y + 1, 4, stride=2), :]
            )
            rows.append(jnp.concatenate([value[i:i + 1] for i in range(4)], 1))
    spread = jnp.concatenate(rows + [jnp.zeros((4, 4 * BZ), F32)], 0)
    entry = lax.broadcasted_iota(jnp.int32, (4 * BZ, BZ), 0)
    lanes = lane_index((4 * BZ, BZ))
    chosen = (entry // BZ == lanes // 32) & (entry % BZ == (lanes % 32) * 4)
    packed = jnp.dot(
        spread, chosen.astype(F32), precision=lax.Precision.HIGHEST, preferred_element_type=F32
    )
    lanes = lane_index((1, BZ))
    top_row = jnp.zeros((1, BZ), F32)
    for cx in range(2):
        coarse[...] = jnp.maximum(tops[first_x + 2 * cx], tops[first_x + 2 * cx + 1])
        value = jnp.maximum(
            coarse[pl.ds(first_y, 4, stride=2), :], coarse[pl.ds(first_y + 1, 4, stride=2), :]
        )
        for cy in range(4):
            top_row = jnp.where(lanes // 16 == 2 * cy + cx, value[cy:cy + 1], top_row)
    block = [packed[i:i + 1] for i in range(4)] + [top_row]
    pattern = jnp.concatenate(block * 8, 0)

    def fan(i, carry):
        fan_ref[pl.ds(pl.multiple_of(i * 8 * ROWS, 8), 8 * ROWS), :] = pattern
        return carry

    lax.fori_loop(0, fan_ref.shape[0] // (8 * ROWS), fan, 0)


def finish_kernel(
    wide, deep, mine_ref, other_ref, even_ref, odd_ref,
    load1_ref, active1_ref, wx1_ref, wy1_ref, wz1_ref, diag1_ref, inv1_ref, smooth1_ref,
    load0_ref, active0_ref, wx0_ref, wy0_ref, wz0_ref, diag0_ref, inv0_ref, smooth0_ref,
    out_ref,
    coef, active, wx, wy, wz, diag, residual, image, slope, direction, solution, wanted, spread,
    guess1, update1, second1, children, guess0, update0, second0,
):
    count = 2 * wide
    vector = (deep, BZ)
    lanes = lane_index((BLOCK, deep, BZ))
    zero = jnp.zeros(vector, F32)
    pad = 2

    def pair(first, second):
        return jnp.stack([first, second], 1)

    def y_after(value):
        turned = shift(value, -32, 3)
        first, second = turned[:, 0], turned[:, 1]
        inside = lanes < 96
        return pair(jnp.where(inside, first, second), jnp.where(inside, second, shift(first, -1, 1)))

    def y_before(value):
        turned = shift(value, 32, 3)
        first, second = turned[:, 0], turned[:, 1]
        inside = lanes >= 32
        return pair(jnp.where(inside, first, shift(second, 1, 1)), jnp.where(inside, second, first))

    for ref, spare in ((residual, (*range(pad), *range(count + pad, count + 2 * pad))), (image, (count,)), (slope, (count,))):
        for x in spare:
            ref[x] = jnp.zeros((2, *vector), F32)

    stride = deep * ROWS
    flat = lane_index(vector)
    low = (flat & 16) == 0
    layer = ((flat & 31) * 4).astype(F32)

    def unpack(refs):
        def body(w, slot):
            for c in range(2):
                top, *rows = (
                    refs[c][pl.ds(w * stride + k, deep, stride=ROWS), :] for k in (4, 0, 1, 2, 3)
                )
                tall = (
                    jnp.where(low, top, shift(top, 16, 1)), jnp.where(low, shift(top, -16, 1), top)
                )
                for i in range(2):
                    residual[2 * w + i + pad, c] = rows[i]
                    coef[2 * w + i, c] = rows[2 + i]
                    active[2 * w + i, c] = (layer < tall[i]).astype(F32)

        loop(0, wide, 2, body)

    own_core = lax.axis_index("core")

    @pl.when(own_core == 0)
    def _():
        unpack((mine_ref, other_ref))

    @pl.when(own_core == 1)
    def _():
        unpack((other_ref, mine_ref))

    lanes4 = lane_index((BLOCK, 2, deep, BZ))
    highest = (lanes4 & 31) == 31
    shape4 = (BLOCK, 2, deep, BZ)
    last_y = (
        (lanes4 >= 96)
        & (lax.broadcasted_iota(jnp.int32, shape4, 1) == 1)
        & (lax.broadcasted_iota(jnp.int32, shape4, 2) == deep - 1)
    )

    def coarse_weight(a, b):
        return 8.0 * a * b / (a + b)

    coef[count] = jnp.zeros((2, *vector), F32)
    active[count] = jnp.zeros((2, *vector), F32)
    wx[0] = jnp.zeros((2, *vector), F32)

    def setup(i, face):
        x = i * BLOCK
        coefs, masks = coef[pl.ds(x, BLOCK + 1)], active[pl.ds(x, BLOCK + 1)]
        here, mask = coefs[:BLOCK], masks[:BLOCK]
        after = coarse_weight(here, coefs[1:])
        before = jnp.concatenate([face, after[:-1]], 0)
        beside = jnp.where(last_y, 0.0, coarse_weight(here, y_after(here)))
        above = coarse_weight(here, shift(here, -1, 3))
        inner = jnp.where(highest, 0.0, above)
        top = jnp.where(highest, 4.0 * here, above)
        total = after + before + beside + y_before(beside) + top + shift(inner, 1, 3)
        diag[pl.ds(x, BLOCK)] = mask * total
        wx[pl.ds(x + 1, BLOCK)] = after * (mask * masks[1:])
        wy[pl.ds(x, BLOCK)] = beside * (mask * y_after(mask))
        wz[pl.ds(x, BLOCK)] = inner * (mask * shift(mask, -1, 3))
        return after[-1:]

    lax.fori_loop(0, count // BLOCK, setup, jnp.zeros((1, 2, *vector), F32))

    def whole(total):
        return jnp.sum(jnp.sum(total, axis=0, keepdims=True), axis=1, keepdims=True)

    def fold(total, value):
        return total + jnp.sum(value, axis=(0, 1))

    first = 2 * lax.axis_index("wide")
    ratio = scale = norm = jnp.zeros((1, 1), F32)
    for iteration in range(ITERS):
        start = iteration == 0
        if not start:
            wide_ratio = jnp.broadcast_to(ratio, vector)[None, None]
            wide_scale = jnp.broadcast_to(scale, vector)[None, None]

        def renew(x, size):
            value = residual[pl.ds(x + pad, size)]
            if start:
                return value
            slope_here = image[pl.ds(x, size)]
            if iteration > 1:
                slope_here = slope_here + wide_ratio * slope[pl.ds(x, size)]
            if iteration < ITERS - 1:
                slope[pl.ds(x, size)] = slope_here
            value = value - wide_scale * slope_here
            residual[pl.ds(x + pad, size)] = value
            return value

        def apply(i, carry):
            x = i * BLOCK
            norm_sum, image_sum, last = carry
            grown = jnp.concatenate([last, renew(x + 1, BLOCK)], 0)
            before, here, after = grown[:BLOCK], grown[1:BLOCK + 1], grown[2:]
            weight_y, weight_z = wy[pl.ds(x, BLOCK)], wz[pl.ds(x, BLOCK)]
            faces = wx[pl.ds(x, BLOCK + 1)]
            coupled = faces[1:] * after + faces[:-1] * before
            coupled = coupled + weight_y * y_after(here) + y_before(weight_y * here)
            coupled = coupled + weight_z * shift(here, -1, 3) + shift(weight_z * here, 1, 3)
            value = diag[pl.ds(x, BLOCK)] * here - coupled
            image[pl.ds(x, BLOCK)] = value
            return fold(norm_sum, here * here), fold(image_sum, here * value), grown[BLOCK:]

        opening = jnp.concatenate([jnp.zeros((1, 2, *vector), F32), renew(0, 1)], 0)
        norm_sum, image_sum, _ = lax.fori_loop(0, count // BLOCK, apply, (zero, zero, opening))
        fresh, curvature = whole(norm_sum), whole(image_sum)
        here = residual[pl.ds(first, 6)]
        if start:
            scale = fresh / curvature
            direction[...] = here
            solution[...] = jnp.broadcast_to(scale, vector)[None, None] * here
        else:
            ratio = fresh / norm
            scale = fresh / (curvature - ratio * fresh / scale)
            here = here + jnp.broadcast_to(ratio, vector)[None, None] * direction[...]
            direction[...] = here
            solution[...] = solution[...] + jnp.broadcast_to(scale, vector)[None, None] * here
        norm = fresh

    position = 2 * lax.axis_index("z") + own_core
    wanted[...] = jnp.zeros(wanted.shape, F32)
    for j in range(3):
        group = jnp.clip(position + j - 1, 0, 2 * deep - 1)
        core, row = group & 1, group >> 1
        for i in range(6):
            wanted[3 * i + j:3 * i + j + 1, :] = solution[i, core, pl.ds(row, 1), :]
    entry = lax.broadcasted_iota(jnp.int32, (BZ, 4 * BZ), 0)
    columns = lane_index((BZ, 4 * BZ))
    chosen = entry == (columns // BZ) * 32 + (columns % BZ) // 4
    spread[...] = jnp.dot(
        wanted[...], chosen.astype(F32), precision=lax.Precision.HIGHEST, preferred_element_type=F32
    )
    even = lax.axis_index("wide") % 2 == 0
    for i in range(6):
        rows = []
        for y in range(12):
            r, c = 3 * i + y // 4, y % 4
            row = spread[r:r + 1, c * BZ:(c + 1) * BZ]
            rows.append(jnp.broadcast_to(row, (2, BZ)))
        parent = jnp.concatenate(rows, 0)
        for x in (2 * i, 2 * i + 1):
            if x in (0, MX - 1):
                continue
            if x <= 2:
                value = jnp.where(even, odd_ref[x - 1], even_ref[x - 1])
            elif x >= MX - 3:
                value = jnp.where(even, even_ref[x - (MX - 3)], odd_ref[x - (MX - 3)])
            else:
                value = smooth1_ref[x]
            guess1[x] = value + active1_ref[x] * parent

    def middle_operate(ref, x):
        return operate(
            ref[x - 1], ref[x], ref[x + 1], wx1_ref[x + 1], wx1_ref[x], wy1_ref[x], wz1_ref[x],
            diag1_ref[x], active1_ref[x], 2,
        )

    def middle_first(x, slot):
        residual_here = load1_ref[x] - middle_operate(guess1, x)
        value = residual_here * (inv1_ref[x] * inverse_center)
        update1[x] = value
        second1[x] = guess1[x] + value

    loop(2, MX - 2, 4, middle_first)

    def middle_second(x, slot):
        residual_here = load1_ref[x] - middle_operate(second1, x)
        value = second1[x] + (
            carry_weight * update1[x] + fresh_weight * residual_here * inv1_ref[x]
        )
        guess1[x] = value

    loop(3, MX - 3, 3, middle_second)

    def fine_guess(x, slot):
        value = guess1[x]
        children[slot, pl.ds(0, MY, stride=2), :] = value
        children[slot, pl.ds(1, MY, stride=2), :] = value
        child = children[slot, Y0:Y0 + TY, :]
        for i in range(2):
            k = 2 * x + i - X0
            guess0[k] = smooth0_ref[k] + active0_ref[k] * child

    loop(X0 // 2, (X0 + TX) // 2, 2, fine_guess)

    def fine_operate(ref, x):
        return operate(
            ref[x - 1], ref[x], ref[x + 1], wx0_ref[x + 1], wx0_ref[x], wy0_ref[x], wz0_ref[x],
            diag0_ref[x], active0_ref[x], 1,
        )

    def fine_first(x, slot):
        residual_here = load0_ref[x] - fine_operate(guess0, x)
        value = residual_here * (inv0_ref[x] * inverse_center)
        update0[x] = value
        second0[x] = guess0[x] + value

    loop(1, TX - 1, 2, fine_first)
    margin = BX - X0

    def fine_second(x, slot):
        residual_here = load0_ref[x] - fine_operate(second0, x)
        value = second0[x] + (
            carry_weight * update0[x] + fresh_weight * residual_here * inv0_ref[x]
        )
        out_ref[x - margin] = value[BY - Y0:2 * BY - Y0]

    loop(margin, margin + BX, 2, fine_second)


def in_vmem(count):
    return [pl.BlockSpec(memory_space=pltpu.VMEM)] * count


def grids(count, *shape):
    return [jax.ShapeDtypeStruct(shape, F32)] * count


def scratch(count, *shape):
    return [pltpu.VMEM(shape, F32)] * count


def strip_part(own, before, after):
    return pl.pallas_call(
        strip_kernel,
        out_shape=grids(2, STRIP + (STRIP + 1) // 2, 8, BZ),
        in_specs=in_vmem(3),
        out_specs=in_vmem(2),
        compiler_params=pltpu.CompilerParams(vmem_limit_bytes=4 * 2**20),
        name="strip_part",
    )(own, before, after)


def local_part(own, before, after, up, down, fan):
    middle = grids(8, MX, MY, BZ)
    middle[2] = jax.ShapeDtypeStruct((MX + 1, MY, BZ), F32)
    outs = (
        grids(1, fan * ROWS, BZ) + grids(1, 2, MY, BZ) + middle + grids(8, TX, TY, BZ)
    )
    big = scratch(10, EX, EY, BZ)
    big[3] = pltpu.VMEM((EX + 1, EY, BZ), F32)
    return pl.pallas_call(
        local_kernel,
        out_shape=outs,
        in_specs=in_vmem(5),
        out_specs=in_vmem(len(outs)),
        scratch_shapes=big + scratch(2, MX, MY, BZ) + scratch(1, 2, EY, BZ)
        + scratch(1, MX, MY, BZ) + scratch(1, MY, BZ),
        compiler_params=pltpu.CompilerParams(vmem_limit_bytes=24 * 2**20),
        name="local_part",
    )(own, before, after, up, down)


def finish_part(wide, deep, mine, other, even, odd, kept):
    count = 2 * wide
    tile = (2, deep, BZ)
    return pl.pallas_call(
        functools.partial(finish_kernel, wide, deep),
        out_shape=jax.ShapeDtypeStruct((BX, BY, BZ), F32),
        in_specs=in_vmem(4 + len(kept)),
        out_specs=pl.BlockSpec(memory_space=pltpu.VMEM),
        scratch_shapes=scratch(3, count + 1, *tile)
        + scratch(3, count, *tile) + scratch(1, count + 4, *tile) + scratch(2, count + 1, *tile)
        + scratch(2, 6, *tile) + scratch(1, 24, BZ) + scratch(1, 24, 4 * BZ)
        + scratch(3, MX, MY, BZ) + scratch(1, 2, EY, BZ) + scratch(3, TX, TY, BZ),
        compiler_params=pltpu.CompilerParams(vmem_limit_bytes=24 * 2**20),
        name="finish_part",
    )(mine, other, even, odd, *kept)


def upward(size):
    return [(i, i + 1) for i in range(size - 1)]


def downward(size):
    return [(i + 1, i) for i in range(size - 1)]


def swapped(size, start):
    pairs = [(i, i + 1) for i in range(start, size - 1, 2)]
    return pairs + [(j, i) for i, j in pairs]


def pack_kernel(
    source_ref, coef_ref, tops_ref, own_ref, right_ref, left_ref, tops, sems
):
    moves = (
        (tops_ref, tops),
        (source_ref, own_ref.at[pl.ds(0, BX)]),
        (coef_ref, own_ref.at[pl.ds(BX, BX)]),
        (source_ref.at[pl.ds(BX - NS, NS)], right_ref.at[pl.ds(0, NS)]),
        (coef_ref.at[pl.ds(BX - NC, NC)], right_ref.at[pl.ds(NS, NC)]),
        (source_ref.at[pl.ds(0, NS)], left_ref.at[pl.ds(0, NS)]),
        (coef_ref.at[pl.ds(0, NC)], left_ref.at[pl.ds(NS, NC)]),
    )
    copies = [pltpu.make_async_copy(*move, sems.at[i]) for i, move in enumerate(moves)]
    for copy in copies:
        copy.start()
    copies[0].wait()
    values = tops[...].astype(F32)
    same = lax.broadcasted_iota(jnp.int32, (BY, BY), 0) == lane_index((BY, BY))
    lanes = lane_index((BY, BZ))
    turned = jnp.zeros((BY, BZ), F32)
    for x in range(BX):
        column = jnp.sum(jnp.where(same, values[x:x + 1], 0.0), axis=1, keepdims=True)
        turned = jnp.where(lanes == x, column, turned)
    own_ref[PACK - 1] = turned
    right_ref[SIDE - 1] = turned
    left_ref[SIDE - 1] = turned
    for copy in copies[1:]:
        copy.wait()


def pack_part(source, conductivity, ice_cells):
    return pl.pallas_call(
        pack_kernel,
        out_shape=grids(1, PACK, BY, BZ) + grids(2, SIDE, BY, BZ),
        in_specs=[pl.BlockSpec(memory_space=pltpu.HBM)] * 3,
        out_specs=in_vmem(3),
        scratch_shapes=[pltpu.VMEM((BX, BY), jnp.int32), pltpu.SemaphoreType.DMA((7,))],
        compiler_params=pltpu.CompilerParams(vmem_limit_bytes=4 * 2**20),
        name="pack_part",
    )(source, conductivity, ice_cells)


def shards(wide, deep, source, conductivity, ice_cells):
    own, right, left = pack_part(source, conductivity, ice_cells)
    before = lax.ppermute(right, "wide", upward(wide))
    after = lax.ppermute(left, "wide", downward(wide))
    up, down = strip_part(own, before, after)
    up = lax.ppermute(up, ("z", "core"), upward(2 * deep))
    down = lax.ppermute(down, ("z", "core"), downward(2 * deep))
    fan, edge, *kept = local_part(own, before, after, up, down, wide * deep)
    even = lax.ppermute(edge, "wide", swapped(wide, 0))
    odd = lax.ppermute(edge, "wide", swapped(wide, 1))
    fan = fan.reshape(wide * deep, 1, ROWS * BZ)
    mine = lax.all_to_all(fan, ("wide", "z"), 0, 0, tiled=True)
    mine = mine.reshape(wide * deep * ROWS, BZ)
    other = lax.ppermute(mine, "core", [(0, 1), (1, 0)])
    return finish_part(wide, deep, mine, other, even, odd, kept)


def solution(mesh):
    wide, deep = mesh.shape["wide"], mesh.shape["grp"] // 2
    split = Mesh(mesh.devices.reshape(wide, deep, 2), ("wide", "z", "core"))
    group = ("z", "core")
    return jax.shard_map(
        functools.partial(shards, wide, deep),
        mesh=split,
        in_specs=(P("wide", group, None), P("wide", group, None), P("wide", group)),
        out_specs=P("wide", group, None),
        check_vma=False,
    )
```

```python
import functools

import jax
import jax.numpy as jnp
from jax import lax
from jax.experimental import pallas as pl
from jax.experimental.pallas import tpu as pltpu
from jax.sharding import Mesh
from jax.sharding import PartitionSpec as P

ITERS = 6

cheb_center = (2.0 + 0.3) / 2.0
cheb_radius = (2.0 - 0.3) / 2.0
first_ratio = cheb_radius / cheb_center
second_ratio = 1.0 / (2.0 * cheb_center / cheb_radius - first_ratio)
carry_weight = second_ratio * first_ratio
fresh_weight = 2.0 * second_ratio / cheb_radius
inverse_center = 1.0 / cheb_center

F32 = jnp.float32
BX, BY, BZ = 8, 16, 128
PACK = 2 * BX + 1
NS, NC = 6, 7
SIDE = NS + NC + 1
STRIP = 2 * SIDE + PACK
HALF = 4
EX, EY = 3 * BX, 3 * BY
MX, MY = EX // 2, EY // 2
TX, TY = 12, 32
X0, Y0 = 6, 8
BLOCK = 16
ROWS = 5


def lane_index(shape):
    return lax.broadcasted_iota(jnp.int32, shape, len(shape) - 1)


def pair_weight(factor, coef, neighbour):
    total = coef + neighbour
    return (2.0 * factor) * coef * neighbour / jnp.where(total > 0.0, total, 1.0)


def shift(value, amount, axis):
    return pltpu.roll(value, amount % value.shape[axis], axis)


def operate(before, value, after, weight_x, weight_x_before, weight_y, weight_z, diagonal, active, step_z):
    coupled = weight_x * after + weight_x_before * before
    coupled = coupled + weight_y * shift(value, -1, 0)
    coupled = coupled + shift(weight_y * value, 1, 0)
    coupled = coupled + weight_z * shift(value, -step_z, 1)
    coupled = coupled + shift(weight_z * value, step_z, 1)
    return active * (diagonal * value - coupled)


def pair_lanes(value, step, combine):
    lanes = lane_index(value.shape)
    other = jnp.where((lanes & step) == 0, shift(value, -step, 1), shift(value, step, 1))
    return combine(value, other)


def loop(low, high, step, body):
    assert (high - low) % step == 0

    def turn(i, carry):
        for k in range(step):
            body(low + i * step + k, k)
        return carry

    lax.fori_loop(0, (high - low) // step, turn, 0)


def face_weights(factor, coef_ref, wx_ref, wy_ref, wz_ref, low, high, step, step_z):
    def body(x, slot):
        coef = coef_ref[x]
        lanes = lane_index(coef.shape)
        wx_ref[x + 1] = pair_weight(factor, coef, coef_ref[x + 1])
        wy_ref[x] = pair_weight(factor, coef, shift(coef, -1, 0))
        weight = pair_weight(factor, coef, shift(coef, -step_z, 1))
        wz_ref[x] = jnp.where(lanes >= BZ - step_z, 0.0, weight)

    wx_ref[low] = pair_weight(factor, coef_ref[low - 1], coef_ref[low])
    loop(low, high, step, body)


def diagonal_of(factor, x, coef_ref, wx_ref, wy_ref, wz_ref, step_z):
    coef = coef_ref[x]
    lanes = lane_index(coef.shape)
    weight_y, weight_z = wy_ref[x], wz_ref[x]
    top = jnp.where(lanes >= BZ - step_z, factor * coef, weight_z)
    total = wx_ref[x + 1] + wx_ref[x] + weight_y + shift(weight_y, 1, 0)
    return total + top + shift(weight_z, step_z, 1)


def inverse_of(diagonal):
    return 1.0 / jnp.where(diagonal > 0.0, diagonal, 1.0)


def strip_kernel(own_ref, before_ref, after_ref, up_ref, down_ref):
    for i in range(STRIP):
        if i < SIDE:
            row = before_ref[i]
        elif i < SIDE + PACK:
            row = own_ref[i - SIDE]
        else:
            row = after_ref[i - SIDE - PACK]
        k, part = STRIP + i // 2, slice(HALF * (i % 2), HALF * (i % 2 + 1))
        up_ref[i] = row[BY - 8:]
        up_ref[k, part] = row[BY - 8 - HALF:BY - 8]
        down_ref[i] = row[:8]
        down_ref[k, part] = row[8:8 + HALF]


def local_kernel(
    own_ref, before_ref, after_ref, up_ref, down_ref,
    fan_ref, edge_ref,
    load1_ref, active1_ref, wx1_ref, wy1_ref, wz1_ref, diag1_ref, inv1_ref, smooth1_ref,
    load0_ref, active0_ref, wx0_ref, wy0_ref, wz0_ref, diag0_ref, inv0_ref, smooth0_ref,
    source, coef, active, wx, wy, wz, diag, inv, update, smooth, coef1, update1, pairs, tops, coarse,
):
    edge_rows = jnp.zeros((8 - HALF, BZ), F32)

    def extended(i):
        if i < SIDE:
            own = before_ref[i]
        elif i < SIDE + PACK:
            own = own_ref[i - SIDE]
        else:
            own = after_ref[i - SIDE - PACK]
        k, part = STRIP + i // 2, slice(HALF * (i % 2), HALF * (i % 2 + 1))
        return jnp.concatenate(
            [edge_rows, up_ref[k, part], up_ref[i], own, down_ref[i], down_ref[k, part], edge_rows], 0
        )

    middle = SIDE
    last = SIDE + PACK
    for i in range(NS):
        source[BX - NS + i] = extended(i)
        source[2 * BX + i] = extended(last + i)
    for i in range(NC):
        coef[BX - NC + i] = extended(NS + i)
        coef[2 * BX + i] = extended(last + NS + i)
    for i in range(BX):
        source[BX + i] = extended(middle + i)
        coef[BX + i] = extended(middle + BX + i)
    for j, i in enumerate((SIDE - 1, last - 1, STRIP - 1)):
        columns = extended(i)
        for x in range(BX):
            active[j * BX + x] = jnp.broadcast_to(columns[:, x:x + 1], (EY, BZ))

    low0, high0 = BX - NS, 2 * BX + NS
    low1, high1 = low0 // 2 + 1, high0 // 2 - 1

    def middle_tops(x, slot):
        pairs[slot] = jnp.maximum(active[2 * x], active[2 * x + 1])
        value = jnp.maximum(
            pairs[slot, pl.ds(0, MY, stride=2), :], pairs[slot, pl.ds(1, MY, stride=2), :]
        )
        tops[x] = value
        layer = (lane_index((MY, BZ)) & ~1).astype(F32)
        active1_ref[x] = (layer < value).astype(F32)

    loop(0, MX, 2, middle_tops)

    def fine_mask(x, slot):
        layer = lane_index((EY, BZ)).astype(F32)
        mask = (layer < active[x]).astype(F32)
        active[x] = mask
        source[x] = mask * source[x]

    loop(low0, high0, 2, fine_mask)

    face_weights(1.0, coef, wx, wy, wz, low0, high0, 2, 1)

    def fine_start(x, slot):
        diagonal = diagonal_of(1.0, x, coef, wx, wy, wz, 1)
        inverse = inverse_of(diagonal)
        diag[x] = diagonal
        inv[x] = inverse
        update[x] = source[x] * (inverse * inverse_center)

    loop(low0, high0, 2, fine_start)

    def fine_operate(ref, x):
        return operate(ref[x - 1], ref[x], ref[x + 1], wx[x + 1], wx[x], wy[x], wz[x], diag[x], active[x], 1)

    def fine_finish(x, slot):
        residual = source[x] - fine_operate(update, x)
        first = update[x]
        smooth[x] = first + (carry_weight * first + fresh_weight * residual * inv[x])

    loop(low0 + 1, high0 - 1, 2, fine_finish)

    def keep(i, slot):
        for kept, ref in (
            (load0_ref, source), (active0_ref, active), (wy0_ref, wy), (wz0_ref, wz),
            (diag0_ref, diag), (inv0_ref, inv), (smooth0_ref, smooth),
        ):
            kept[i] = ref[X0 + i, Y0:Y0 + TY, :]
        wx0_ref[i] = wx[X0 + i, Y0:Y0 + TY, :]

    loop(0, TX, 2, keep)

    def restrict(value, slot):
        pairs[slot] = pair_lanes(value, 1, jnp.add)
        return pairs[slot, pl.ds(0, MY, stride=2), :] + pairs[slot, pl.ds(1, MY, stride=2), :]

    def middle_coef(x, slot):
        coef1[x] = restrict(coef[2 * x] + coef[2 * x + 1], slot) * 0.125

    loop(low1 - 1, high1 + 1, 2, middle_coef)

    def middle_load(x, slot):
        left = source[2 * x] - fine_operate(smooth, 2 * x)
        right = source[2 * x + 1] - fine_operate(smooth, 2 * x + 1)
        load1_ref[x] = restrict(left + right, slot)

    loop(low1, high1, 2, middle_load)

    face_weights(2.0, coef1, wx1_ref, wy1_ref, wz1_ref, low1, high1, 4, 2)

    def middle_start(x, slot):
        diagonal = diagonal_of(2.0, x, coef1, wx1_ref, wy1_ref, wz1_ref, 2)
        inverse = inverse_of(diagonal)
        diag1_ref[x] = diagonal
        inv1_ref[x] = inverse
        update1[x] = load1_ref[x] * (inverse * inverse_center)

    loop(low1, high1, 4, middle_start)

    def middle_operate(ref, x):
        return operate(
            ref[x - 1], ref[x], ref[x + 1], wx1_ref[x + 1], wx1_ref[x], wy1_ref[x], wz1_ref[x],
            diag1_ref[x], active1_ref[x], 2,
        )

    def middle_finish(x, slot):
        residual = load1_ref[x] - middle_operate(update1, x)
        first = update1[x]
        smooth1_ref[x] = first + (carry_weight * first + fresh_weight * residual * inv1_ref[x])

    loop(low1 + 1, high1 - 1, 3, middle_finish)
    for i in range(2):
        edge_ref[i] = smooth1_ref[MX // 2 - 1 + i]

    first_x, first_y = MX // 3, MY // 3
    rows = []
    for part in range(2):
        for cx in range(2):
            if part == 0:
                total = sum(
                    load1_ref[x] - middle_operate(smooth1_ref, x)
                    for x in (first_x + 2 * cx, first_x + 2 * cx + 1)
                )
            else:
                total = (coef1[first_x + 2 * cx] + coef1[first_x + 2 * cx + 1]) * 0.125
            coarse[...] = pair_lanes(total, 2, jnp.add)
            value = (
                coarse[pl.ds(first_y, 4, stride=2), :] + coarse[pl.ds(first_y + 1, 4, stride=2), :]
            )
            rows.append(jnp.concatenate([value[i:i + 1] for i in range(4)], 1))
    spread = jnp.concatenate(rows + [jnp.zeros((4, 4 * BZ), F32)], 0)
    entry = lax.broadcasted_iota(jnp.int32, (4 * BZ, BZ), 0)
    lanes = lane_index((4 * BZ, BZ))
    chosen = (entry // BZ == lanes // 32) & (entry % BZ == (lanes % 32) * 4)
    packed = jnp.dot(
        spread, chosen.astype(F32), precision=lax.Precision.HIGHEST, preferred_element_type=F32
    )
    lanes = lane_index((1, BZ))
    top_row = jnp.zeros((1, BZ), F32)
    for cx in range(2):
        coarse[...] = jnp.maximum(tops[first_x + 2 * cx], tops[first_x + 2 * cx + 1])
        value = jnp.maximum(
            coarse[pl.ds(first_y, 4, stride=2), :], coarse[pl.ds(first_y + 1, 4, stride=2), :]
        )
        for cy in range(4):
            top_row = jnp.where(lanes // 16 == 2 * cy + cx, value[cy:cy + 1], top_row)
    block = [packed[i:i + 1] for i in range(4)] + [top_row]
    pattern = jnp.concatenate(block * 8, 0)

    def fan(i, carry):
        fan_ref[pl.ds(pl.multiple_of(i * 8 * ROWS, 8), 8 * ROWS), :] = pattern
        return carry

    lax.fori_loop(0, fan_ref.shape[0] // (8 * ROWS), fan, 0)


def coarse_kernel(
    wide, deep, mine_ref, other_ref, wanted,
    coef, active, wx, wy, wz, diag, residual, image, slope, direction, solution,
):
    count = 2 * wide
    vector = (deep, BZ)
    lanes = lane_index((BLOCK, deep, BZ))
    zero = jnp.zeros(vector, F32)
    pad = 2

    def pair(first, second):
        return jnp.stack([first, second], 1)

    def y_after(value):
        turned = shift(value, -32, 3)
        first, second = turned[:, 0], turned[:, 1]
        inside = lanes < 96
        return pair(jnp.where(inside, first, second), jnp.where(inside, second, shift(first, -1, 1)))

    def y_before(value):
        turned = shift(value, 32, 3)
        first, second = turned[:, 0], turned[:, 1]
        inside = lanes >= 32
        return pair(jnp.where(inside, first, shift(second, 1, 1)), jnp.where(inside, second, first))

    for ref, spare in ((residual, (*range(pad), *range(count + pad, count + 2 * pad))), (image, (count,)), (slope, (count,))):
        for x in spare:
            ref[x] = jnp.zeros((2, *vector), F32)

    stride = deep * ROWS
    flat = lane_index(vector)
    low = (flat & 16) == 0
    layer = ((flat & 31) * 4).astype(F32)

    def unpack(refs):
        def body(w, slot):
            for c in range(2):
                top, *rows = (
                    refs[c][pl.ds(w * stride + k, deep, stride=ROWS), :] for k in (4, 0, 1, 2, 3)
                )
                tall = (
                    jnp.where(low, top, shift(top, 16, 1)), jnp.where(low, shift(top, -16, 1), top)
                )
                for i in range(2):
                    residual[2 * w + i + pad, c] = rows[i]
                    coef[2 * w + i, c] = rows[2 + i]
                    active[2 * w + i, c] = (layer < tall[i]).astype(F32)

        loop(0, wide, 2, body)

    own_core = lax.axis_index("core")

    @pl.when(own_core == 0)
    def _():
        unpack((mine_ref, other_ref))

    @pl.when(own_core == 1)
    def _():
        unpack((other_ref, mine_ref))

    lanes4 = lane_index((BLOCK, 2, deep, BZ))
    highest = (lanes4 & 31) == 31
    shape4 = (BLOCK, 2, deep, BZ)
    last_y = (
        (lanes4 >= 96)
        & (lax.broadcasted_iota(jnp.int32, shape4, 1) == 1)
        & (lax.broadcasted_iota(jnp.int32, shape4, 2) == deep - 1)
    )

    def coarse_weight(a, b):
        return 8.0 * a * b / (a + b)

    coef[count] = jnp.zeros((2, *vector), F32)
    active[count] = jnp.zeros((2, *vector), F32)
    wx[0] = jnp.zeros((2, *vector), F32)

    def setup(i, face):
        x = i * BLOCK
        coefs, masks = coef[pl.ds(x, BLOCK + 1)], active[pl.ds(x, BLOCK + 1)]
        here, mask = coefs[:BLOCK], masks[:BLOCK]
        after = coarse_weight(here, coefs[1:])
        before = jnp.concatenate([face, after[:-1]], 0)
        beside = jnp.where(last_y, 0.0, coarse_weight(here, y_after(here)))
        above = coarse_weight(here, shift(here, -1, 3))
        inner = jnp.where(highest, 0.0, above)
        top = jnp.where(highest, 4.0 * here, above)
        total = after + before + beside + y_before(beside) + top + shift(inner, 1, 3)
        diag[pl.ds(x, BLOCK)] = mask * total
        wx[pl.ds(x + 1, BLOCK)] = after * (mask * masks[1:])
        wy[pl.ds(x, BLOCK)] = beside * (mask * y_after(mask))
        wz[pl.ds(x, BLOCK)] = inner * (mask * shift(mask, -1, 3))
        return after[-1:]

    lax.fori_loop(0, count // BLOCK, setup, jnp.zeros((1, 2, *vector), F32))

    def whole(total):
        return jnp.sum(jnp.sum(total, axis=0, keepdims=True), axis=1, keepdims=True)

    def fold(total, value):
        return total + jnp.sum(value, axis=(0, 1))

    first = 2 * lax.axis_index("wide")
    ratio = scale = norm = jnp.zeros((1, 1), F32)
    for iteration in range(ITERS):
        start = iteration == 0
        if not start:
            wide_ratio = jnp.broadcast_to(ratio, vector)[None, None]
            wide_scale = jnp.broadcast_to(scale, vector)[None, None]

        def renew(x, size):
            value = residual[pl.ds(x + pad, size)]
            if start:
                return value
            slope_here = image[pl.ds(x, size)]
            if iteration > 1:
                slope_here = slope_here + wide_ratio * slope[pl.ds(x, size)]
            if iteration < ITERS - 1:
                slope[pl.ds(x, size)] = slope_here
            value = value - wide_scale * slope_here
            residual[pl.ds(x + pad, size)] = value
            return value

        def apply(i, carry):
            x = i * BLOCK
            norm_sum, image_sum, last = carry
            grown = jnp.concatenate([last, renew(x + 1, BLOCK)], 0)
            before, here, after = grown[:BLOCK], grown[1:BLOCK + 1], grown[2:]
            weight_y, weight_z = wy[pl.ds(x, BLOCK)], wz[pl.ds(x, BLOCK)]
            faces = wx[pl.ds(x, BLOCK + 1)]
            coupled = faces[1:] * after + faces[:-1] * before
            coupled = coupled + weight_y * y_after(here) + y_before(weight_y * here)
            coupled = coupled + weight_z * shift(here, -1, 3) + shift(weight_z * here, 1, 3)
            value = diag[pl.ds(x, BLOCK)] * here - coupled
            image[pl.ds(x, BLOCK)] = value
            return fold(norm_sum, here * here), fold(image_sum, here * value), grown[BLOCK:]

        opening = jnp.concatenate([jnp.zeros((1, 2, *vector), F32), renew(0, 1)], 0)
        norm_sum, image_sum, _ = lax.fori_loop(0, count // BLOCK, apply, (zero, zero, opening))
        fresh, curvature = whole(norm_sum), whole(image_sum)
        here = residual[pl.ds(first, 6)]
        if start:
            scale = fresh / curvature
            direction[...] = here
            solution[...] = jnp.broadcast_to(scale, vector)[None, None] * here
        else:
            ratio = fresh / norm
            scale = fresh / (curvature - ratio * fresh / scale)
            here = here + jnp.broadcast_to(ratio, vector)[None, None] * direction[...]
            direction[...] = here
            solution[...] = solution[...] + jnp.broadcast_to(scale, vector)[None, None] * here
        norm = fresh

    position = 2 * lax.axis_index("z") + own_core
    wanted[...] = jnp.zeros(wanted.shape, F32)
    for j in range(3):
        group = jnp.clip(position + j - 1, 0, 2 * deep - 1)
        core, row = group & 1, group >> 1
        for i in range(6):
            wanted[3 * i + j:3 * i + j + 1, :] = solution[i, core, pl.ds(row, 1), :]


def finish_kernel(
    wanted, even_ref, odd_ref,
    load1_ref, active1_ref, wx1_ref, wy1_ref, wz1_ref, diag1_ref, inv1_ref, smooth1_ref,
    load0_ref, active0_ref, wx0_ref, wy0_ref, wz0_ref, diag0_ref, inv0_ref, smooth0_ref,
    out_ref,
    spread, guess1, update1, second1, children, guess0, update0, second0,
):
    entry = lax.broadcasted_iota(jnp.int32, (BZ, 4 * BZ), 0)
    columns = lane_index((BZ, 4 * BZ))
    chosen = entry == (columns // BZ) * 32 + (columns % BZ) // 4
    spread[...] = jnp.dot(
        wanted[...], chosen.astype(F32), precision=lax.Precision.HIGHEST, preferred_element_type=F32
    )
    even = lax.axis_index("wide") % 2 == 0
    for i in range(6):
        rows = []
        for y in range(12):
            r, c = 3 * i + y // 4, y % 4
            row = spread[r:r + 1, c * BZ:(c + 1) * BZ]
            rows.append(jnp.broadcast_to(row, (2, BZ)))
        parent = jnp.concatenate(rows, 0)
        for x in (2 * i, 2 * i + 1):
            if x in (0, MX - 1):
                continue
            if x <= 2:
                value = jnp.where(even, odd_ref[x - 1], even_ref[x - 1])
            elif x >= MX - 3:
                value = jnp.where(even, even_ref[x - (MX - 3)], odd_ref[x - (MX - 3)])
            else:
                value = smooth1_ref[x]
            guess1[x] = value + active1_ref[x] * parent

    def middle_operate(ref, x):
        return operate(
            ref[x - 1], ref[x], ref[x + 1], wx1_ref[x + 1], wx1_ref[x], wy1_ref[x], wz1_ref[x],
            diag1_ref[x], active1_ref[x], 2,
        )

    def middle_first(x, slot):
        residual_here = load1_ref[x] - middle_operate(guess1, x)
        value = residual_here * (inv1_ref[x] * inverse_center)
        update1[x] = value
        second1[x] = guess1[x] + value

    loop(2, MX - 2, 4, middle_first)

    def middle_second(x, slot):
        residual_here = load1_ref[x] - middle_operate(second1, x)
        value = second1[x] + (
            carry_weight * update1[x] + fresh_weight * residual_here * inv1_ref[x]
        )
        guess1[x] = value

    loop(3, MX - 3, 3, middle_second)

    def fine_guess(x, slot):
        value = guess1[x]
        children[slot, pl.ds(0, MY, stride=2), :] = value
        children[slot, pl.ds(1, MY, stride=2), :] = value
        child = children[slot, Y0:Y0 + TY, :]
        for i in range(2):
            k = 2 * x + i - X0
            guess0[k] = smooth0_ref[k] + active0_ref[k] * child

    loop(X0 // 2, (X0 + TX) // 2, 2, fine_guess)

    def fine_operate(ref, x):
        return operate(
            ref[x - 1], ref[x], ref[x + 1], wx0_ref[x + 1], wx0_ref[x], wy0_ref[x], wz0_ref[x],
            diag0_ref[x], active0_ref[x], 1,
        )

    def fine_first(x, slot):
        residual_here = load0_ref[x] - fine_operate(guess0, x)
        value = residual_here * (inv0_ref[x] * inverse_center)
        update0[x] = value
        second0[x] = guess0[x] + value

    loop(1, TX - 1, 2, fine_first)
    margin = BX - X0

    def fine_second(x, slot):
        residual_here = load0_ref[x] - fine_operate(second0, x)
        value = second0[x] + (
            carry_weight * update0[x] + fresh_weight * residual_here * inv0_ref[x]
        )
        out_ref[x - margin] = value[BY - Y0:2 * BY - Y0]

    loop(margin, margin + BX, 2, fine_second)


def in_vmem(count):
    return [pl.BlockSpec(memory_space=pltpu.VMEM)] * count


def grids(count, *shape):
    return [jax.ShapeDtypeStruct(shape, F32)] * count


def scratch(count, *shape):
    return [pltpu.VMEM(shape, F32)] * count


def strip_part(own, before, after):
    return pl.pallas_call(
        strip_kernel,
        out_shape=grids(2, STRIP + (STRIP + 1) // 2, 8, BZ),
        in_specs=in_vmem(3),
        out_specs=in_vmem(2),
        compiler_params=pltpu.CompilerParams(vmem_limit_bytes=4 * 2**20),
        name="strip_part",
    )(own, before, after)


def local_part(own, before, after, up, down, fan):
    middle = grids(8, MX, MY, BZ)
    middle[2] = jax.ShapeDtypeStruct((MX + 1, MY, BZ), F32)
    outs = (
        grids(1, fan * ROWS, BZ) + grids(1, 2, MY, BZ) + middle + grids(8, TX, TY, BZ)
    )
    big = scratch(10, EX, EY, BZ)
    big[3] = pltpu.VMEM((EX + 1, EY, BZ), F32)
    return pl.pallas_call(
        local_kernel,
        out_shape=outs,
        in_specs=in_vmem(5),
        out_specs=in_vmem(len(outs)),
        scratch_shapes=big + scratch(2, MX, MY, BZ) + scratch(1, 2, EY, BZ)
        + scratch(1, MX, MY, BZ) + scratch(1, MY, BZ),
        compiler_params=pltpu.CompilerParams(vmem_limit_bytes=24 * 2**20),
        name="local_part",
    )(own, before, after, up, down)


def coarse_part(wide, deep, mine, other):
    count = 2 * wide
    tile = (2, deep, BZ)
    work = count * 2 * deep * BZ
    return pl.pallas_call(
        functools.partial(coarse_kernel, wide, deep),
        out_shape=jax.ShapeDtypeStruct((24, BZ), F32),
        in_specs=in_vmem(2),
        out_specs=pl.BlockSpec(memory_space=pltpu.VMEM),
        scratch_shapes=scratch(3, count + 1, *tile)
        + scratch(3, count, *tile) + scratch(1, count + 4, *tile) + scratch(2, count + 1, *tile)
        + scratch(2, 6, *tile),
        compiler_params=pltpu.CompilerParams(vmem_limit_bytes=16 * 2**20),
        cost_estimate=pl.CostEstimate(flops=250 * work, bytes_accessed=8 * work * 4, transcendentals=0),
        name="coarse_part",
    )(mine, other)


def finish_part(wanted, even, odd, kept):
    return pl.pallas_call(
        finish_kernel,
        out_shape=jax.ShapeDtypeStruct((BX, BY, BZ), F32),
        in_specs=in_vmem(3 + len(kept)),
        out_specs=pl.BlockSpec(memory_space=pltpu.VMEM),
        scratch_shapes=scratch(1, 24, 4 * BZ)
        + scratch(3, MX, MY, BZ) + scratch(1, 2, EY, BZ) + scratch(3, TX, TY, BZ),
        compiler_params=pltpu.CompilerParams(vmem_limit_bytes=8 * 2**20),
        name="finish_part",
    )(wanted, even, odd, *kept)


def upward(size):
    return [(i, i + 1) for i in range(size - 1)]


def downward(size):
    return [(i + 1, i) for i in range(size - 1)]


def swapped(size, start):
    pairs = [(i, i + 1) for i in range(start, size - 1, 2)]
    return pairs + [(j, i) for i, j in pairs]


def pack_kernel(
    source_ref, coef_ref, tops_ref, own_ref, right_ref, left_ref, tops, sems
):
    moves = (
        (tops_ref, tops),
        (source_ref, own_ref.at[pl.ds(0, BX)]),
        (coef_ref, own_ref.at[pl.ds(BX, BX)]),
        (source_ref.at[pl.ds(BX - NS, NS)], right_ref.at[pl.ds(0, NS)]),
        (coef_ref.at[pl.ds(BX - NC, NC)], right_ref.at[pl.ds(NS, NC)]),
        (source_ref.at[pl.ds(0, NS)], left_ref.at[pl.ds(0, NS)]),
        (coef_ref.at[pl.ds(0, NC)], left_ref.at[pl.ds(NS, NC)]),
    )
    copies = [pltpu.make_async_copy(*move, sems.at[i]) for i, move in enumerate(moves)]
    for copy in copies:
        copy.start()
    copies[0].wait()
    values = tops[...].astype(F32)
    same = lax.broadcasted_iota(jnp.int32, (BY, BY), 0) == lane_index((BY, BY))
    lanes = lane_index((BY, BZ))
    turned = jnp.zeros((BY, BZ), F32)
    for x in range(BX):
        column = jnp.sum(jnp.where(same, values[x:x + 1], 0.0), axis=1, keepdims=True)
        turned = jnp.where(lanes == x, column, turned)
    own_ref[PACK - 1] = turned
    right_ref[SIDE - 1] = turned
    left_ref[SIDE - 1] = turned
    for copy in copies[1:]:
        copy.wait()


def pack_part(source, conductivity, ice_cells):
    return pl.pallas_call(
        pack_kernel,
        out_shape=grids(1, PACK, BY, BZ) + grids(2, SIDE, BY, BZ),
        in_specs=[pl.BlockSpec(memory_space=pltpu.HBM)] * 3,
        out_specs=in_vmem(3),
        scratch_shapes=[pltpu.VMEM((BX, BY), jnp.int32), pltpu.SemaphoreType.DMA((7,))],
        compiler_params=pltpu.CompilerParams(vmem_limit_bytes=4 * 2**20),
        name="pack_part",
    )(*(pltpu.with_memory_space_constraint(v, pltpu.HBM) for v in (source, conductivity, ice_cells)))


def shards(wide, deep, source, conductivity, ice_cells):
    own, right, left = pack_part(source, conductivity, ice_cells)
    before = lax.ppermute(right, "wide", upward(wide))
    after = lax.ppermute(left, "wide", downward(wide))
    up, down = strip_part(own, before, after)
    up = lax.ppermute(up, ("z", "core"), upward(2 * deep))
    down = lax.ppermute(down, ("z", "core"), downward(2 * deep))
    fan, edge, *kept = local_part(own, before, after, up, down, wide * deep)
    fan = fan.reshape(wide * deep, 1, ROWS * BZ)
    mine = lax.all_to_all(fan, ("wide", "z"), 0, 0, tiled=True)
    mine = mine.reshape(wide * deep * ROWS, BZ)
    other = lax.ppermute(mine, "core", [(0, 1), (1, 0)])
    even = lax.ppermute(edge, "wide", swapped(wide, 0))
    odd = lax.ppermute(edge, "wide", swapped(wide, 1))
    wanted = coarse_part(wide, deep, mine, other)
    return finish_part(wanted, even, odd, kept)


def solution(mesh):
    wide, deep = mesh.shape["wide"], mesh.shape["grp"] // 2
    split = Mesh(mesh.devices.reshape(wide, deep, 2), ("wide", "z", "core"))
    group = ("z", "core")
    return jax.shard_map(
        functools.partial(shards, wide, deep),
        mesh=split,
        in_specs=(P("wide", group, None), P("wide", group, None), P("wide", group)),
        out_specs=P("wide", group, None),
        check_vma=False,
    )
```

```python
import functools

import jax
import jax.numpy as jnp
from jax import lax
from jax.experimental import pallas as pl
from jax.experimental.pallas import tpu as pltpu
from jax.sharding import Mesh
from jax.sharding import PartitionSpec as P

ITERS = 6

cheb_center = (2.0 + 0.3) / 2.0
cheb_radius = (2.0 - 0.3) / 2.0
first_ratio = cheb_radius / cheb_center
second_ratio = 1.0 / (2.0 * cheb_center / cheb_radius - first_ratio)
carry_weight = second_ratio * first_ratio
fresh_weight = 2.0 * second_ratio / cheb_radius
inverse_center = 1.0 / cheb_center

F32 = jnp.float32
BX, BY, BZ = 8, 16, 128
PACK = 2 * BX + 1
NS, NC = 6, 7
SIDE = NS + NC + 1
STRIP = 2 * SIDE + PACK
HALF = 4
EX, EY = 3 * BX, 3 * BY
MX, MY = EX // 2, EY // 2
TX, TY = 12, 32
X0, Y0 = 6, 8
BLOCK = 16
ROWS = 5


def lane_index(shape):
    return lax.broadcasted_iota(jnp.int32, shape, len(shape) - 1)


def pair_weight(factor, coef, neighbour):
    total = coef + neighbour
    return (2.0 * factor) * coef * neighbour / jnp.where(total > 0.0, total, 1.0)


def shift(value, amount, axis):
    return pltpu.roll(value, amount % value.shape[axis], axis)


def operate(before, value, after, weight_x, weight_x_before, weight_y, weight_z, diagonal, active, step_z):
    coupled = weight_x * after + weight_x_before * before
    coupled = coupled + weight_y * shift(value, -1, 0)
    coupled = coupled + shift(weight_y * value, 1, 0)
    coupled = coupled + weight_z * shift(value, -step_z, 1)
    coupled = coupled + shift(weight_z * value, step_z, 1)
    return active * (diagonal * value - coupled)


def pair_lanes(value, step, combine):
    lanes = lane_index(value.shape)
    other = jnp.where((lanes & step) == 0, shift(value, -step, 1), shift(value, step, 1))
    return combine(value, other)


def loop(low, high, step, body):
    assert (high - low) % step == 0

    def turn(i, carry):
        for k in range(step):
            body(low + i * step + k, k)
        return carry

    lax.fori_loop(0, (high - low) // step, turn, 0)


def face_weights(factor, coef_ref, wx_ref, wy_ref, wz_ref, low, high, step, step_z):
    def body(x, slot):
        coef = coef_ref[x]
        lanes = lane_index(coef.shape)
        wx_ref[x + 1] = pair_weight(factor, coef, coef_ref[x + 1])
        wy_ref[x] = pair_weight(factor, coef, shift(coef, -1, 0))
        weight = pair_weight(factor, coef, shift(coef, -step_z, 1))
        wz_ref[x] = jnp.where(lanes >= BZ - step_z, 0.0, weight)

    wx_ref[low] = pair_weight(factor, coef_ref[low - 1], coef_ref[low])
    loop(low, high, step, body)


def diagonal_of(factor, x, coef_ref, wx_ref, wy_ref, wz_ref, step_z):
    coef = coef_ref[x]
    lanes = lane_index(coef.shape)
    weight_y, weight_z = wy_ref[x], wz_ref[x]
    top = jnp.where(lanes >= BZ - step_z, factor * coef, weight_z)
    total = wx_ref[x + 1] + wx_ref[x] + weight_y + shift(weight_y, 1, 0)
    return total + top + shift(weight_z, step_z, 1)


def inverse_of(diagonal):
    return 1.0 / jnp.where(diagonal > 0.0, diagonal, 1.0)


def pick(even, first, second):
    return jnp.where(even, first, second)


def strip_row(i, own_ref, left_ref, right_ref, even):
    if i < SIDE:
        return pick(even, left_ref[i], right_ref[i])
    if i < SIDE + PACK:
        return own_ref[i - SIDE]
    k = i - SIDE - PACK
    return pick(even, right_ref[k], left_ref[k])


def strip_kernel(own_ref, left_ref, right_ref, far_ref, near_ref):
    even = lax.axis_index("wide") % 2 == 0
    first_core = lax.axis_index("core") == 0
    for i in range(STRIP):
        row = strip_row(i, own_ref, left_ref, right_ref, even)
        k, part = STRIP + i // 2, slice(HALF * (i % 2), HALF * (i % 2 + 1))
        low, low_half = row[:8], row[8:8 + HALF]
        high, high_half = row[BY - 8:], row[BY - 8 - HALF:BY - 8]
        far_ref[i] = pick(first_core, low, high)
        far_ref[k, part] = pick(first_core, low_half, high_half)
        near_ref[i] = pick(first_core, high, low)
        near_ref[k, part] = pick(first_core, high_half, low_half)


def local_kernel(
    own_ref, left_ref, right_ref, far_ref, near_ref,
    fan_ref, edge_ref,
    load1_ref, active1_ref, wx1_ref, wy1_ref, wz1_ref, diag1_ref, inv1_ref, smooth1_ref,
    load0_ref, active0_ref, wx0_ref, wy0_ref, wz0_ref, diag0_ref, inv0_ref, smooth0_ref,
    source, coef, active, wx, wy, wz, diag, inv, update, smooth, coef1, update1, pairs, tops, coarse,
):
    edge_rows = jnp.zeros((8 - HALF, BZ), F32)

    even = lax.axis_index("wide") % 2 == 0
    first_core = lax.axis_index("core") == 0

    def extended(i):
        k, part = STRIP + i // 2, slice(HALF * (i % 2), HALF * (i % 2 + 1))
        far, near, far_half, near_half = far_ref[i], near_ref[i], far_ref[k, part], near_ref[k, part]
        return jnp.concatenate(
            [
                edge_rows,
                pick(first_core, far_half, near_half),
                pick(first_core, far, near),
                strip_row(i, own_ref, left_ref, right_ref, even),
                pick(first_core, near, far),
                pick(first_core, near_half, far_half),
                edge_rows,
            ],
            0,
        )

    middle = SIDE
    last = SIDE + PACK
    for i in range(NS):
        source[BX - NS + i] = extended(i)
        source[2 * BX + i] = extended(last + i)
    for i in range(NC):
        coef[BX - NC + i] = extended(NS + i)
        coef[2 * BX + i] = extended(last + NS + i)
    for i in range(BX):
        source[BX + i] = extended(middle + i)
        coef[BX + i] = extended(middle + BX + i)
    for j, i in enumerate((SIDE - 1, last - 1, STRIP - 1)):
        columns = extended(i)
        for x in range(BX):
            active[j * BX + x] = jnp.broadcast_to(columns[:, x:x + 1], (EY, BZ))

    low0, high0 = BX - NS, 2 * BX + NS
    low1, high1 = low0 // 2 + 1, high0 // 2 - 1

    def middle_tops(x, slot):
        pairs[slot] = jnp.maximum(active[2 * x], active[2 * x + 1])
        value = jnp.maximum(
            pairs[slot, pl.ds(0, MY, stride=2), :], pairs[slot, pl.ds(1, MY, stride=2), :]
        )
        tops[x] = value
        layer = (lane_index((MY, BZ)) & ~1).astype(F32)
        active1_ref[x] = (layer < value).astype(F32)

    loop(0, MX, 2, middle_tops)

    def fine_mask(x, slot):
        layer = lane_index((EY, BZ)).astype(F32)
        mask = (layer < active[x]).astype(F32)
        active[x] = mask
        source[x] = mask * source[x]

    loop(low0, high0, 2, fine_mask)

    face_weights(1.0, coef, wx, wy, wz, low0, high0, 2, 1)

    def fine_start(x, slot):
        diagonal = diagonal_of(1.0, x, coef, wx, wy, wz, 1)
        inverse = inverse_of(diagonal)
        diag[x] = diagonal
        inv[x] = inverse
        update[x] = source[x] * (inverse * inverse_center)

    loop(low0, high0, 2, fine_start)

    def fine_operate(ref, x):
        return operate(ref[x - 1], ref[x], ref[x + 1], wx[x + 1], wx[x], wy[x], wz[x], diag[x], active[x], 1)

    def fine_finish(x, slot):
        residual = source[x] - fine_operate(update, x)
        first = update[x]
        smooth[x] = first + (carry_weight * first + fresh_weight * residual * inv[x])

    loop(low0 + 1, high0 - 1, 2, fine_finish)

    def keep(i, slot):
        for kept, ref in (
            (load0_ref, source), (active0_ref, active), (wy0_ref, wy), (wz0_ref, wz),
            (diag0_ref, diag), (inv0_ref, inv), (smooth0_ref, smooth),
        ):
            kept[i] = ref[X0 + i, Y0:Y0 + TY, :]
        wx0_ref[i] = wx[X0 + i, Y0:Y0 + TY, :]

    loop(0, TX, 2, keep)

    def restrict(value, slot):
        pairs[slot] = pair_lanes(value, 1, jnp.add)
        return pairs[slot, pl.ds(0, MY, stride=2), :] + pairs[slot, pl.ds(1, MY, stride=2), :]

    def middle_coef(x, slot):
        coef1[x] = restrict(coef[2 * x] + coef[2 * x + 1], slot) * 0.125

    loop(low1 - 1, high1 + 1, 2, middle_coef)

    def middle_load(x, slot):
        left = source[2 * x] - fine_operate(smooth, 2 * x)
        right = source[2 * x + 1] - fine_operate(smooth, 2 * x + 1)
        load1_ref[x] = restrict(left + right, slot)

    loop(low1, high1, 2, middle_load)

    face_weights(2.0, coef1, wx1_ref, wy1_ref, wz1_ref, low1, high1, 4, 2)

    def middle_start(x, slot):
        diagonal = diagonal_of(2.0, x, coef1, wx1_ref, wy1_ref, wz1_ref, 2)
        inverse = inverse_of(diagonal)
        diag1_ref[x] = diagonal
        inv1_ref[x] = inverse
        update1[x] = load1_ref[x] * (inverse * inverse_center)

    loop(low1, high1, 4, middle_start)

    def middle_operate(ref, x):
        return operate(
            ref[x - 1], ref[x], ref[x + 1], wx1_ref[x + 1], wx1_ref[x], wy1_ref[x], wz1_ref[x],
            diag1_ref[x], active1_ref[x], 2,
        )

    def middle_finish(x, slot):
        residual = load1_ref[x] - middle_operate(update1, x)
        first = update1[x]
        smooth1_ref[x] = first + (carry_weight * first + fresh_weight * residual * inv1_ref[x])

    loop(low1 + 1, high1 - 1, 3, middle_finish)
    for i in range(2):
        edge_ref[i] = smooth1_ref[MX // 2 - 1 + i]

    first_x, first_y = MX // 3, MY // 3
    rows = []
    for part in range(2):
        for cx in range(2):
            if part == 0:
                total = sum(
                    load1_ref[x] - middle_operate(smooth1_ref, x)
                    for x in (first_x + 2 * cx, first_x + 2 * cx + 1)
                )
            else:
                total = (coef1[first_x + 2 * cx] + coef1[first_x + 2 * cx + 1]) * 0.125
            coarse[...] = pair_lanes(total, 2, jnp.add)
            value = (
                coarse[pl.ds(first_y, 4, stride=2), :] + coarse[pl.ds(first_y + 1, 4, stride=2), :]
            )
            rows.append(jnp.concatenate([value[i:i + 1] for i in range(4)], 1))
    spread = jnp.concatenate(rows + [jnp.zeros((4, 4 * BZ), F32)], 0)
    entry = lax.broadcasted_iota(jnp.int32, (4 * BZ, BZ), 0)
    lanes = lane_index((4 * BZ, BZ))
    chosen = (entry // BZ == lanes // 32) & (entry % BZ == (lanes % 32) * 4)
    packed = jnp.dot(
        spread, chosen.astype(F32), precision=lax.Precision.HIGHEST, preferred_element_type=F32
    )
    lanes = lane_index((1, BZ))
    top_row = jnp.zeros((1, BZ), F32)
    for cx in range(2):
        coarse[...] = jnp.maximum(tops[first_x + 2 * cx], tops[first_x + 2 * cx + 1])
        value = jnp.maximum(
            coarse[pl.ds(first_y, 4, stride=2), :], coarse[pl.ds(first_y + 1, 4, stride=2), :]
        )
        for cy in range(4):
            top_row = jnp.where(lanes // 16 == 2 * cy + cx, value[cy:cy + 1], top_row)
    block = [packed[i:i + 1] for i in range(4)] + [top_row]
    pattern = jnp.concatenate(block * 8, 0)

    def fan(i, carry):
        fan_ref[pl.ds(pl.multiple_of(i * 8 * ROWS, 8), 8 * ROWS), :] = pattern
        return carry

    lax.fori_loop(0, fan_ref.shape[0] // (8 * ROWS), fan, 0)


def coarse_kernel(
    wide, deep, mine_ref, other_ref, wanted,
    coef, active, wx, wy, wz, diag, residual, image, slope, direction, solution,
):
    count = 2 * wide
    vector = (deep, BZ)
    lanes = lane_index((BLOCK, deep, BZ))
    zero = jnp.zeros(vector, F32)
    pad = 2

    def pair(first, second):
        return jnp.stack([first, second], 1)

    def y_after(value):
        turned = shift(value, -32, 3)
        first, second = turned[:, 0], turned[:, 1]
        inside = lanes < 96
        return pair(jnp.where(inside, first, second), jnp.where(inside, second, shift(first, -1, 1)))

    def y_before(value):
        turned = shift(value, 32, 3)
        first, second = turned[:, 0], turned[:, 1]
        inside = lanes >= 32
        return pair(jnp.where(inside, first, shift(second, 1, 1)), jnp.where(inside, second, first))

    for ref, spare in ((residual, (*range(pad), *range(count + pad, count + 2 * pad))), (image, (count,)), (slope, (count,))):
        for x in spare:
            ref[x] = jnp.zeros((2, *vector), F32)

    stride = deep * ROWS
    flat = lane_index(vector)
    low = (flat & 16) == 0
    layer = ((flat & 31) * 4).astype(F32)

    def unpack(refs):
        def body(w, slot):
            for c in range(2):
                top, *rows = (
                    refs[c][pl.ds(w * stride + k, deep, stride=ROWS), :] for k in (4, 0, 1, 2, 3)
                )
                tall = (
                    jnp.where(low, top, shift(top, 16, 1)), jnp.where(low, shift(top, -16, 1), top)
                )
                for i in range(2):
                    residual[2 * w + i + pad, c] = rows[i]
                    coef[2 * w + i, c] = rows[2 + i]
                    active[2 * w + i, c] = (layer < tall[i]).astype(F32)

        loop(0, wide, 2, body)

    own_core = lax.axis_index("core")

    @pl.when(own_core == 0)
    def _():
        unpack((mine_ref, other_ref))

    @pl.when(own_core == 1)
    def _():
        unpack((other_ref, mine_ref))

    lanes4 = lane_index((BLOCK, 2, deep, BZ))
    highest = (lanes4 & 31) == 31
    shape4 = (BLOCK, 2, deep, BZ)
    last_y = (
        (lanes4 >= 96)
        & (lax.broadcasted_iota(jnp.int32, shape4, 1) == 1)
        & (lax.broadcasted_iota(jnp.int32, shape4, 2) == deep - 1)
    )

    def coarse_weight(a, b):
        return 8.0 * a * b / (a + b)

    coef[count] = jnp.zeros((2, *vector), F32)
    active[count] = jnp.zeros((2, *vector), F32)
    wx[0] = jnp.zeros((2, *vector), F32)

    def setup(i, face):
        x = i * BLOCK
        coefs, masks = coef[pl.ds(x, BLOCK + 1)], active[pl.ds(x, BLOCK + 1)]
        here, mask = coefs[:BLOCK], masks[:BLOCK]
        after = coarse_weight(here, coefs[1:])
        before = jnp.concatenate([face, after[:-1]], 0)
        beside = jnp.where(last_y, 0.0, coarse_weight(here, y_after(here)))
        above = coarse_weight(here, shift(here, -1, 3))
        inner = jnp.where(highest, 0.0, above)
        top = jnp.where(highest, 4.0 * here, above)
        total = after + before + beside + y_before(beside) + top + shift(inner, 1, 3)
        diag[pl.ds(x, BLOCK)] = mask * total
        wx[pl.ds(x + 1, BLOCK)] = after * (mask * masks[1:])
        wy[pl.ds(x, BLOCK)] = beside * (mask * y_after(mask))
        wz[pl.ds(x, BLOCK)] = inner * (mask * shift(mask, -1, 3))
        return after[-1:]

    lax.fori_loop(0, count // BLOCK, setup, jnp.zeros((1, 2, *vector), F32))

    def whole(total):
        return jnp.sum(jnp.sum(total, axis=0, keepdims=True), axis=1, keepdims=True)

    def fold(total, value):
        return total + jnp.sum(value, axis=(0, 1))

    first = 2 * lax.axis_index("wide")
    ratio = scale = norm = jnp.zeros((1, 1), F32)
    for iteration in range(ITERS):
        start = iteration == 0
        if not start:
            wide_ratio = jnp.broadcast_to(ratio, vector)[None, None]
            wide_scale = jnp.broadcast_to(scale, vector)[None, None]

        def renew(x, size):
            value = residual[pl.ds(x + pad, size)]
            if start:
                return value
            slope_here = image[pl.ds(x, size)]
            if iteration > 1:
                slope_here = slope_here + wide_ratio * slope[pl.ds(x, size)]
            if iteration < ITERS - 1:
                slope[pl.ds(x, size)] = slope_here
            value = value - wide_scale * slope_here
            residual[pl.ds(x + pad, size)] = value
            return value

        def apply(i, carry):
            x = i * BLOCK
            norm_sum, image_sum, last = carry
            grown = jnp.concatenate([last, renew(x + 1, BLOCK)], 0)
            before, here, after = grown[:BLOCK], grown[1:BLOCK + 1], grown[2:]
            weight_y, weight_z = wy[pl.ds(x, BLOCK)], wz[pl.ds(x, BLOCK)]
            faces = wx[pl.ds(x, BLOCK + 1)]
            coupled = faces[1:] * after + faces[:-1] * before
            coupled = coupled + weight_y * y_after(here) + y_before(weight_y * here)
            coupled = coupled + weight_z * shift(here, -1, 3) + shift(weight_z * here, 1, 3)
            value = diag[pl.ds(x, BLOCK)] * here - coupled
            image[pl.ds(x, BLOCK)] = value
            return fold(norm_sum, here * here), fold(image_sum, here * value), grown[BLOCK:]

        opening = jnp.concatenate([jnp.zeros((1, 2, *vector), F32), renew(0, 1)], 0)
        norm_sum, image_sum, _ = lax.fori_loop(0, count // BLOCK, apply, (zero, zero, opening))
        fresh, curvature = whole(norm_sum), whole(image_sum)
        here = residual[pl.ds(first, 6)]
        if start:
            scale = fresh / curvature
            direction[...] = here
            solution[...] = jnp.broadcast_to(scale, vector)[None, None] * here
        else:
            ratio = fresh / norm
            scale = fresh / (curvature - ratio * fresh / scale)
            here = here + jnp.broadcast_to(ratio, vector)[None, None] * direction[...]
            direction[...] = here
            solution[...] = solution[...] + jnp.broadcast_to(scale, vector)[None, None] * here
        norm = fresh

    position = 2 * lax.axis_index("z") + own_core
    wanted[...] = jnp.zeros(wanted.shape, F32)
    for j in range(3):
        group = jnp.clip(position + j - 1, 0, 2 * deep - 1)
        core, row = group & 1, group >> 1
        for i in range(6):
            wanted[3 * i + j:3 * i + j + 1, :] = solution[i, core, pl.ds(row, 1), :]


def finish_kernel(
    wanted, even_ref, odd_ref,
    load1_ref, active1_ref, wx1_ref, wy1_ref, wz1_ref, diag1_ref, inv1_ref, smooth1_ref,
    load0_ref, active0_ref, wx0_ref, wy0_ref, wz0_ref, diag0_ref, inv0_ref, smooth0_ref,
    out_ref,
    spread, guess1, update1, second1, children, guess0, update0, second0,
):
    entry = lax.broadcasted_iota(jnp.int32, (BZ, 4 * BZ), 0)
    columns = lane_index((BZ, 4 * BZ))
    chosen = entry == (columns // BZ) * 32 + (columns % BZ) // 4
    spread[...] = jnp.dot(
        wanted[...], chosen.astype(F32), precision=lax.Precision.HIGHEST, preferred_element_type=F32
    )
    even = lax.axis_index("wide") % 2 == 0
    for i in range(6):
        rows = []
        for y in range(12):
            r, c = 3 * i + y // 4, y % 4
            row = spread[r:r + 1, c * BZ:(c + 1) * BZ]
            rows.append(jnp.broadcast_to(row, (2, BZ)))
        parent = jnp.concatenate(rows, 0)
        for x in (2 * i, 2 * i + 1):
            if x in (0, MX - 1):
                continue
            if x <= 2:
                value = jnp.where(even, odd_ref[x - 1], even_ref[x - 1])
            elif x >= MX - 3:
                value = jnp.where(even, even_ref[x - (MX - 3)], odd_ref[x - (MX - 3)])
            else:
                value = smooth1_ref[x]
            guess1[x] = value + active1_ref[x] * parent

    def middle_operate(ref, x):
        return operate(
            ref[x - 1], ref[x], ref[x + 1], wx1_ref[x + 1], wx1_ref[x], wy1_ref[x], wz1_ref[x],
            diag1_ref[x], active1_ref[x], 2,
        )

    def middle_first(x, slot):
        residual_here = load1_ref[x] - middle_operate(guess1, x)
        value = residual_here * (inv1_ref[x] * inverse_center)
        update1[x] = value
        second1[x] = guess1[x] + value

    loop(2, MX - 2, 4, middle_first)

    def middle_second(x, slot):
        residual_here = load1_ref[x] - middle_operate(second1, x)
        value = second1[x] + (
            carry_weight * update1[x] + fresh_weight * residual_here * inv1_ref[x]
        )
        guess1[x] = value

    loop(3, MX - 3, 3, middle_second)

    def fine_guess(x, slot):
        value = guess1[x]
        children[slot, pl.ds(0, MY, stride=2), :] = value
        children[slot, pl.ds(1, MY, stride=2), :] = value
        child = children[slot, Y0:Y0 + TY, :]
        for i in range(2):
            k = 2 * x + i - X0
            guess0[k] = smooth0_ref[k] + active0_ref[k] * child

    loop(X0 // 2, (X0 + TX) // 2, 2, fine_guess)

    def fine_operate(ref, x):
        return operate(
            ref[x - 1], ref[x], ref[x + 1], wx0_ref[x + 1], wx0_ref[x], wy0_ref[x], wz0_ref[x],
            diag0_ref[x], active0_ref[x], 1,
        )

    def fine_first(x, slot):
        residual_here = load0_ref[x] - fine_operate(guess0, x)
        value = residual_here * (inv0_ref[x] * inverse_center)
        update0[x] = value
        second0[x] = guess0[x] + value

    loop(1, TX - 1, 2, fine_first)
    margin = BX - X0

    def fine_second(x, slot):
        residual_here = load0_ref[x] - fine_operate(second0, x)
        value = second0[x] + (
            carry_weight * update0[x] + fresh_weight * residual_here * inv0_ref[x]
        )
        out_ref[x - margin] = value[BY - Y0:2 * BY - Y0]

    loop(margin, margin + BX, 2, fine_second)


def in_vmem(count):
    return [pl.BlockSpec(memory_space=pltpu.VMEM)] * count


def grids(count, *shape):
    return [jax.ShapeDtypeStruct(shape, F32)] * count


def scratch(count, *shape):
    return [pltpu.VMEM(shape, F32)] * count


def strip_part(own, odd, even):
    return pl.pallas_call(
        strip_kernel,
        out_shape=grids(2, STRIP + (STRIP + 1) // 2, 8, BZ),
        in_specs=in_vmem(3),
        out_specs=in_vmem(2),
        compiler_params=pltpu.CompilerParams(vmem_limit_bytes=4 * 2**20),
        name="strip_part",
    )(own, odd, even)


def local_part(own, odd, even, far, near, fan):
    middle = grids(8, MX, MY, BZ)
    middle[2] = jax.ShapeDtypeStruct((MX + 1, MY, BZ), F32)
    outs = (
        grids(1, fan * ROWS, BZ) + grids(1, 2, MY, BZ) + middle + grids(8, TX, TY, BZ)
    )
    big = scratch(10, EX, EY, BZ)
    big[3] = pltpu.VMEM((EX + 1, EY, BZ), F32)
    return pl.pallas_call(
        local_kernel,
        out_shape=outs,
        in_specs=in_vmem(5),
        out_specs=in_vmem(len(outs)),
        scratch_shapes=big + scratch(2, MX, MY, BZ) + scratch(1, 2, EY, BZ)
        + scratch(1, MX, MY, BZ) + scratch(1, MY, BZ),
        compiler_params=pltpu.CompilerParams(vmem_limit_bytes=24 * 2**20),
        name="local_part",
    )(own, odd, even, far, near)


def coarse_part(wide, deep, mine, other):
    count = 2 * wide
    tile = (2, deep, BZ)
    work = count * 2 * deep * BZ
    return pl.pallas_call(
        functools.partial(coarse_kernel, wide, deep),
        out_shape=jax.ShapeDtypeStruct((24, BZ), F32),
        in_specs=in_vmem(2),
        out_specs=pl.BlockSpec(memory_space=pltpu.VMEM),
        scratch_shapes=scratch(3, count + 1, *tile)
        + scratch(3, count, *tile) + scratch(1, count + 4, *tile) + scratch(2, count + 1, *tile)
        + scratch(2, 6, *tile),
        compiler_params=pltpu.CompilerParams(vmem_limit_bytes=16 * 2**20),
        cost_estimate=pl.CostEstimate(flops=250 * work, bytes_accessed=8 * work * 4, transcendentals=0),
        name="coarse_part",
    )(mine, other)


def finish_part(wanted, even, odd, kept):
    return pl.pallas_call(
        finish_kernel,
        out_shape=jax.ShapeDtypeStruct((BX, BY, BZ), F32),
        in_specs=in_vmem(3 + len(kept)),
        out_specs=pl.BlockSpec(memory_space=pltpu.VMEM),
        scratch_shapes=scratch(1, 24, 4 * BZ)
        + scratch(3, MX, MY, BZ) + scratch(1, 2, EY, BZ) + scratch(3, TX, TY, BZ),
        compiler_params=pltpu.CompilerParams(vmem_limit_bytes=8 * 2**20),
        name="finish_part",
    )(wanted, even, odd, *kept)


def swapped(size, start):
    pairs = [(i, i + 1) for i in range(start, size - 1, 2)]
    return pairs + [(j, i) for i, j in pairs]


def pack_kernel(source_ref, coef_ref, tops_ref, own_ref, odd_ref, even_ref, tops, sems):
    odd = lax.axis_index("wide") % 2
    moves = (
        (tops_ref, tops),
        (source_ref, own_ref.at[pl.ds(0, BX)]),
        (coef_ref, own_ref.at[pl.ds(BX, BX)]),
        (source_ref.at[pl.ds(odd * (BX - NS), NS)], odd_ref.at[pl.ds(0, NS)]),
        (coef_ref.at[pl.ds(odd * (BX - NC), NC)], odd_ref.at[pl.ds(NS, NC)]),
        (source_ref.at[pl.ds((1 - odd) * (BX - NS), NS)], even_ref.at[pl.ds(0, NS)]),
        (coef_ref.at[pl.ds((1 - odd) * (BX - NC), NC)], even_ref.at[pl.ds(NS, NC)]),
    )
    copies = [pltpu.make_async_copy(*move, sems.at[i]) for i, move in enumerate(moves)]
    for copy in copies:
        copy.start()
    copies[0].wait()
    values = tops[...].astype(F32)
    same = lax.broadcasted_iota(jnp.int32, (BY, BY), 0) == lane_index((BY, BY))
    lanes = lane_index((BY, BZ))
    turned = jnp.zeros((BY, BZ), F32)
    for x in range(BX):
        column = jnp.sum(jnp.where(same, values[x:x + 1], 0.0), axis=1, keepdims=True)
        turned = jnp.where(lanes == x, column, turned)
    own_ref[PACK - 1] = turned
    odd_ref[SIDE - 1] = turned
    even_ref[SIDE - 1] = turned
    for copy in copies[1:]:
        copy.wait()


def pack_part(source, conductivity, ice_cells):
    return pl.pallas_call(
        pack_kernel,
        out_shape=grids(1, PACK, BY, BZ) + grids(2, SIDE, BY, BZ),
        in_specs=[pl.BlockSpec(memory_space=pltpu.HBM)] * 3,
        out_specs=in_vmem(3),
        scratch_shapes=[pltpu.VMEM((BX, BY), jnp.int32), pltpu.SemaphoreType.DMA((7,))],
        compiler_params=pltpu.CompilerParams(vmem_limit_bytes=4 * 2**20),
        name="pack_part",
    )(*(pltpu.with_memory_space_constraint(v, pltpu.HBM) for v in (source, conductivity, ice_cells)))


def shards(wide, deep, source, conductivity, ice_cells):
    own, odd, even = pack_part(source, conductivity, ice_cells)
    odd = lax.ppermute(odd, "wide", swapped(wide, 1))
    even = lax.ppermute(even, "wide", swapped(wide, 0))
    far, near = strip_part(own, odd, even)
    far = lax.ppermute(far, ("z", "core"), swapped(2 * deep, 1))
    near = lax.ppermute(near, ("z", "core"), swapped(2 * deep, 0))
    fan, edge, *kept = local_part(own, odd, even, far, near, wide * deep)
    fan = fan.reshape(wide * deep, 1, ROWS * BZ)
    mine = lax.all_to_all(fan, ("wide", "z"), 0, 0, tiled=True)
    mine = mine.reshape(wide * deep * ROWS, BZ)
    other = lax.ppermute(mine, "core", [(0, 1), (1, 0)])
    even = lax.ppermute(edge, "wide", swapped(wide, 0))
    odd = lax.ppermute(edge, "wide", swapped(wide, 1))
    wanted = coarse_part(wide, deep, mine, other)
    return finish_part(wanted, even, odd, kept)


def solution(mesh):
    wide, deep = mesh.shape["wide"], mesh.shape["grp"] // 2
    split = Mesh(mesh.devices.reshape(wide, deep, 2), ("wide", "z", "core"))
    group = ("z", "core")
    return jax.shard_map(
        functools.partial(shards, wide, deep),
        mesh=split,
        in_specs=(P("wide", group, None), P("wide", group, None), P("wide", group)),
        out_specs=P("wide", group, None),
        check_vma=False,
    )
```

```python
import functools

import jax
import jax.numpy as jnp
from jax import lax
from jax.experimental import pallas as pl
from jax.experimental.pallas import tpu as pltpu
from jax.sharding import Mesh
from jax.sharding import PartitionSpec as P

ITERS = 6

cheb_center = (2.0 + 0.3) / 2.0
cheb_radius = (2.0 - 0.3) / 2.0
first_ratio = cheb_radius / cheb_center
second_ratio = 1.0 / (2.0 * cheb_center / cheb_radius - first_ratio)
carry_weight = second_ratio * first_ratio
fresh_weight = 2.0 * second_ratio / cheb_radius
inverse_center = 1.0 / cheb_center

F32 = jnp.float32
BX, BY, BZ = 8, 16, 128
PACK = 2 * BX + 1
NS, NC = 6, 7
SIDE = NS + NC + 1
STRIP = 2 * SIDE + PACK
HALF = 4
EX, EY = 3 * BX, 3 * BY
MX, MY = EX // 2, EY // 2
TX, TY = 12, 32
X0, Y0 = 6, 8
BLOCK = 4
SETUP = 2
ROWS = 5


def lane_index(shape):
    return lax.broadcasted_iota(jnp.int32, shape, len(shape) - 1)


def pair_weight(factor, coef, neighbour):
    total = coef + neighbour
    return (2.0 * factor) * coef * neighbour / jnp.where(total > 0.0, total, 1.0)


def shift(value, amount, axis):
    return pltpu.roll(value, amount % value.shape[axis], axis)


def operate(before, value, after, weight_x, weight_x_before, weight_y, weight_z, diagonal, active, step_z):
    coupled = weight_x * after + weight_x_before * before
    coupled = coupled + weight_y * shift(value, -1, 0)
    coupled = coupled + shift(weight_y * value, 1, 0)
    coupled = coupled + weight_z * shift(value, -step_z, 1)
    coupled = coupled + shift(weight_z * value, step_z, 1)
    return active * (diagonal * value - coupled)


def pair_lanes(value, step, combine):
    lanes = lane_index(value.shape)
    other = jnp.where((lanes & step) == 0, shift(value, -step, 1), shift(value, step, 1))
    return combine(value, other)


def loop(low, high, step, body):
    assert (high - low) % step == 0

    def turn(i, carry):
        for k in range(step):
            body(low + i * step + k, k)
        return carry

    lax.fori_loop(0, (high - low) // step, turn, 0)


def face_weights(factor, coef_ref, wx_ref, wy_ref, wz_ref, low, high, step, step_z):
    def body(x, slot):
        coef = coef_ref[x]
        lanes = lane_index(coef.shape)
        wx_ref[x + 1] = pair_weight(factor, coef, coef_ref[x + 1])
        wy_ref[x] = pair_weight(factor, coef, shift(coef, -1, 0))
        weight = pair_weight(factor, coef, shift(coef, -step_z, 1))
        wz_ref[x] = jnp.where(lanes >= BZ - step_z, 0.0, weight)

    wx_ref[low] = pair_weight(factor, coef_ref[low - 1], coef_ref[low])
    loop(low, high, step, body)


def diagonal_of(factor, x, coef_ref, wx_ref, wy_ref, wz_ref, step_z):
    coef = coef_ref[x]
    lanes = lane_index(coef.shape)
    weight_y, weight_z = wy_ref[x], wz_ref[x]
    top = jnp.where(lanes >= BZ - step_z, factor * coef, weight_z)
    total = wx_ref[x + 1] + wx_ref[x] + weight_y + shift(weight_y, 1, 0)
    return total + top + shift(weight_z, step_z, 1)


def inverse_of(diagonal):
    return 1.0 / jnp.where(diagonal > 0.0, diagonal, 1.0)


def pick(even, first, second):
    return jnp.where(even, first, second)


def strip_row(i, own_ref, left_ref, right_ref, even):
    if i < SIDE:
        return pick(even, left_ref[i], right_ref[i])
    if i < SIDE + PACK:
        return own_ref[i - SIDE]
    k = i - SIDE - PACK
    return pick(even, right_ref[k], left_ref[k])


def strip_kernel(own_ref, left_ref, right_ref, far_ref, near_ref):
    even = lax.axis_index("wide") % 2 == 0
    first_core = lax.axis_index("core") == 0
    for i in range(STRIP):
        row = strip_row(i, own_ref, left_ref, right_ref, even)
        k, part = STRIP + i // 2, slice(HALF * (i % 2), HALF * (i % 2 + 1))
        low, low_half = row[:8], row[8:8 + HALF]
        high, high_half = row[BY - 8:], row[BY - 8 - HALF:BY - 8]
        far_ref[i] = pick(first_core, low, high)
        far_ref[k, part] = pick(first_core, low_half, high_half)
        near_ref[i] = pick(first_core, high, low)
        near_ref[k, part] = pick(first_core, high_half, low_half)


def local_kernel(
    own_ref, left_ref, right_ref, far_ref, near_ref,
    fan_ref, edge_ref,
    load1_ref, active1_ref, wx1_ref, wy1_ref, wz1_ref, diag1_ref, inv1_ref, smooth1_ref,
    load0_ref, active0_ref, wx0_ref, wy0_ref, wz0_ref, diag0_ref, inv0_ref, smooth0_ref,
    source, coef, active, wx, wy, wz, diag, inv, update, smooth, coef1, update1, pairs, tops, coarse,
):
    edge_rows = jnp.zeros((8 - HALF, BZ), F32)

    even = lax.axis_index("wide") % 2 == 0
    first_core = lax.axis_index("core") == 0

    def extended(i):
        k, part = STRIP + i // 2, slice(HALF * (i % 2), HALF * (i % 2 + 1))
        far, near, far_half, near_half = far_ref[i], near_ref[i], far_ref[k, part], near_ref[k, part]
        return jnp.concatenate(
            [
                edge_rows,
                pick(first_core, far_half, near_half),
                pick(first_core, far, near),
                strip_row(i, own_ref, left_ref, right_ref, even),
                pick(first_core, near, far),
                pick(first_core, near_half, far_half),
                edge_rows,
            ],
            0,
        )

    middle = SIDE
    last = SIDE + PACK
    for i in range(NS):
        source[BX - NS + i] = extended(i)
        source[2 * BX + i] = extended(last + i)
    for i in range(NC):
        coef[BX - NC + i] = extended(NS + i)
        coef[2 * BX + i] = extended(last + NS + i)
    for i in range(BX):
        source[BX + i] = extended(middle + i)
        coef[BX + i] = extended(middle + BX + i)
    for j, i in enumerate((SIDE - 1, last - 1, STRIP - 1)):
        columns = extended(i)
        for x in range(BX):
            active[j * BX + x] = jnp.broadcast_to(columns[:, x:x + 1], (EY, BZ))

    low0, high0 = BX - NS, 2 * BX + NS
    low1, high1 = low0 // 2 + 1, high0 // 2 - 1

    def middle_tops(x, slot):
        pairs[slot] = jnp.maximum(active[2 * x], active[2 * x + 1])
        value = jnp.maximum(
            pairs[slot, pl.ds(0, MY, stride=2), :], pairs[slot, pl.ds(1, MY, stride=2), :]
        )
        tops[x] = value
        layer = (lane_index((MY, BZ)) & ~1).astype(F32)
        active1_ref[x] = (layer < value).astype(F32)

    loop(0, MX, 2, middle_tops)

    def fine_mask(x, slot):
        layer = lane_index((EY, BZ)).astype(F32)
        mask = (layer < active[x]).astype(F32)
        active[x] = mask
        source[x] = mask * source[x]

    loop(low0, high0, 2, fine_mask)

    face_weights(1.0, coef, wx, wy, wz, low0, high0, 2, 1)

    def fine_start(x, slot):
        diagonal = diagonal_of(1.0, x, coef, wx, wy, wz, 1)
        inverse = inverse_of(diagonal)
        diag[x] = diagonal
        inv[x] = inverse
        update[x] = source[x] * (inverse * inverse_center)

    loop(low0, high0, 2, fine_start)

    def fine_operate(ref, x):
        return operate(ref[x - 1], ref[x], ref[x + 1], wx[x + 1], wx[x], wy[x], wz[x], diag[x], active[x], 1)

    def fine_finish(x, slot):
        residual = source[x] - fine_operate(update, x)
        first = update[x]
        smooth[x] = first + (carry_weight * first + fresh_weight * residual * inv[x])

    loop(low0 + 1, high0 - 1, 2, fine_finish)

    def keep(i, slot):
        for kept, ref in (
            (load0_ref, source), (active0_ref, active), (wy0_ref, wy), (wz0_ref, wz),
            (diag0_ref, diag), (inv0_ref, inv), (smooth0_ref, smooth),
        ):
            kept[i] = ref[X0 + i, Y0:Y0 + TY, :]
        wx0_ref[i] = wx[X0 + i, Y0:Y0 + TY, :]

    loop(0, TX, 2, keep)

    def restrict(value, slot):
        pairs[slot] = pair_lanes(value, 1, jnp.add)
        return pairs[slot, pl.ds(0, MY, stride=2), :] + pairs[slot, pl.ds(1, MY, stride=2), :]

    def middle_coef(x, slot):
        coef1[x] = restrict(coef[2 * x] + coef[2 * x + 1], slot) * 0.125

    loop(low1 - 1, high1 + 1, 2, middle_coef)

    def middle_load(x, slot):
        left = source[2 * x] - fine_operate(smooth, 2 * x)
        right = source[2 * x + 1] - fine_operate(smooth, 2 * x + 1)
        load1_ref[x] = restrict(left + right, slot)

    loop(low1, high1, 2, middle_load)

    face_weights(2.0, coef1, wx1_ref, wy1_ref, wz1_ref, low1, high1, 4, 2)

    def middle_start(x, slot):
        diagonal = diagonal_of(2.0, x, coef1, wx1_ref, wy1_ref, wz1_ref, 2)
        inverse = inverse_of(diagonal)
        diag1_ref[x] = diagonal
        inv1_ref[x] = inverse
        update1[x] = load1_ref[x] * (inverse * inverse_center)

    loop(low1, high1, 4, middle_start)

    def middle_operate(ref, x):
        return operate(
            ref[x - 1], ref[x], ref[x + 1], wx1_ref[x + 1], wx1_ref[x], wy1_ref[x], wz1_ref[x],
            diag1_ref[x], active1_ref[x], 2,
        )

    def middle_finish(x, slot):
        residual = load1_ref[x] - middle_operate(update1, x)
        first = update1[x]
        smooth1_ref[x] = first + (carry_weight * first + fresh_weight * residual * inv1_ref[x])

    loop(low1 + 1, high1 - 1, 3, middle_finish)
    for i in range(2):
        edge_ref[i] = smooth1_ref[MX // 2 - 1 + i]

    first_x, first_y = MX // 3, MY // 3
    rows = []
    for part in range(2):
        for cx in range(2):
            if part == 0:
                total = sum(
                    load1_ref[x] - middle_operate(smooth1_ref, x)
                    for x in (first_x + 2 * cx, first_x + 2 * cx + 1)
                )
            else:
                total = (coef1[first_x + 2 * cx] + coef1[first_x + 2 * cx + 1]) * 0.125
            coarse[...] = pair_lanes(total, 2, jnp.add)
            value = (
                coarse[pl.ds(first_y, 4, stride=2), :] + coarse[pl.ds(first_y + 1, 4, stride=2), :]
            )
            rows.append(jnp.concatenate([value[i:i + 1] for i in range(4)], 1))
    spread = jnp.concatenate(rows + [jnp.zeros((4, 4 * BZ), F32)], 0)
    entry = lax.broadcasted_iota(jnp.int32, (4 * BZ, BZ), 0)
    lanes = lane_index((4 * BZ, BZ))
    chosen = (entry // BZ == lanes // 32) & (entry % BZ == (lanes % 32) * 4)
    packed = jnp.dot(
        spread, chosen.astype(F32), precision=lax.Precision.HIGHEST, preferred_element_type=F32
    )
    lanes = lane_index((1, BZ))
    top_row = jnp.zeros((1, BZ), F32)
    for cx in range(2):
        coarse[...] = jnp.maximum(tops[first_x + 2 * cx], tops[first_x + 2 * cx + 1])
        value = jnp.maximum(
            coarse[pl.ds(first_y, 4, stride=2), :], coarse[pl.ds(first_y + 1, 4, stride=2), :]
        )
        for cy in range(4):
            top_row = jnp.where(lanes // 16 == 2 * cy + cx, value[cy:cy + 1], top_row)
    block = [packed[i:i + 1] for i in range(4)] + [top_row]
    pattern = jnp.concatenate(block * 8, 0)

    def fan(i, carry):
        fan_ref[pl.ds(pl.multiple_of(i * 8 * ROWS, 8), 8 * ROWS), :] = pattern
        return carry

    lax.fori_loop(0, fan_ref.shape[0] // (8 * ROWS), fan, 0)


def block_transpose(values, lanes):
    odd, high = (lanes & 32) != 0, (lanes & 64) != 0
    turn = [jnp.where(odd, values[(j + 1) % 4], values[j]) for j in range(4)]
    turn = [jnp.where(high, turn[(j + 2) % 4], turn[j]) for j in range(4)]
    skew = [shift(turn[(4 - d) % 4], -32 * d, 1) if d else turn[0] for d in range(4)]
    back = [jnp.where(odd, skew[(j + 3) % 4], skew[j]) for j in range(4)]
    return [jnp.where(high, back[(j + 2) % 4], back[j]) for j in range(4)]


def coarse_kernel(
    wide, deep, mine_ref, other_ref, wanted,
    coef, active, wx, wy, wz, diag, residual, image, slope, direction, solution,
):
    count = 2 * wide
    planes = count // 4
    block = min(BLOCK, planes)
    vector = (deep, BZ)
    lanes = lane_index(vector)
    zero = jnp.zeros(vector, F32)
    highest = (lanes & 31) == 31
    last_row = lax.broadcasted_iota(jnp.int32, vector, 0) == deep - 1
    last_block = lanes >= 96

    def y_after(value):
        return jnp.concatenate([value[:, 1:], shift(value[:, :1], -1, 2)], 1)

    def y_before(value):
        return jnp.concatenate([shift(value[:, 7:], 1, 2), value[:, :7]], 1)

    stride = deep * ROWS
    low = (lanes & 16) == 0
    layer = ((lanes & 31) * 4).astype(F32)

    def unpack(refs):
        def body(w, slot):
            for c in range(2):
                def turned(k):
                    return block_transpose(
                        [
                            refs[c][pl.ds((q * (wide // 4) + w) * stride + k, deep, stride=ROWS), :]
                            for q in range(4)
                        ],
                        lanes,
                    )

                loads, coefs, tops = (turned(0), turned(1)), (turned(2), turned(3)), turned(4)
                for y in range(4):
                    tall = (
                        jnp.where(low, tops[y], shift(tops[y], 16, 1)),
                        jnp.where(low, shift(tops[y], -16, 1), tops[y]),
                    )
                    for i in range(2):
                        residual[2 * w + i, 4 * c + y] = loads[i][y]
                        coef[2 * w + i, 4 * c + y] = coefs[i][y]
                        active[2 * w + i, 4 * c + y] = (layer < tall[i]).astype(F32)

        loop(0, planes // 2, 1, body)

    own_core = lax.axis_index("core")

    @pl.when(own_core == 0)
    def _():
        unpack((mine_ref, other_ref))

    @pl.when(own_core == 1)
    def _():
        unpack((other_ref, mine_ref))

    def coarse_weight(a, b):
        return 8.0 * a * b / (a + b)

    coef[planes] = jnp.where(last_block, 0.0, shift(coef[0], -32, 2))
    active[planes] = jnp.where(last_block, 0.0, shift(active[0], -32, 2))

    def setup(i, face):
        x = i * SETUP
        coefs, masks = coef[pl.ds(x, SETUP + 1)], active[pl.ds(x, SETUP + 1)]
        here, mask = coefs[:SETUP], masks[:SETUP]
        after = coarse_weight(here, coefs[1:])
        before = jnp.concatenate([face, after[:-1]], 0)
        beside = coarse_weight(here, y_after(here))
        beside = jnp.concatenate([beside[:, :7], jnp.where(last_row, 0.0, beside[:, 7:])], 1)
        above = coarse_weight(here, shift(here, -1, 3))
        inner = jnp.where(highest, 0.0, above)
        top = jnp.where(highest, 4.0 * here, above)
        total = after + before + beside + y_before(beside) + top + shift(inner, 1, 3)
        diag[pl.ds(x, SETUP)] = mask * total
        wx[pl.ds(x + 1, SETUP)] = after * (mask * masks[1:])
        wy[pl.ds(x, SETUP)] = beside * (mask * y_after(mask))
        wz[pl.ds(x, SETUP)] = inner * (mask * shift(mask, -1, 3))
        return after[-1:]

    closing = coarse_weight(coef[planes - 1:planes], coef[planes:planes + 1])
    lax.fori_loop(0, planes // SETUP, setup, shift(closing, 32, 3))
    wx[0] = shift(wx[planes], 32, 2)

    def whole(total):
        return jnp.sum(jnp.sum(total, axis=0, keepdims=True), axis=1, keepdims=True)

    def fold(total, value):
        return total + jnp.sum(value, axis=(0, 1))

    first_x = 2 * lax.axis_index("wide") - 2
    position = 2 * lax.axis_index("z") + own_core
    xs = [jnp.clip(first_x + i, 0, count - 1) for i in range(6)]
    groups = [jnp.clip(position + j - 1, 0, 2 * deep - 1) for j in range(3)]
    direction[...] = jnp.zeros(direction.shape, F32)
    solution[...] = jnp.zeros(solution.shape, F32)
    wanted[...] = jnp.zeros(wanted.shape, F32)

    ratio = scale = norm = jnp.zeros((1, 1), F32)
    for iteration in range(ITERS):
        start = iteration == 0
        if not start:
            wide_ratio = jnp.broadcast_to(ratio, vector)[None, None]
            wide_scale = jnp.broadcast_to(scale, vector)[None, None]

        def renew(x, size, keep=True):
            value = residual[pl.ds(x, size)]
            if start:
                return value
            slope_here = image[pl.ds(x, size)]
            if iteration > 1:
                slope_here = slope_here + wide_ratio * slope[pl.ds(x, size)]
            value = value - wide_scale * slope_here
            if keep:
                if iteration < ITERS - 1:
                    slope[pl.ds(x, size)] = slope_here
                residual[pl.ds(x, size)] = value
            return value

        def apply(x, carry, later):
            norm_sum, image_sum, last = carry
            grown = jnp.concatenate([last, later], 0)
            before, here, after = grown[:block], grown[1:block + 1], grown[2:]
            weight_y, weight_z = wy[pl.ds(x, block)], wz[pl.ds(x, block)]
            faces = wx[pl.ds(x, block + 1)]
            coupled = faces[1:] * after + faces[:-1] * before
            coupled = coupled + weight_y * y_after(here) + y_before(weight_y * here)
            coupled = coupled + weight_z * shift(here, -1, 3) + shift(weight_z * here, 1, 3)
            value = diag[pl.ds(x, block)] * here - coupled
            image[pl.ds(x, block)] = value
            return fold(norm_sum, here * here), fold(image_sum, here * value), grown[block:]

        before_first = shift(renew(planes - 1, 1, False), 32, 3)
        opening = renew(0, 1)
        carry = (zero, zero, jnp.concatenate([before_first, opening], 0))

        def turn(i, carry):
            x = i * block
            return apply(x, carry, renew(x + 1, block))

        carry = lax.fori_loop(0, planes // block - 1, turn, carry)
        x = planes - block
        beyond = shift(residual[0:1], -32, 3)
        if block > 1:
            beyond = jnp.concatenate([renew(x + 1, block - 1), beyond], 0)
        norm_sum, image_sum, _ = apply(x, carry, beyond)
        for i in range(6):
            for j in range(3):
                for y in range(4):
                    row = 16 * i + 4 * j + y
                    wanted[row:row + 1, :] = residual[
                        lax.rem(xs[i], planes), 4 * (groups[j] & 1) + y, pl.ds(groups[j] >> 1, 1), :
                    ]
        fresh, curvature = whole(norm_sum), whole(image_sum)
        here = wanted[...]
        if start:
            scale = fresh / curvature
        else:
            ratio = fresh / norm
            scale = fresh / (curvature - ratio * fresh / scale)
            here = here + ratio * direction[...]
        direction[...] = here
        solution[...] = solution[...] + scale * here
        norm = fresh

    columns = lane_index((16, BZ))
    for i in range(6):
        own_block = columns // 32 == xs[i] // planes
        wanted[16 * i:16 * i + 16] = jnp.where(own_block, solution[16 * i:16 * i + 16], 0.0)


def finish_kernel(
    wanted, even_ref, odd_ref,
    load1_ref, active1_ref, wx1_ref, wy1_ref, wz1_ref, diag1_ref, inv1_ref, smooth1_ref,
    load0_ref, active0_ref, wx0_ref, wy0_ref, wz0_ref, diag0_ref, inv0_ref, smooth0_ref,
    out_ref,
    spread, guess1, update1, second1, children, guess0, update0, second0,
):
    entry = lax.broadcasted_iota(jnp.int32, (BZ, BZ), 0)
    chosen = entry % 32 == lane_index((BZ, BZ)) // 4
    spread[...] = jnp.dot(
        wanted[...], chosen.astype(F32), precision=lax.Precision.HIGHEST, preferred_element_type=F32
    )
    even = lax.axis_index("wide") % 2 == 0
    for i in range(6):
        rows = []
        for y in range(12):
            row = spread[16 * i + y:16 * i + y + 1]
            rows.append(jnp.broadcast_to(row, (2, BZ)))
        parent = jnp.concatenate(rows, 0)
        for x in (2 * i, 2 * i + 1):
            if x in (0, MX - 1):
                continue
            if x <= 2:
                value = jnp.where(even, odd_ref[x - 1], even_ref[x - 1])
            elif x >= MX - 3:
                value = jnp.where(even, even_ref[x - (MX - 3)], odd_ref[x - (MX - 3)])
            else:
                value = smooth1_ref[x]
            guess1[x] = value + active1_ref[x] * parent

    def middle_operate(ref, x):
        return operate(
            ref[x - 1], ref[x], ref[x + 1], wx1_ref[x + 1], wx1_ref[x], wy1_ref[x], wz1_ref[x],
            diag1_ref[x], active1_ref[x], 2,
        )

    def middle_first(x, slot):
        residual_here = load1_ref[x] - middle_operate(guess1, x)
        value = residual_here * (inv1_ref[x] * inverse_center)
        update1[x] = value
        second1[x] = guess1[x] + value

    loop(2, MX - 2, 4, middle_first)

    def middle_second(x, slot):
        residual_here = load1_ref[x] - middle_operate(second1, x)
        value = second1[x] + (
            carry_weight * update1[x] + fresh_weight * residual_here * inv1_ref[x]
        )
        guess1[x] = value

    loop(3, MX - 3, 3, middle_second)

    def fine_guess(x, slot):
        value = guess1[x]
        children[slot, pl.ds(0, MY, stride=2), :] = value
        children[slot, pl.ds(1, MY, stride=2), :] = value
        child = children[slot, Y0:Y0 + TY, :]
        for i in range(2):
            k = 2 * x + i - X0
            guess0[k] = smooth0_ref[k] + active0_ref[k] * child

    loop(X0 // 2, (X0 + TX) // 2, 2, fine_guess)

    def fine_operate(ref, x):
        return operate(
            ref[x - 1], ref[x], ref[x + 1], wx0_ref[x + 1], wx0_ref[x], wy0_ref[x], wz0_ref[x],
            diag0_ref[x], active0_ref[x], 1,
        )

    def fine_first(x, slot):
        residual_here = load0_ref[x] - fine_operate(guess0, x)
        value = residual_here * (inv0_ref[x] * inverse_center)
        update0[x] = value
        second0[x] = guess0[x] + value

    loop(1, TX - 1, 2, fine_first)
    margin = BX - X0

    def fine_second(x, slot):
        residual_here = load0_ref[x] - fine_operate(second0, x)
        value = second0[x] + (
            carry_weight * update0[x] + fresh_weight * residual_here * inv0_ref[x]
        )
        out_ref[x - margin] = value[BY - Y0:2 * BY - Y0]

    loop(margin, margin + BX, 2, fine_second)


def in_vmem(count):
    return [pl.BlockSpec(memory_space=pltpu.VMEM)] * count


def grids(count, *shape):
    return [jax.ShapeDtypeStruct(shape, F32)] * count


def scratch(count, *shape):
    return [pltpu.VMEM(shape, F32)] * count


def strip_part(own, odd, even):
    return pl.pallas_call(
        strip_kernel,
        out_shape=grids(2, STRIP + (STRIP + 1) // 2, 8, BZ),
        in_specs=in_vmem(3),
        out_specs=in_vmem(2),
        compiler_params=pltpu.CompilerParams(vmem_limit_bytes=4 * 2**20),
        name="strip_part",
    )(own, odd, even)


def local_part(own, odd, even, far, near, fan):
    middle = grids(8, MX, MY, BZ)
    middle[2] = jax.ShapeDtypeStruct((MX + 1, MY, BZ), F32)
    outs = (
        grids(1, fan * ROWS, BZ) + grids(1, 2, MY, BZ) + middle + grids(8, TX, TY, BZ)
    )
    big = scratch(10, EX, EY, BZ)
    big[3] = pltpu.VMEM((EX + 1, EY, BZ), F32)
    return pl.pallas_call(
        local_kernel,
        out_shape=outs,
        in_specs=in_vmem(5),
        out_specs=in_vmem(len(outs)),
        scratch_shapes=big + scratch(2, MX, MY, BZ) + scratch(1, 2, EY, BZ)
        + scratch(1, MX, MY, BZ) + scratch(1, MY, BZ),
        compiler_params=pltpu.CompilerParams(vmem_limit_bytes=24 * 2**20),
        name="local_part",
    )(own, odd, even, far, near)


def coarse_part(wide, deep, mine, other):
    count = 2 * wide
    planes = count // 4
    tile = (8, deep, BZ)
    work = count * 2 * deep * BZ
    return pl.pallas_call(
        functools.partial(coarse_kernel, wide, deep),
        out_shape=jax.ShapeDtypeStruct((96, BZ), F32),
        in_specs=in_vmem(2),
        out_specs=pl.BlockSpec(memory_space=pltpu.VMEM),
        scratch_shapes=scratch(3, planes + 1, *tile) + scratch(6, planes, *tile)
        + scratch(2, 96, BZ),
        compiler_params=pltpu.CompilerParams(vmem_limit_bytes=16 * 2**20),
        cost_estimate=pl.CostEstimate(flops=250 * work, bytes_accessed=8 * work * 4, transcendentals=0),
        name="coarse_part",
    )(mine, other)


def finish_part(wanted, even, odd, kept):
    return pl.pallas_call(
        finish_kernel,
        out_shape=jax.ShapeDtypeStruct((BX, BY, BZ), F32),
        in_specs=in_vmem(3 + len(kept)),
        out_specs=pl.BlockSpec(memory_space=pltpu.VMEM),
        scratch_shapes=scratch(1, 96, BZ)
        + scratch(3, MX, MY, BZ) + scratch(1, 2, EY, BZ) + scratch(3, TX, TY, BZ),
        compiler_params=pltpu.CompilerParams(vmem_limit_bytes=8 * 2**20),
        name="finish_part",
    )(wanted, even, odd, *kept)


def swapped(size, start):
    pairs = [(i, i + 1) for i in range(start, size - 1, 2)]
    return pairs + [(j, i) for i, j in pairs]


def pack_kernel(source_ref, coef_ref, tops_ref, own_ref, odd_ref, even_ref, tops, sems):
    odd = lax.axis_index("wide") % 2
    moves = (
        (tops_ref, tops),
        (source_ref, own_ref.at[pl.ds(0, BX)]),
        (coef_ref, own_ref.at[pl.ds(BX, BX)]),
        (source_ref.at[pl.ds(odd * (BX - NS), NS)], odd_ref.at[pl.ds(0, NS)]),
        (coef_ref.at[pl.ds(odd * (BX - NC), NC)], odd_ref.at[pl.ds(NS, NC)]),
        (source_ref.at[pl.ds((1 - odd) * (BX - NS), NS)], even_ref.at[pl.ds(0, NS)]),
        (coef_ref.at[pl.ds((1 - odd) * (BX - NC), NC)], even_ref.at[pl.ds(NS, NC)]),
    )
    copies = [pltpu.make_async_copy(*move, sems.at[i]) for i, move in enumerate(moves)]
    for copy in copies:
        copy.start()
    copies[0].wait()
    values = tops[...].astype(F32)
    same = lax.broadcasted_iota(jnp.int32, (BY, BY), 0) == lane_index((BY, BY))
    lanes = lane_index((BY, BZ))
    turned = jnp.zeros((BY, BZ), F32)
    for x in range(BX):
        column = jnp.sum(jnp.where(same, values[x:x + 1], 0.0), axis=1, keepdims=True)
        turned = jnp.where(lanes == x, column, turned)
    own_ref[PACK - 1] = turned
    odd_ref[SIDE - 1] = turned
    even_ref[SIDE - 1] = turned
    for copy in copies[1:]:
        copy.wait()


def pack_part(source, conductivity, ice_cells):
    return pl.pallas_call(
        pack_kernel,
        out_shape=grids(1, PACK, BY, BZ) + grids(2, SIDE, BY, BZ),
        in_specs=[pl.BlockSpec(memory_space=pltpu.HBM)] * 3,
        out_specs=in_vmem(3),
        scratch_shapes=[pltpu.VMEM((BX, BY), jnp.int32), pltpu.SemaphoreType.DMA((7,))],
        compiler_params=pltpu.CompilerParams(vmem_limit_bytes=4 * 2**20),
        name="pack_part",
    )(*(pltpu.with_memory_space_constraint(v, pltpu.HBM) for v in (source, conductivity, ice_cells)))


def shards(wide, deep, source, conductivity, ice_cells):
    own, odd, even = pack_part(source, conductivity, ice_cells)
    odd = lax.ppermute(odd, "wide", swapped(wide, 1))
    even = lax.ppermute(even, "wide", swapped(wide, 0))
    far, near = strip_part(own, odd, even)
    far = lax.ppermute(far, ("z", "core"), swapped(2 * deep, 1))
    near = lax.ppermute(near, ("z", "core"), swapped(2 * deep, 0))
    fan, edge, *kept = local_part(own, odd, even, far, near, wide * deep)
    fan = fan.reshape(wide * deep, 1, ROWS * BZ)
    mine = lax.all_to_all(fan, ("wide", "z"), 0, 0, tiled=True)
    mine = mine.reshape(wide * deep * ROWS, BZ)
    other = lax.ppermute(mine, "core", [(0, 1), (1, 0)])
    even = lax.ppermute(edge, "wide", swapped(wide, 0))
    odd = lax.ppermute(edge, "wide", swapped(wide, 1))
    wanted = coarse_part(wide, deep, mine, other)
    return finish_part(wanted, even, odd, kept)


def solution(mesh):
    wide, deep = mesh.shape["wide"], mesh.shape["grp"] // 2
    split = Mesh(mesh.devices.reshape(wide, deep, 2), ("wide", "z", "core"))
    group = ("z", "core")
    return jax.shard_map(
        functools.partial(shards, wide, deep),
        mesh=split,
        in_specs=(P("wide", group, None), P("wide", group, None), P("wide", group)),
        out_specs=P("wide", group, None),
        check_vma=False,
    )
```

```python
import functools

import jax
import jax.numpy as jnp
from jax import lax
from jax.experimental import pallas as pl
from jax.experimental.pallas import tpu as pltpu
from jax.sharding import Mesh
from jax.sharding import PartitionSpec as P

ITERS = 6

cheb_center = (2.0 + 0.3) / 2.0
cheb_radius = (2.0 - 0.3) / 2.0
first_ratio = cheb_radius / cheb_center
second_ratio = 1.0 / (2.0 * cheb_center / cheb_radius - first_ratio)
carry_weight = second_ratio * first_ratio
fresh_weight = 2.0 * second_ratio / cheb_radius
inverse_center = 1.0 / cheb_center

F32 = jnp.float32
BX, BY, BZ = 8, 16, 128
PACK = 2 * BX + 1
NS, NC = 6, 7
SIDE = NS + NC + 1
STRIP = 2 * SIDE + PACK
HALF = 4
EX, EY = 3 * BX, 3 * BY
MX, MY = EX // 2, EY // 2
TX, TY = 12, 32
X0, Y0 = 6, 8
BLOCK = 4
SETUP = 2
ROWS = 5


def lane_index(shape):
    return lax.broadcasted_iota(jnp.int32, shape, len(shape) - 1)


def pair_weight(factor, coef, neighbour):
    total = coef + neighbour
    return (2.0 * factor) * coef * neighbour / jnp.where(total > 0.0, total, 1.0)


def shift(value, amount, axis):
    return pltpu.roll(value, amount % value.shape[axis], axis)


def operate(before, value, after, weight_x, weight_x_before, weight_y, weight_z, diagonal, active, step_z):
    coupled = weight_x * after + weight_x_before * before
    coupled = coupled + weight_y * shift(value, -1, 0)
    coupled = coupled + shift(weight_y * value, 1, 0)
    coupled = coupled + weight_z * shift(value, -step_z, 1)
    coupled = coupled + shift(weight_z * value, step_z, 1)
    return active * (diagonal * value - coupled)


def pair_lanes(value, step, combine):
    lanes = lane_index(value.shape)
    other = jnp.where((lanes & step) == 0, shift(value, -step, 1), shift(value, step, 1))
    return combine(value, other)


def loop(low, high, step, body):
    assert (high - low) % step == 0

    def turn(i, carry):
        for k in range(step):
            body(low + i * step + k, k)
        return carry

    lax.fori_loop(0, (high - low) // step, turn, 0)


def face_weights(factor, coef_ref, wx_ref, wy_ref, wz_ref, low, high, step, step_z):
    def body(x, slot):
        coef = coef_ref[x]
        lanes = lane_index(coef.shape)
        wx_ref[x + 1] = pair_weight(factor, coef, coef_ref[x + 1])
        wy_ref[x] = pair_weight(factor, coef, shift(coef, -1, 0))
        weight = pair_weight(factor, coef, shift(coef, -step_z, 1))
        wz_ref[x] = jnp.where(lanes >= BZ - step_z, 0.0, weight)

    wx_ref[low] = pair_weight(factor, coef_ref[low - 1], coef_ref[low])
    loop(low, high, step, body)


def diagonal_of(factor, x, coef_ref, wx_ref, wy_ref, wz_ref, step_z):
    coef = coef_ref[x]
    lanes = lane_index(coef.shape)
    weight_y, weight_z = wy_ref[x], wz_ref[x]
    top = jnp.where(lanes >= BZ - step_z, factor * coef, weight_z)
    total = wx_ref[x + 1] + wx_ref[x] + weight_y + shift(weight_y, 1, 0)
    return total + top + shift(weight_z, step_z, 1)


def inverse_of(diagonal):
    return 1.0 / jnp.where(diagonal > 0.0, diagonal, 1.0)


def pick(even, first, second):
    return jnp.where(even, first, second)


def strip_row(i, own_ref, left_ref, right_ref, even):
    if i < SIDE:
        return pick(even, left_ref[i], right_ref[i])
    if i < SIDE + PACK:
        return own_ref[i - SIDE]
    k = i - SIDE - PACK
    return pick(even, right_ref[k], left_ref[k])


def strip_kernel(own_ref, left_ref, right_ref, far_ref, near_ref):
    even = lax.axis_index("wide") % 2 == 0
    first_core = lax.axis_index("core") == 0
    for i in range(STRIP):
        row = strip_row(i, own_ref, left_ref, right_ref, even)
        k, part = STRIP + i // 2, slice(HALF * (i % 2), HALF * (i % 2 + 1))
        low, low_half = row[:8], row[8:8 + HALF]
        high, high_half = row[BY - 8:], row[BY - 8 - HALF:BY - 8]
        far_ref[i] = pick(first_core, low, high)
        far_ref[k, part] = pick(first_core, low_half, high_half)
        near_ref[i] = pick(first_core, high, low)
        near_ref[k, part] = pick(first_core, high_half, low_half)


def local_kernel(
    own_ref, left_ref, right_ref, far_ref, near_ref,
    fan_ref, edge_ref,
    load1_ref, active1_ref, wx1_ref, wy1_ref, wz1_ref, diag1_ref, inv1_ref, smooth1_ref,
    load0_ref, active0_ref, wx0_ref, wy0_ref, wz0_ref, diag0_ref, inv0_ref, smooth0_ref,
    source, coef, active, wx, wy, wz, diag, inv, update, smooth, coef1, update1, pairs, tops, coarse,
):
    edge_rows = jnp.zeros((8 - HALF, BZ), F32)

    even = lax.axis_index("wide") % 2 == 0
    first_core = lax.axis_index("core") == 0

    def extended(i):
        k, part = STRIP + i // 2, slice(HALF * (i % 2), HALF * (i % 2 + 1))
        far, near, far_half, near_half = far_ref[i], near_ref[i], far_ref[k, part], near_ref[k, part]
        return jnp.concatenate(
            [
                edge_rows,
                pick(first_core, far_half, near_half),
                pick(first_core, far, near),
                strip_row(i, own_ref, left_ref, right_ref, even),
                pick(first_core, near, far),
                pick(first_core, near_half, far_half),
                edge_rows,
            ],
            0,
        )

    middle = SIDE
    last = SIDE + PACK
    for i in range(NS):
        source[BX - NS + i] = extended(i)
        source[2 * BX + i] = extended(last + i)
    for i in range(NC):
        coef[BX - NC + i] = extended(NS + i)
        coef[2 * BX + i] = extended(last + NS + i)
    for i in range(BX):
        source[BX + i] = extended(middle + i)
        coef[BX + i] = extended(middle + BX + i)
    for j, i in enumerate((SIDE - 1, last - 1, STRIP - 1)):
        columns = extended(i)
        for x in range(BX):
            active[j * BX + x] = jnp.broadcast_to(columns[:, x:x + 1], (EY, BZ))

    low0, high0 = BX - NS, 2 * BX + NS
    low1, high1 = low0 // 2 + 1, high0 // 2 - 1

    def middle_tops(x, slot):
        pairs[slot] = jnp.maximum(active[2 * x], active[2 * x + 1])
        value = jnp.maximum(
            pairs[slot, pl.ds(0, MY, stride=2), :], pairs[slot, pl.ds(1, MY, stride=2), :]
        )
        tops[x] = value
        layer = (lane_index((MY, BZ)) & ~1).astype(F32)
        active1_ref[x] = (layer < value).astype(F32)

    loop(0, MX, 2, middle_tops)

    def fine_mask(x, slot):
        layer = lane_index((EY, BZ)).astype(F32)
        mask = (layer < active[x]).astype(F32)
        active[x] = mask
        source[x] = mask * source[x]

    loop(low0, high0, 4, fine_mask)

    face_weights(1.0, coef, wx, wy, wz, low0, high0, 4, 1)

    def fine_start(x, slot):
        diagonal = diagonal_of(1.0, x, coef, wx, wy, wz, 1)
        inverse = inverse_of(diagonal)
        diag[x] = diagonal
        inv[x] = inverse
        update[x] = source[x] * (inverse * inverse_center)

    loop(low0, high0, 4, fine_start)

    def fine_operate(ref, x):
        return operate(ref[x - 1], ref[x], ref[x + 1], wx[x + 1], wx[x], wy[x], wz[x], diag[x], active[x], 1)

    def fine_finish(x, slot):
        residual = source[x] - fine_operate(update, x)
        first = update[x]
        smooth[x] = first + (carry_weight * first + fresh_weight * residual * inv[x])

    loop(low0 + 1, high0 - 1, 3, fine_finish)

    def keep(i, slot):
        for kept, ref in (
            (load0_ref, source), (active0_ref, active), (wy0_ref, wy), (wz0_ref, wz),
            (diag0_ref, diag), (inv0_ref, inv), (smooth0_ref, smooth),
        ):
            kept[i] = ref[X0 + i, Y0:Y0 + TY, :]
        wx0_ref[i] = wx[X0 + i, Y0:Y0 + TY, :]

    loop(0, TX, 4, keep)

    def restrict(value, slot):
        pairs[slot] = pair_lanes(value, 1, jnp.add)
        return pairs[slot, pl.ds(0, MY, stride=2), :] + pairs[slot, pl.ds(1, MY, stride=2), :]

    def middle_coef(x, slot):
        coef1[x] = restrict(coef[2 * x] + coef[2 * x + 1], slot) * 0.125

    loop(low1 - 1, high1 + 1, 2, middle_coef)

    def middle_load(x, slot):
        left = source[2 * x] - fine_operate(smooth, 2 * x)
        right = source[2 * x + 1] - fine_operate(smooth, 2 * x + 1)
        load1_ref[x] = restrict(left + right, slot)

    loop(low1, high1, 2, middle_load)

    face_weights(2.0, coef1, wx1_ref, wy1_ref, wz1_ref, low1, high1, 4, 2)

    def middle_start(x, slot):
        diagonal = diagonal_of(2.0, x, coef1, wx1_ref, wy1_ref, wz1_ref, 2)
        inverse = inverse_of(diagonal)
        diag1_ref[x] = diagonal
        inv1_ref[x] = inverse
        update1[x] = load1_ref[x] * (inverse * inverse_center)

    loop(low1, high1, 4, middle_start)

    def middle_operate(ref, x):
        return operate(
            ref[x - 1], ref[x], ref[x + 1], wx1_ref[x + 1], wx1_ref[x], wy1_ref[x], wz1_ref[x],
            diag1_ref[x], active1_ref[x], 2,
        )

    def middle_finish(x, slot):
        residual = load1_ref[x] - middle_operate(update1, x)
        first = update1[x]
        smooth1_ref[x] = first + (carry_weight * first + fresh_weight * residual * inv1_ref[x])

    loop(low1 + 1, high1 - 1, 3, middle_finish)
    for i in range(2):
        edge_ref[i] = smooth1_ref[MX // 2 - 1 + i]

    first_x, first_y = MX // 3, MY // 3
    rows = []
    for part in range(2):
        for cx in range(2):
            if part == 0:
                total = sum(
                    load1_ref[x] - middle_operate(smooth1_ref, x)
                    for x in (first_x + 2 * cx, first_x + 2 * cx + 1)
                )
            else:
                total = (coef1[first_x + 2 * cx] + coef1[first_x + 2 * cx + 1]) * 0.125
            coarse[...] = pair_lanes(total, 2, jnp.add)
            value = (
                coarse[pl.ds(first_y, 4, stride=2), :] + coarse[pl.ds(first_y + 1, 4, stride=2), :]
            )
            rows.append(jnp.concatenate([value[i:i + 1] for i in range(4)], 1))
    spread = jnp.concatenate(rows + [jnp.zeros((4, 4 * BZ), F32)], 0)
    entry = lax.broadcasted_iota(jnp.int32, (4 * BZ, BZ), 0)
    lanes = lane_index((4 * BZ, BZ))
    chosen = (entry // BZ == lanes // 32) & (entry % BZ == (lanes % 32) * 4)
    packed = jnp.dot(
        spread, chosen.astype(F32), precision=lax.Precision.HIGHEST, preferred_element_type=F32
    )
    lanes = lane_index((1, BZ))
    top_row = jnp.zeros((1, BZ), F32)
    for cx in range(2):
        coarse[...] = jnp.maximum(tops[first_x + 2 * cx], tops[first_x + 2 * cx + 1])
        value = jnp.maximum(
            coarse[pl.ds(first_y, 4, stride=2), :], coarse[pl.ds(first_y + 1, 4, stride=2), :]
        )
        for cy in range(4):
            top_row = jnp.where(lanes // 16 == 2 * cy + cx, value[cy:cy + 1], top_row)
    block = [packed[i:i + 1] for i in range(4)] + [top_row]
    pattern = jnp.concatenate(block * 8, 0)

    def fan(i, carry):
        fan_ref[pl.ds(pl.multiple_of(i * 8 * ROWS, 8), 8 * ROWS), :] = pattern
        return carry

    lax.fori_loop(0, fan_ref.shape[0] // (8 * ROWS), fan, 0)


def block_transpose(values, lanes):
    odd, high = (lanes & 32) != 0, (lanes & 64) != 0
    turn = [jnp.where(odd, values[(j + 1) % 4], values[j]) for j in range(4)]
    turn = [jnp.where(high, turn[(j + 2) % 4], turn[j]) for j in range(4)]
    skew = [shift(turn[(4 - d) % 4], -32 * d, 1) if d else turn[0] for d in range(4)]
    back = [jnp.where(odd, skew[(j + 3) % 4], skew[j]) for j in range(4)]
    return [jnp.where(high, back[(j + 2) % 4], back[j]) for j in range(4)]


def coarse_kernel(
    wide, deep, mine_ref, other_ref, wanted,
    coef, active, wx, wy, wz, diag, residual, image, slope, direction, solution,
):
    count = 2 * wide
    planes = count // 4
    block = min(BLOCK, planes)
    vector = (deep, BZ)
    lanes = lane_index(vector)
    zero = jnp.zeros(vector, F32)
    highest = (lanes & 31) == 31
    last_row = lax.broadcasted_iota(jnp.int32, vector, 0) == deep - 1
    last_block = lanes >= 96

    def y_after(value):
        return jnp.concatenate([value[:, 1:], shift(value[:, :1], -1, 2)], 1)

    def y_before(value):
        return jnp.concatenate([shift(value[:, 7:], 1, 2), value[:, :7]], 1)

    stride = deep * ROWS
    low = (lanes & 16) == 0
    layer = ((lanes & 31) * 4).astype(F32)

    def unpack(refs):
        def body(w, slot):
            def turned(c, k):
                return block_transpose(
                    [
                        refs[c][pl.ds((q * (wide // 4) + w) * stride + k, deep, stride=ROWS), :]
                        for q in range(4)
                    ],
                    lanes,
                )

            parts = [[turned(c, k) for k in range(ROWS)] for c in range(2)]
            for c in range(2):
                *fields, tops = parts[c]
                for y in range(4):
                    tall = (
                        jnp.where(low, tops[y], shift(tops[y], 16, 1)),
                        jnp.where(low, shift(tops[y], -16, 1), tops[y]),
                    )
                    for i in range(2):
                        residual[2 * w + i, 4 * c + y] = fields[i][y]
                        coef[2 * w + i, 4 * c + y] = fields[2 + i][y]
                        active[2 * w + i, 4 * c + y] = (layer < tall[i]).astype(F32)

        loop(0, planes // 2, 1, body)

    own_core = lax.axis_index("core")

    @pl.when(own_core == 0)
    def _():
        unpack((mine_ref, other_ref))

    @pl.when(own_core == 1)
    def _():
        unpack((other_ref, mine_ref))

    def coarse_weight(a, b):
        return 8.0 * a * b / (a + b)

    coef[planes] = jnp.where(last_block, 0.0, shift(coef[0], -32, 2))
    active[planes] = jnp.where(last_block, 0.0, shift(active[0], -32, 2))

    def setup(i, face):
        x = i * SETUP
        coefs, masks = coef[pl.ds(x, SETUP + 1)], active[pl.ds(x, SETUP + 1)]
        here, mask = coefs[:SETUP], masks[:SETUP]
        after = coarse_weight(here, coefs[1:])
        before = jnp.concatenate([face, after[:-1]], 0)
        beside = coarse_weight(here, y_after(here))
        beside = jnp.concatenate([beside[:, :7], jnp.where(last_row, 0.0, beside[:, 7:])], 1)
        above = coarse_weight(here, shift(here, -1, 3))
        inner = jnp.where(highest, 0.0, above)
        top = jnp.where(highest, 4.0 * here, above)
        total = after + before + beside + y_before(beside) + top + shift(inner, 1, 3)
        diag[pl.ds(x, SETUP)] = mask * total
        wx[pl.ds(x + 1, SETUP)] = after * (mask * masks[1:])
        wy[pl.ds(x, SETUP)] = beside * (mask * y_after(mask))
        wz[pl.ds(x, SETUP)] = inner * (mask * shift(mask, -1, 3))
        return after[-1:]

    closing = coarse_weight(coef[planes - 1:planes], coef[planes:planes + 1])
    lax.fori_loop(0, planes // SETUP, setup, shift(closing, 32, 3))
    wx[0] = shift(wx[planes], 32, 2)

    def whole(total):
        return jnp.sum(jnp.sum(total, axis=0, keepdims=True), axis=1, keepdims=True)

    def fold(total, value):
        return total + jnp.sum(value, axis=(0, 1))

    first_x = 2 * lax.axis_index("wide") - 2
    position = 2 * lax.axis_index("z") + own_core
    xs = [jnp.clip(first_x + i, 0, count - 1) for i in range(6)]
    groups = [jnp.clip(position + j - 1, 0, 2 * deep - 1) for j in range(3)]
    direction[...] = jnp.zeros(direction.shape, F32)
    solution[...] = jnp.zeros(solution.shape, F32)
    wanted[...] = jnp.zeros(wanted.shape, F32)

    ratio = scale = norm = jnp.zeros((1, 1), F32)
    for iteration in range(ITERS):
        start = iteration == 0
        if not start:
            wide_ratio = jnp.broadcast_to(ratio, vector)[None, None]
            wide_scale = jnp.broadcast_to(scale, vector)[None, None]

        def renew(x, size, keep=True):
            value = residual[pl.ds(x, size)]
            if start:
                return value
            slope_here = image[pl.ds(x, size)]
            if iteration > 1:
                slope_here = slope_here + wide_ratio * slope[pl.ds(x, size)]
            value = value - wide_scale * slope_here
            if keep:
                if iteration < ITERS - 1:
                    slope[pl.ds(x, size)] = slope_here
                residual[pl.ds(x, size)] = value
            return value

        def apply(x, carry, later):
            norm_sum, image_sum, last = carry
            grown = jnp.concatenate([last, later], 0)
            before, here, after = grown[:block], grown[1:block + 1], grown[2:]
            weight_y, weight_z = wy[pl.ds(x, block)], wz[pl.ds(x, block)]
            faces = wx[pl.ds(x, block + 1)]
            coupled = faces[1:] * after + faces[:-1] * before
            coupled = coupled + weight_y * y_after(here) + y_before(weight_y * here)
            coupled = coupled + weight_z * shift(here, -1, 3) + shift(weight_z * here, 1, 3)
            value = diag[pl.ds(x, block)] * here - coupled
            image[pl.ds(x, block)] = value
            return fold(norm_sum, here * here), fold(image_sum, here * value), grown[block:]

        before_first = shift(renew(planes - 1, 1, False), 32, 3)
        opening = renew(0, 1)
        carry = (zero, zero, jnp.concatenate([before_first, opening], 0))

        def turn(i, carry):
            x = i * block
            return apply(x, carry, renew(x + 1, block))

        carry = lax.fori_loop(0, planes // block - 1, turn, carry)
        x = planes - block
        beyond = shift(residual[0:1], -32, 3)
        if block > 1:
            beyond = jnp.concatenate([renew(x + 1, block - 1), beyond], 0)
        norm_sum, image_sum, _ = apply(x, carry, beyond)
        for i in range(6):
            for j in range(3):
                for y in range(4):
                    row = 16 * i + 4 * j + y
                    wanted[row:row + 1, :] = residual[
                        lax.rem(xs[i], planes), 4 * (groups[j] & 1) + y, pl.ds(groups[j] >> 1, 1), :
                    ]
        fresh, curvature = whole(norm_sum), whole(image_sum)
        here = wanted[...]
        if start:
            scale = fresh / curvature
        else:
            ratio = fresh / norm
            scale = fresh / (curvature - ratio * fresh / scale)
            here = here + ratio * direction[...]
        direction[...] = here
        solution[...] = solution[...] + scale * here
        norm = fresh

    columns = lane_index((16, BZ))
    for i in range(6):
        own_block = columns // 32 == xs[i] // planes
        wanted[16 * i:16 * i + 16] = jnp.where(own_block, solution[16 * i:16 * i + 16], 0.0)


def finish_kernel(
    wanted, even_ref, odd_ref,
    load1_ref, active1_ref, wx1_ref, wy1_ref, wz1_ref, diag1_ref, inv1_ref, smooth1_ref,
    load0_ref, active0_ref, wx0_ref, wy0_ref, wz0_ref, diag0_ref, inv0_ref, smooth0_ref,
    out_ref,
    spread, guess1, update1, second1, children, guess0, update0, second0,
):
    entry = lax.broadcasted_iota(jnp.int32, (BZ, BZ), 0)
    chosen = entry % 32 == lane_index((BZ, BZ)) // 4
    spread[...] = jnp.dot(
        wanted[...], chosen.astype(F32), precision=lax.Precision.HIGHEST, preferred_element_type=F32
    )
    even = lax.axis_index("wide") % 2 == 0
    for i in range(6):
        rows = []
        for y in range(12):
            row = spread[16 * i + y:16 * i + y + 1]
            rows.append(jnp.broadcast_to(row, (2, BZ)))
        parent = jnp.concatenate(rows, 0)
        for x in (2 * i, 2 * i + 1):
            if x in (0, MX - 1):
                continue
            if x <= 2:
                value = jnp.where(even, odd_ref[x - 1], even_ref[x - 1])
            elif x >= MX - 3:
                value = jnp.where(even, even_ref[x - (MX - 3)], odd_ref[x - (MX - 3)])
            else:
                value = smooth1_ref[x]
            guess1[x] = value + active1_ref[x] * parent

    def middle_operate(ref, x):
        return operate(
            ref[x - 1], ref[x], ref[x + 1], wx1_ref[x + 1], wx1_ref[x], wy1_ref[x], wz1_ref[x],
            diag1_ref[x], active1_ref[x], 2,
        )

    def middle_first(x, slot):
        residual_here = load1_ref[x] - middle_operate(guess1, x)
        value = residual_here * (inv1_ref[x] * inverse_center)
        update1[x] = value
        second1[x] = guess1[x] + value

    loop(2, MX - 2, 4, middle_first)

    def middle_second(x, slot):
        residual_here = load1_ref[x] - middle_operate(second1, x)
        value = second1[x] + (
            carry_weight * update1[x] + fresh_weight * residual_here * inv1_ref[x]
        )
        guess1[x] = value

    loop(3, MX - 3, 3, middle_second)

    def fine_guess(x, slot):
        value = guess1[x]
        children[slot, pl.ds(0, MY, stride=2), :] = value
        children[slot, pl.ds(1, MY, stride=2), :] = value
        child = children[slot, Y0:Y0 + TY, :]
        for i in range(2):
            k = 2 * x + i - X0
            guess0[k] = smooth0_ref[k] + active0_ref[k] * child

    loop(X0 // 2, (X0 + TX) // 2, 2, fine_guess)

    def fine_operate(ref, x):
        return operate(
            ref[x - 1], ref[x], ref[x + 1], wx0_ref[x + 1], wx0_ref[x], wy0_ref[x], wz0_ref[x],
            diag0_ref[x], active0_ref[x], 1,
        )

    def fine_first(x, slot):
        residual_here = load0_ref[x] - fine_operate(guess0, x)
        value = residual_here * (inv0_ref[x] * inverse_center)
        update0[x] = value
        second0[x] = guess0[x] + value

    loop(1, TX - 1, 5, fine_first)
    margin = BX - X0

    def fine_second(x, slot):
        residual_here = load0_ref[x] - fine_operate(second0, x)
        value = second0[x] + (
            carry_weight * update0[x] + fresh_weight * residual_here * inv0_ref[x]
        )
        out_ref[x - margin] = value[BY - Y0:2 * BY - Y0]

    loop(margin, margin + BX, 4, fine_second)


def in_vmem(count):
    return [pl.BlockSpec(memory_space=pltpu.VMEM)] * count


def grids(count, *shape):
    return [jax.ShapeDtypeStruct(shape, F32)] * count


def scratch(count, *shape):
    return [pltpu.VMEM(shape, F32)] * count


def strip_part(own, odd, even):
    return pl.pallas_call(
        strip_kernel,
        out_shape=grids(2, STRIP + (STRIP + 1) // 2, 8, BZ),
        in_specs=in_vmem(3),
        out_specs=in_vmem(2),
        compiler_params=pltpu.CompilerParams(vmem_limit_bytes=4 * 2**20),
        name="strip_part",
    )(own, odd, even)


def local_part(own, odd, even, far, near, fan):
    middle = grids(8, MX, MY, BZ)
    middle[2] = jax.ShapeDtypeStruct((MX + 1, MY, BZ), F32)
    outs = (
        grids(1, fan * ROWS, BZ) + grids(1, 2, MY, BZ) + middle + grids(8, TX, TY, BZ)
    )
    big = scratch(10, EX, EY, BZ)
    big[3] = pltpu.VMEM((EX + 1, EY, BZ), F32)
    return pl.pallas_call(
        local_kernel,
        out_shape=outs,
        in_specs=in_vmem(5),
        out_specs=in_vmem(len(outs)),
        scratch_shapes=big + scratch(2, MX, MY, BZ) + scratch(1, 2, EY, BZ)
        + scratch(1, MX, MY, BZ) + scratch(1, MY, BZ),
        compiler_params=pltpu.CompilerParams(vmem_limit_bytes=24 * 2**20),
        name="local_part",
    )(own, odd, even, far, near)


def coarse_part(wide, deep, mine, other):
    count = 2 * wide
    planes = count // 4
    tile = (8, deep, BZ)
    work = count * 2 * deep * BZ
    return pl.pallas_call(
        functools.partial(coarse_kernel, wide, deep),
        out_shape=jax.ShapeDtypeStruct((96, BZ), F32),
        in_specs=in_vmem(2),
        out_specs=pl.BlockSpec(memory_space=pltpu.VMEM),
        scratch_shapes=scratch(3, planes + 1, *tile) + scratch(6, planes, *tile)
        + scratch(2, 96, BZ),
        compiler_params=pltpu.CompilerParams(vmem_limit_bytes=16 * 2**20),
        cost_estimate=pl.CostEstimate(flops=250 * work, bytes_accessed=8 * work * 4, transcendentals=0),
        name="coarse_part",
    )(mine, other)


def finish_part(wanted, even, odd, kept):
    return pl.pallas_call(
        finish_kernel,
        out_shape=jax.ShapeDtypeStruct((BX, BY, BZ), F32),
        in_specs=in_vmem(3 + len(kept)),
        out_specs=pl.BlockSpec(memory_space=pltpu.VMEM),
        scratch_shapes=scratch(1, 96, BZ)
        + scratch(3, MX, MY, BZ) + scratch(1, 2, EY, BZ) + scratch(3, TX, TY, BZ),
        compiler_params=pltpu.CompilerParams(vmem_limit_bytes=8 * 2**20),
        name="finish_part",
    )(wanted, even, odd, *kept)


def swapped(size, start):
    pairs = [(i, i + 1) for i in range(start, size - 1, 2)]
    return pairs + [(j, i) for i, j in pairs]


def pack_kernel(source_ref, coef_ref, tops_ref, own_ref, odd_ref, even_ref, tops, sems):
    odd = lax.axis_index("wide") % 2
    moves = (
        (tops_ref, tops),
        (source_ref, own_ref.at[pl.ds(0, BX)]),
        (coef_ref, own_ref.at[pl.ds(BX, BX)]),
        (source_ref.at[pl.ds(odd * (BX - NS), NS)], odd_ref.at[pl.ds(0, NS)]),
        (coef_ref.at[pl.ds(odd * (BX - NC), NC)], odd_ref.at[pl.ds(NS, NC)]),
        (source_ref.at[pl.ds((1 - odd) * (BX - NS), NS)], even_ref.at[pl.ds(0, NS)]),
        (coef_ref.at[pl.ds((1 - odd) * (BX - NC), NC)], even_ref.at[pl.ds(NS, NC)]),
    )
    copies = [pltpu.make_async_copy(*move, sems.at[i]) for i, move in enumerate(moves)]
    for copy in copies:
        copy.start()
    copies[0].wait()
    values = tops[...].astype(F32)
    same = lax.broadcasted_iota(jnp.int32, (BY, BY), 0) == lane_index((BY, BY))
    lanes = lane_index((BY, BZ))
    turned = jnp.zeros((BY, BZ), F32)
    for x in range(BX):
        column = jnp.sum(jnp.where(same, values[x:x + 1], 0.0), axis=1, keepdims=True)
        turned = jnp.where(lanes == x, column, turned)
    own_ref[PACK - 1] = turned
    odd_ref[SIDE - 1] = turned
    even_ref[SIDE - 1] = turned
    for copy in copies[1:]:
        copy.wait()


def pack_part(source, conductivity, ice_cells):
    return pl.pallas_call(
        pack_kernel,
        out_shape=grids(1, PACK, BY, BZ) + grids(2, SIDE, BY, BZ),
        in_specs=[pl.BlockSpec(memory_space=pltpu.HBM)] * 3,
        out_specs=in_vmem(3),
        scratch_shapes=[pltpu.VMEM((BX, BY), jnp.int32), pltpu.SemaphoreType.DMA((7,))],
        compiler_params=pltpu.CompilerParams(vmem_limit_bytes=4 * 2**20),
        name="pack_part",
    )(*(pltpu.with_memory_space_constraint(v, pltpu.HBM) for v in (source, conductivity, ice_cells)))


def shards(wide, deep, source, conductivity, ice_cells):
    own, odd, even = pack_part(source, conductivity, ice_cells)
    odd = lax.ppermute(odd, "wide", swapped(wide, 1))
    even = lax.ppermute(even, "wide", swapped(wide, 0))
    far, near = strip_part(own, odd, even)
    far = lax.ppermute(far, ("z", "core"), swapped(2 * deep, 1))
    near = lax.ppermute(near, ("z", "core"), swapped(2 * deep, 0))
    fan, edge, *kept = local_part(own, odd, even, far, near, wide * deep)
    fan = fan.reshape(wide * deep, 1, ROWS * BZ)
    mine = lax.all_to_all(fan, ("wide", "z"), 0, 0, tiled=True)
    mine = mine.reshape(wide * deep * ROWS, BZ)
    other = lax.ppermute(mine, "core", [(0, 1), (1, 0)])
    even = lax.ppermute(edge, "wide", swapped(wide, 0))
    odd = lax.ppermute(edge, "wide", swapped(wide, 1))
    wanted = coarse_part(wide, deep, mine, other)
    return finish_part(wanted, even, odd, kept)


def solution(mesh):
    wide, deep = mesh.shape["wide"], mesh.shape["grp"] // 2
    split = Mesh(mesh.devices.reshape(wide, deep, 2), ("wide", "z", "core"))
    group = ("z", "core")
    return jax.shard_map(
        functools.partial(shards, wide, deep),
        mesh=split,
        in_specs=(P("wide", group, None), P("wide", group, None), P("wide", group)),
        out_specs=P("wide", group, None),
        check_vma=False,
    )
```

```python
import functools

import jax
import jax.numpy as jnp
from jax import lax
from jax.experimental import pallas as pl
from jax.experimental.pallas import tpu as pltpu
from jax.sharding import Mesh
from jax.sharding import PartitionSpec as P

ITERS = 6

cheb_center = (2.0 + 0.3) / 2.0
cheb_radius = (2.0 - 0.3) / 2.0
first_ratio = cheb_radius / cheb_center
second_ratio = 1.0 / (2.0 * cheb_center / cheb_radius - first_ratio)
carry_weight = second_ratio * first_ratio
fresh_weight = 2.0 * second_ratio / cheb_radius
inverse_center = 1.0 / cheb_center

F32 = jnp.float32
BX, BY, BZ = 8, 16, 128
PACK = 2 * BX + 1
NS, NC = 6, 7
SIDE = NS + NC + 1
STRIP = 2 * SIDE + PACK
HALF = 4
EX, EY = 3 * BX, 3 * BY
MX, MY = EX // 2, EY // 2
TX, TY = 12, 32
X0, Y0 = 6, 8
BLOCK = 4
SETUP = 2
ROWS = 5


def lane_index(shape):
    return lax.broadcasted_iota(jnp.int32, shape, len(shape) - 1)


def pair_weight(factor, coef, neighbour):
    total = coef + neighbour
    return (2.0 * factor) * coef * neighbour / jnp.where(total > 0.0, total, 1.0)


def shift(value, amount, axis):
    return pltpu.roll(value, amount % value.shape[axis], axis)


def operate(before, value, after, weight_x, weight_x_before, weight_y, weight_z, diagonal, active, step_z):
    coupled = weight_x * after + weight_x_before * before
    coupled = coupled + weight_y * shift(value, -1, 0)
    coupled = coupled + shift(weight_y * value, 1, 0)
    coupled = coupled + weight_z * shift(value, -step_z, 1)
    coupled = coupled + shift(weight_z * value, step_z, 1)
    return active * (diagonal * value - coupled)


def pair_lanes(value, step, combine):
    lanes = lane_index(value.shape)
    other = jnp.where((lanes & step) == 0, shift(value, -step, 1), shift(value, step, 1))
    return combine(value, other)


def loop(low, high, step, body):
    assert (high - low) % step == 0

    def turn(i, carry):
        for k in range(step):
            body(low + i * step + k, k)
        return carry

    lax.fori_loop(0, (high - low) // step, turn, 0)


def face_weights(factor, coef_ref, wx_ref, wy_ref, wz_ref, low, high, step, step_z):
    def body(x, slot):
        coef = coef_ref[x]
        lanes = lane_index(coef.shape)
        wx_ref[x + 1] = pair_weight(factor, coef, coef_ref[x + 1])
        wy_ref[x] = pair_weight(factor, coef, shift(coef, -1, 0))
        weight = pair_weight(factor, coef, shift(coef, -step_z, 1))
        wz_ref[x] = jnp.where(lanes >= BZ - step_z, 0.0, weight)

    wx_ref[low] = pair_weight(factor, coef_ref[low - 1], coef_ref[low])
    loop(low, high, step, body)


def diagonal_of(factor, x, coef_ref, wx_ref, wy_ref, wz_ref, step_z):
    coef = coef_ref[x]
    lanes = lane_index(coef.shape)
    weight_y, weight_z = wy_ref[x], wz_ref[x]
    top = jnp.where(lanes >= BZ - step_z, factor * coef, weight_z)
    total = wx_ref[x + 1] + wx_ref[x] + weight_y + shift(weight_y, 1, 0)
    return total + top + shift(weight_z, step_z, 1)


def inverse_of(diagonal):
    return 1.0 / jnp.where(diagonal > 0.0, diagonal, 1.0)


def pick(even, first, second):
    return jnp.where(even, first, second)


def strip_row(i, own_ref, left_ref, right_ref, even):
    if i < SIDE:
        return pick(even, left_ref[i], right_ref[i])
    if i < SIDE + PACK:
        return own_ref[i - SIDE]
    k = i - SIDE - PACK
    return pick(even, right_ref[k], left_ref[k])


def strip_kernel(own_ref, left_ref, right_ref, far_ref, near_ref):
    even = lax.axis_index("wide") % 2 == 0
    first_core = lax.axis_index("core") == 0
    for i in range(STRIP):
        row = strip_row(i, own_ref, left_ref, right_ref, even)
        k, part = STRIP + i // 2, slice(HALF * (i % 2), HALF * (i % 2 + 1))
        low, low_half = row[:8], row[8:8 + HALF]
        high, high_half = row[BY - 8:], row[BY - 8 - HALF:BY - 8]
        far_ref[i] = pick(first_core, low, high)
        far_ref[k, part] = pick(first_core, low_half, high_half)
        near_ref[i] = pick(first_core, high, low)
        near_ref[k, part] = pick(first_core, high_half, low_half)


def local_kernel(
    own_ref, left_ref, right_ref, far_ref, near_ref,
    fan_ref, edge_ref,
    load1_ref, active1_ref, wx1_ref, wy1_ref, wz1_ref, diag1_ref, inv1_ref, smooth1_ref,
    load0_ref, active0_ref, wx0_ref, wy0_ref, wz0_ref, diag0_ref, inv0_ref, smooth0_ref,
    source, coef, active, wx, wy, wz, diag, inv, update, smooth, coef1, update1, pairs, tops, coarse,
):
    edge_rows = jnp.zeros((8 - HALF, BZ), F32)

    even = lax.axis_index("wide") % 2 == 0
    first_core = lax.axis_index("core") == 0

    def extended(i):
        k, part = STRIP + i // 2, slice(HALF * (i % 2), HALF * (i % 2 + 1))
        far, near, far_half, near_half = far_ref[i], near_ref[i], far_ref[k, part], near_ref[k, part]
        return jnp.concatenate(
            [
                edge_rows,
                pick(first_core, far_half, near_half),
                pick(first_core, far, near),
                strip_row(i, own_ref, left_ref, right_ref, even),
                pick(first_core, near, far),
                pick(first_core, near_half, far_half),
                edge_rows,
            ],
            0,
        )

    middle = SIDE
    last = SIDE + PACK
    for i in range(NS):
        source[BX - NS + i] = extended(i)
        source[2 * BX + i] = extended(last + i)
    for i in range(NC):
        coef[BX - NC + i] = extended(NS + i)
        coef[2 * BX + i] = extended(last + NS + i)
    for i in range(BX):
        source[BX + i] = extended(middle + i)
        coef[BX + i] = extended(middle + BX + i)
    for j, i in enumerate((SIDE - 1, last - 1, STRIP - 1)):
        columns = extended(i)
        for x in range(BX):
            active[j * BX + x] = jnp.broadcast_to(columns[:, x:x + 1], (EY, BZ))

    low0, high0 = BX - NS, 2 * BX + NS
    low1, high1 = low0 // 2 + 1, high0 // 2 - 1

    def middle_tops(x, slot):
        pairs[slot] = jnp.maximum(active[2 * x], active[2 * x + 1])
        value = jnp.maximum(
            pairs[slot, pl.ds(0, MY, stride=2), :], pairs[slot, pl.ds(1, MY, stride=2), :]
        )
        tops[x] = value
        layer = (lane_index((MY, BZ)) & ~1).astype(F32)
        active1_ref[x] = (layer < value).astype(F32)

    loop(0, MX, 4, middle_tops)

    def fine_mask(x, slot):
        layer = lane_index((EY, BZ)).astype(F32)
        mask = (layer < active[x]).astype(F32)
        active[x] = mask
        source[x] = mask * source[x]

    loop(low0, high0, 4, fine_mask)

    face_weights(1.0, coef, wx, wy, wz, low0, high0, 4, 1)

    def fine_start(x, slot):
        diagonal = diagonal_of(1.0, x, coef, wx, wy, wz, 1)
        inverse = inverse_of(diagonal)
        diag[x] = diagonal
        inv[x] = inverse
        update[x] = source[x] * (inverse * inverse_center)

    loop(low0, high0, 4, fine_start)

    def fine_operate(ref, x):
        return operate(ref[x - 1], ref[x], ref[x + 1], wx[x + 1], wx[x], wy[x], wz[x], diag[x], active[x], 1)

    def fine_finish(x, slot):
        residual = source[x] - fine_operate(update, x)
        first = update[x]
        smooth[x] = first + (carry_weight * first + fresh_weight * residual * inv[x])

    loop(low0 + 1, high0 - 1, 3, fine_finish)

    def keep(i, slot):
        for kept, ref in (
            (load0_ref, source), (active0_ref, active), (wy0_ref, wy), (wz0_ref, wz),
            (diag0_ref, diag), (inv0_ref, inv), (smooth0_ref, smooth),
        ):
            kept[i] = ref[X0 + i, Y0:Y0 + TY, :]
        wx0_ref[i] = wx[X0 + i, Y0:Y0 + TY, :]

    loop(0, TX, 4, keep)

    def restrict(value, slot):
        pairs[slot] = pair_lanes(value, 1, jnp.add)
        return pairs[slot, pl.ds(0, MY, stride=2), :] + pairs[slot, pl.ds(1, MY, stride=2), :]

    def middle_coef(x, slot):
        coef1[x] = restrict(coef[2 * x] + coef[2 * x + 1], slot) * 0.125

    loop(low1 - 1, high1 + 1, 5, middle_coef)

    def middle_load(x, slot):
        left = source[2 * x] - fine_operate(smooth, 2 * x)
        right = source[2 * x + 1] - fine_operate(smooth, 2 * x + 1)
        load1_ref[x] = restrict(left + right, slot)

    loop(low1, high1, 4, middle_load)

    face_weights(2.0, coef1, wx1_ref, wy1_ref, wz1_ref, low1, high1, 4, 2)

    def middle_start(x, slot):
        diagonal = diagonal_of(2.0, x, coef1, wx1_ref, wy1_ref, wz1_ref, 2)
        inverse = inverse_of(diagonal)
        diag1_ref[x] = diagonal
        inv1_ref[x] = inverse
        update1[x] = load1_ref[x] * (inverse * inverse_center)

    loop(low1, high1, 4, middle_start)

    def middle_operate(ref, x):
        return operate(
            ref[x - 1], ref[x], ref[x + 1], wx1_ref[x + 1], wx1_ref[x], wy1_ref[x], wz1_ref[x],
            diag1_ref[x], active1_ref[x], 2,
        )

    def middle_finish(x, slot):
        residual = load1_ref[x] - middle_operate(update1, x)
        first = update1[x]
        smooth1_ref[x] = first + (carry_weight * first + fresh_weight * residual * inv1_ref[x])

    loop(low1 + 1, high1 - 1, 3, middle_finish)
    for i in range(2):
        edge_ref[i] = smooth1_ref[MX // 2 - 1 + i]

    first_x, first_y = MX // 3, MY // 3
    rows = []
    for part in range(2):
        for cx in range(2):
            if part == 0:
                total = sum(
                    load1_ref[x] - middle_operate(smooth1_ref, x)
                    for x in (first_x + 2 * cx, first_x + 2 * cx + 1)
                )
            else:
                total = (coef1[first_x + 2 * cx] + coef1[first_x + 2 * cx + 1]) * 0.125
            coarse[...] = pair_lanes(total, 2, jnp.add)
            value = (
                coarse[pl.ds(first_y, 4, stride=2), :] + coarse[pl.ds(first_y + 1, 4, stride=2), :]
            )
            rows.append(jnp.concatenate([value[i:i + 1] for i in range(4)], 1))
    spread = jnp.concatenate(rows + [jnp.zeros((4, 4 * BZ), F32)], 0)
    entry = lax.broadcasted_iota(jnp.int32, (4 * BZ, BZ), 0)
    lanes = lane_index((4 * BZ, BZ))
    chosen = (entry // BZ == lanes // 32) & (entry % BZ == (lanes % 32) * 4)
    packed = jnp.dot(
        spread, chosen.astype(F32), precision=lax.Precision.HIGHEST, preferred_element_type=F32
    )
    lanes = lane_index((1, BZ))
    top_row = jnp.zeros((1, BZ), F32)
    for cx in range(2):
        coarse[...] = jnp.maximum(tops[first_x + 2 * cx], tops[first_x + 2 * cx + 1])
        value = jnp.maximum(
            coarse[pl.ds(first_y, 4, stride=2), :], coarse[pl.ds(first_y + 1, 4, stride=2), :]
        )
        for cy in range(4):
            top_row = jnp.where(lanes // 16 == 2 * cy + cx, value[cy:cy + 1], top_row)
    block = [packed[i:i + 1] for i in range(4)] + [top_row]
    pattern = jnp.concatenate(block * 8, 0)

    def fan(i, carry):
        fan_ref[pl.ds(pl.multiple_of(i * 8 * ROWS, 8), 8 * ROWS), :] = pattern
        return carry

    lax.fori_loop(0, fan_ref.shape[0] // (8 * ROWS), fan, 0)


def block_transpose(values, lanes):
    odd, high = (lanes & 32) != 0, (lanes & 64) != 0
    turn = [jnp.where(odd, values[(j + 1) % 4], values[j]) for j in range(4)]
    turn = [jnp.where(high, turn[(j + 2) % 4], turn[j]) for j in range(4)]
    skew = [shift(turn[(4 - d) % 4], -32 * d, 1) if d else turn[0] for d in range(4)]
    back = [jnp.where(odd, skew[(j + 3) % 4], skew[j]) for j in range(4)]
    return [jnp.where(high, back[(j + 2) % 4], back[j]) for j in range(4)]


def coarse_kernel(
    wide, deep, mine_ref, other_ref, wanted,
    coef, active, wx, wy, wz, diag, residual, image, slope, direction, solution,
):
    count = 2 * wide
    planes = count // 4
    block = min(BLOCK, planes)
    vector = (deep, BZ)
    lanes = lane_index(vector)
    zero = jnp.zeros(vector, F32)
    highest = (lanes & 31) == 31
    last_row = lax.broadcasted_iota(jnp.int32, vector, 0) == deep - 1
    last_block = lanes >= 96

    def y_after(value):
        return jnp.concatenate([value[:, 1:], shift(value[:, :1], -1, 2)], 1)

    def y_before(value):
        return jnp.concatenate([shift(value[:, 7:], 1, 2), value[:, :7]], 1)

    stride = deep * ROWS
    low = (lanes & 16) == 0
    layer = ((lanes & 31) * 4).astype(F32)

    def unpack(refs):
        def body(w, slot):
            def turned(c, k):
                return block_transpose(
                    [
                        refs[c][pl.ds((q * (wide // 4) + w) * stride + k, deep, stride=ROWS), :]
                        for q in range(4)
                    ],
                    lanes,
                )

            parts = [[turned(c, k) for k in range(ROWS)] for c in range(2)]
            for c in range(2):
                *fields, tops = parts[c]
                for y in range(4):
                    tall = (
                        jnp.where(low, tops[y], shift(tops[y], 16, 1)),
                        jnp.where(low, shift(tops[y], -16, 1), tops[y]),
                    )
                    for i in range(2):
                        residual[2 * w + i, 4 * c + y] = fields[i][y]
                        coef[2 * w + i, 4 * c + y] = fields[2 + i][y]
                        active[2 * w + i, 4 * c + y] = (layer < tall[i]).astype(F32)

        loop(0, planes // 2, 1, body)

    own_core = lax.axis_index("core")

    @pl.when(own_core == 0)
    def _():
        unpack((mine_ref, other_ref))

    @pl.when(own_core == 1)
    def _():
        unpack((other_ref, mine_ref))

    def coarse_weight(a, b):
        return 8.0 * a * b / (a + b)

    coef[planes] = jnp.where(last_block, 0.0, shift(coef[0], -32, 2))
    active[planes] = jnp.where(last_block, 0.0, shift(active[0], -32, 2))

    def setup(i, face):
        x = i * SETUP
        coefs, masks = coef[pl.ds(x, SETUP + 1)], active[pl.ds(x, SETUP + 1)]
        here, mask = coefs[:SETUP], masks[:SETUP]
        after = coarse_weight(here, coefs[1:])
        before = jnp.concatenate([face, after[:-1]], 0)
        beside = coarse_weight(here, y_after(here))
        beside = jnp.concatenate([beside[:, :7], jnp.where(last_row, 0.0, beside[:, 7:])], 1)
        above = coarse_weight(here, shift(here, -1, 3))
        inner = jnp.where(highest, 0.0, above)
        top = jnp.where(highest, 4.0 * here, above)
        total = after + before + beside + y_before(beside) + top + shift(inner, 1, 3)
        diag[pl.ds(x, SETUP)] = mask * total
        wx[pl.ds(x + 1, SETUP)] = after * (mask * masks[1:])
        wy[pl.ds(x, SETUP)] = beside * (mask * y_after(mask))
        wz[pl.ds(x, SETUP)] = inner * (mask * shift(mask, -1, 3))
        return after[-1:]

    closing = coarse_weight(coef[planes - 1:planes], coef[planes:planes + 1])
    lax.fori_loop(0, planes // SETUP, setup, shift(closing, 32, 3))
    wx[0] = shift(wx[planes], 32, 2)

    def whole(total):
        return jnp.sum(jnp.sum(total, axis=0, keepdims=True), axis=1, keepdims=True)

    def fold(total, value):
        return total + jnp.sum(value, axis=(0, 1))

    first_x = 2 * lax.axis_index("wide") - 2
    position = 2 * lax.axis_index("z") + own_core
    xs = [jnp.clip(first_x + i, 0, count - 1) for i in range(6)]
    groups = [jnp.clip(position + j - 1, 0, 2 * deep - 1) for j in range(3)]
    direction[...] = jnp.zeros(direction.shape, F32)
    solution[...] = jnp.zeros(solution.shape, F32)
    wanted[...] = jnp.zeros(wanted.shape, F32)

    ratio = scale = norm = jnp.zeros((1, 1), F32)
    for iteration in range(ITERS):
        start = iteration == 0
        if not start:
            wide_ratio = jnp.broadcast_to(ratio, vector)[None, None]
            wide_scale = jnp.broadcast_to(scale, vector)[None, None]

        def renew(x, size, keep=True):
            value = residual[pl.ds(x, size)]
            if start:
                return value
            slope_here = image[pl.ds(x, size)]
            if iteration > 1:
                slope_here = slope_here + wide_ratio * slope[pl.ds(x, size)]
            value = value - wide_scale * slope_here
            if keep:
                if iteration < ITERS - 1:
                    slope[pl.ds(x, size)] = slope_here
                residual[pl.ds(x, size)] = value
            return value

        def apply(x, carry, later):
            norm_sum, image_sum, last = carry
            grown = jnp.concatenate([last, later], 0)
            before, here, after = grown[:block], grown[1:block + 1], grown[2:]
            weight_y, weight_z = wy[pl.ds(x, block)], wz[pl.ds(x, block)]
            faces = wx[pl.ds(x, block + 1)]
            coupled = faces[1:] * after + faces[:-1] * before
            coupled = coupled + weight_y * y_after(here) + y_before(weight_y * here)
            coupled = coupled + weight_z * shift(here, -1, 3) + shift(weight_z * here, 1, 3)
            value = diag[pl.ds(x, block)] * here - coupled
            image[pl.ds(x, block)] = value
            return fold(norm_sum, here * here), fold(image_sum, here * value), grown[block:]

        before_first = shift(renew(planes - 1, 1, False), 32, 3)
        opening = renew(0, 1)
        carry = (zero, zero, jnp.concatenate([before_first, opening], 0))

        def turn(i, carry):
            x = i * block
            return apply(x, carry, renew(x + 1, block))

        carry = lax.fori_loop(0, planes // block - 1, turn, carry)
        x = planes - block
        beyond = shift(residual[0:1], -32, 3)
        if block > 1:
            beyond = jnp.concatenate([renew(x + 1, block - 1), beyond], 0)
        norm_sum, image_sum, _ = apply(x, carry, beyond)
        for i in range(6):
            for j in range(3):
                for y in range(4):
                    row = 16 * i + 4 * j + y
                    wanted[row:row + 1, :] = residual[
                        lax.rem(xs[i], planes), 4 * (groups[j] & 1) + y, pl.ds(groups[j] >> 1, 1), :
                    ]
        fresh, curvature = whole(norm_sum), whole(image_sum)
        here = wanted[...]
        if start:
            scale = fresh / curvature
        else:
            ratio = fresh / norm
            scale = fresh / (curvature - ratio * fresh / scale)
            here = here + ratio * direction[...]
        direction[...] = here
        solution[...] = solution[...] + scale * here
        norm = fresh

    columns = lane_index((16, BZ))
    for i in range(6):
        own_block = columns // 32 == xs[i] // planes
        wanted[16 * i:16 * i + 16] = jnp.where(own_block, solution[16 * i:16 * i + 16], 0.0)


def finish_kernel(
    wanted, even_ref, odd_ref,
    load1_ref, active1_ref, wx1_ref, wy1_ref, wz1_ref, diag1_ref, inv1_ref, smooth1_ref,
    load0_ref, active0_ref, wx0_ref, wy0_ref, wz0_ref, diag0_ref, inv0_ref, smooth0_ref,
    out_ref,
    spread, guess1, update1, second1, children, guess0, update0, second0,
):
    entry = lax.broadcasted_iota(jnp.int32, (BZ, BZ), 0)
    chosen = entry % 32 == lane_index((BZ, BZ)) // 4
    spread[...] = jnp.dot(
        wanted[...], chosen.astype(F32), precision=lax.Precision.HIGHEST, preferred_element_type=F32
    )
    even = lax.axis_index("wide") % 2 == 0
    for i in range(6):
        rows = []
        for y in range(12):
            row = spread[16 * i + y:16 * i + y + 1]
            rows.append(jnp.broadcast_to(row, (2, BZ)))
        parent = jnp.concatenate(rows, 0)
        for x in (2 * i, 2 * i + 1):
            if x in (0, MX - 1):
                continue
            if x <= 2:
                value = jnp.where(even, odd_ref[x - 1], even_ref[x - 1])
            elif x >= MX - 3:
                value = jnp.where(even, even_ref[x - (MX - 3)], odd_ref[x - (MX - 3)])
            else:
                value = smooth1_ref[x]
            guess1[x] = value + active1_ref[x] * parent

    def middle_operate(ref, x):
        return operate(
            ref[x - 1], ref[x], ref[x + 1], wx1_ref[x + 1], wx1_ref[x], wy1_ref[x], wz1_ref[x],
            diag1_ref[x], active1_ref[x], 2,
        )

    def middle_first(x, slot):
        residual_here = load1_ref[x] - middle_operate(guess1, x)
        value = residual_here * (inv1_ref[x] * inverse_center)
        update1[x] = value
        second1[x] = guess1[x] + value

    loop(2, MX - 2, 4, middle_first)

    def middle_second(x, slot):
        residual_here = load1_ref[x] - middle_operate(second1, x)
        value = second1[x] + (
            carry_weight * update1[x] + fresh_weight * residual_here * inv1_ref[x]
        )
        guess1[x] = value

    loop(3, MX - 3, 3, middle_second)

    def fine_guess(x, slot):
        value = guess1[x]
        children[slot, pl.ds(0, MY, stride=2), :] = value
        children[slot, pl.ds(1, MY, stride=2), :] = value
        child = children[slot, Y0:Y0 + TY, :]
        for i in range(2):
            k = 2 * x + i - X0
            guess0[k] = smooth0_ref[k] + active0_ref[k] * child

    loop(X0 // 2, (X0 + TX) // 2, 2, fine_guess)

    def fine_operate(ref, x):
        return operate(
            ref[x - 1], ref[x], ref[x + 1], wx0_ref[x + 1], wx0_ref[x], wy0_ref[x], wz0_ref[x],
            diag0_ref[x], active0_ref[x], 1,
        )

    def fine_first(x, slot):
        residual_here = load0_ref[x] - fine_operate(guess0, x)
        value = residual_here * (inv0_ref[x] * inverse_center)
        update0[x] = value
        second0[x] = guess0[x] + value

    loop(1, TX - 1, 5, fine_first)
    margin = BX - X0

    def fine_second(x, slot):
        residual_here = load0_ref[x] - fine_operate(second0, x)
        value = second0[x] + (
            carry_weight * update0[x] + fresh_weight * residual_here * inv0_ref[x]
        )
        out_ref[x - margin] = value[BY - Y0:2 * BY - Y0]

    loop(margin, margin + BX, 4, fine_second)


def in_vmem(count):
    return [pl.BlockSpec(memory_space=pltpu.VMEM)] * count


def grids(count, *shape):
    return [jax.ShapeDtypeStruct(shape, F32)] * count


def scratch(count, *shape):
    return [pltpu.VMEM(shape, F32)] * count


def strip_part(own, odd, even):
    return pl.pallas_call(
        strip_kernel,
        out_shape=grids(2, STRIP + (STRIP + 1) // 2, 8, BZ),
        in_specs=in_vmem(3),
        out_specs=in_vmem(2),
        compiler_params=pltpu.CompilerParams(vmem_limit_bytes=4 * 2**20),
        name="strip_part",
    )(own, odd, even)


def local_part(own, odd, even, far, near, fan):
    middle = grids(8, MX, MY, BZ)
    middle[2] = jax.ShapeDtypeStruct((MX + 1, MY, BZ), F32)
    outs = (
        grids(1, fan * ROWS, BZ) + grids(1, 2, MY, BZ) + middle + grids(8, TX, TY, BZ)
    )
    big = scratch(10, EX, EY, BZ)
    big[3] = pltpu.VMEM((EX + 1, EY, BZ), F32)
    return pl.pallas_call(
        local_kernel,
        out_shape=outs,
        in_specs=in_vmem(5),
        out_specs=in_vmem(len(outs)),
        scratch_shapes=big + scratch(2, MX, MY, BZ) + scratch(1, 5, EY, BZ)
        + scratch(1, MX, MY, BZ) + scratch(1, MY, BZ),
        compiler_params=pltpu.CompilerParams(vmem_limit_bytes=24 * 2**20),
        name="local_part",
    )(own, odd, even, far, near)


def coarse_part(wide, deep, mine, other):
    count = 2 * wide
    planes = count // 4
    tile = (8, deep, BZ)
    work = count * 2 * deep * BZ
    return pl.pallas_call(
        functools.partial(coarse_kernel, wide, deep),
        out_shape=jax.ShapeDtypeStruct((96, BZ), F32),
        in_specs=in_vmem(2),
        out_specs=pl.BlockSpec(memory_space=pltpu.VMEM),
        scratch_shapes=scratch(3, planes + 1, *tile) + scratch(6, planes, *tile)
        + scratch(2, 96, BZ),
        compiler_params=pltpu.CompilerParams(vmem_limit_bytes=16 * 2**20),
        cost_estimate=pl.CostEstimate(flops=250 * work, bytes_accessed=8 * work * 4, transcendentals=0),
        name="coarse_part",
    )(mine, other)


def finish_part(wanted, even, odd, kept):
    return pl.pallas_call(
        finish_kernel,
        out_shape=jax.ShapeDtypeStruct((BX, BY, BZ), F32),
        in_specs=in_vmem(3 + len(kept)),
        out_specs=pl.BlockSpec(memory_space=pltpu.VMEM),
        scratch_shapes=scratch(1, 96, BZ)
        + scratch(3, MX, MY, BZ) + scratch(1, 2, EY, BZ) + scratch(3, TX, TY, BZ),
        compiler_params=pltpu.CompilerParams(vmem_limit_bytes=8 * 2**20),
        name="finish_part",
    )(wanted, even, odd, *kept)


def swapped(size, start):
    pairs = [(i, i + 1) for i in range(start, size - 1, 2)]
    return pairs + [(j, i) for i, j in pairs]


def pack_kernel(source_ref, coef_ref, tops_ref, own_ref, odd_ref, even_ref, tops, sems):
    odd = lax.axis_index("wide") % 2
    moves = (
        (tops_ref, tops),
        (source_ref, own_ref.at[pl.ds(0, BX)]),
        (coef_ref, own_ref.at[pl.ds(BX, BX)]),
        (source_ref.at[pl.ds(odd * (BX - NS), NS)], odd_ref.at[pl.ds(0, NS)]),
        (coef_ref.at[pl.ds(odd * (BX - NC), NC)], odd_ref.at[pl.ds(NS, NC)]),
        (source_ref.at[pl.ds((1 - odd) * (BX - NS), NS)], even_ref.at[pl.ds(0, NS)]),
        (coef_ref.at[pl.ds((1 - odd) * (BX - NC), NC)], even_ref.at[pl.ds(NS, NC)]),
    )
    copies = [pltpu.make_async_copy(*move, sems.at[i]) for i, move in enumerate(moves)]
    for copy in copies:
        copy.start()
    copies[0].wait()
    values = tops[...].astype(F32)
    same = lax.broadcasted_iota(jnp.int32, (BY, BY), 0) == lane_index((BY, BY))
    lanes = lane_index((BY, BZ))
    turned = jnp.zeros((BY, BZ), F32)
    for x in range(BX):
        column = jnp.sum(jnp.where(same, values[x:x + 1], 0.0), axis=1, keepdims=True)
        turned = jnp.where(lanes == x, column, turned)
    own_ref[PACK - 1] = turned
    odd_ref[SIDE - 1] = turned
    even_ref[SIDE - 1] = turned
    for copy in copies[1:]:
        copy.wait()


def pack_part(source, conductivity, ice_cells):
    return pl.pallas_call(
        pack_kernel,
        out_shape=grids(1, PACK, BY, BZ) + grids(2, SIDE, BY, BZ),
        in_specs=[pl.BlockSpec(memory_space=pltpu.HBM)] * 3,
        out_specs=in_vmem(3),
        scratch_shapes=[pltpu.VMEM((BX, BY), jnp.int32), pltpu.SemaphoreType.DMA((7,))],
        compiler_params=pltpu.CompilerParams(vmem_limit_bytes=4 * 2**20),
        name="pack_part",
    )(*(pltpu.with_memory_space_constraint(v, pltpu.HBM) for v in (source, conductivity, ice_cells)))


def shards(wide, deep, source, conductivity, ice_cells):
    own, odd, even = pack_part(source, conductivity, ice_cells)
    odd = lax.ppermute(odd, "wide", swapped(wide, 1))
    even = lax.ppermute(even, "wide", swapped(wide, 0))
    far, near = strip_part(own, odd, even)
    far = lax.ppermute(far, ("z", "core"), swapped(2 * deep, 1))
    near = lax.ppermute(near, ("z", "core"), swapped(2 * deep, 0))
    fan, edge, *kept = local_part(own, odd, even, far, near, wide * deep)
    fan = fan.reshape(wide * deep, 1, ROWS * BZ)
    mine = lax.all_to_all(fan, ("wide", "z"), 0, 0, tiled=True)
    mine = mine.reshape(wide * deep * ROWS, BZ)
    other = lax.ppermute(mine, "core", [(0, 1), (1, 0)])
    even = lax.ppermute(edge, "wide", swapped(wide, 0))
    odd = lax.ppermute(edge, "wide", swapped(wide, 1))
    wanted = coarse_part(wide, deep, mine, other)
    return finish_part(wanted, even, odd, kept)


def solution(mesh):
    wide, deep = mesh.shape["wide"], mesh.shape["grp"] // 2
    split = Mesh(mesh.devices.reshape(wide, deep, 2), ("wide", "z", "core"))
    group = ("z", "core")
    return jax.shard_map(
        functools.partial(shards, wide, deep),
        mesh=split,
        in_specs=(P("wide", group, None), P("wide", group, None), P("wide", group)),
        out_specs=P("wide", group, None),
        check_vma=False,
    )
```
